32 devices in a mesh: seq: 16 (over z, x, core), head: 2 (over y).
Axes of the slice: x: 2, y: 2, z: 4, core: 2. Of those that a mesh axis runs over, the one named last changes fastest.
Arguments:
- qkv: bfloat16 [3, 8192, 4096], P(None, ('seq', 'head')), may hold values from -6 to 6
- send_rows: int32 [16, 16, 40], P('seq'), may hold values from -1 to 511, as said below
- recv_pos: int32 [16, 16, 40], P('seq'), may hold values from -1 to 511, as said below
- req_lengths: int32 [4], replicated, may hold values from 1 to 4096, 8192 in all
- norm_gain: float32 [4096], P('head'), may hold values from 0.5 to 1.5
Outputs:
- attn_out: bfloat16 [8192, 4096], P('seq', 'head')
The draws below stay inside these ranges and needn't reach their ends.
Inputs may be any that keep to these rules, and one draw needn't show every extreme that they name: send_rows[l, o, c] is a row of loader group l (rows l * 512 to l * 512 + 511 of qkv, counted from the group's first) sent to owner o in slot c, or -1 for an empty slot; used slots come first. Every row of a group is sent exactly once. At most 40 rows go from one group to one owner, and in every draw some pairs carry exactly 40, so that every group sends and every owner receives 40 rows from one pair. The number of rows from group l to owner o depends only on (o - l) modulo the number of groups. recv_pos[o, l, c] is the position within owner o's block of 512 packed positions where slot c from group l lands, and -1 exactly where send_rows[l, o, c] is -1; every position of a block is filled exactly once.
All inputs are finite; a program needn't handle non-finite values.
Results may differ from the reference program's by a relative error of at most 0.003.
Values may be sent and summed in bfloat16 or wider, within the bound.
No kernel may reach another device: no remote copies, remote signals or barrier semaphores. Data moves between devices by JAX's collectives and lax.ppermute only.
A program may use at most 128 MiB of HBM per device.

```python
import math
import jax
import jax.numpy as jnp
import numpy as np
from jax import lax

HEADS = 32
HEAD_DIM = 128
TOK_DEV = 512
REQS = 4
TOKENS = 8192
HD = 4096
MEAN = 32
CAP = 40
LONGEST = 4096
N_SEQ = 16


def route_tables(key):
    base_key = jax.random.fold_in(key, 11)
    pair_key, size_key, send_key, land_key = jax.random.split(base_key, 4)
    slack_rows = CAP - MEAN
    shuffled = jax.random.permutation(pair_key, N_SEQ)
    pair_moves = jax.random.randint(size_key, (N_SEQ // 2,), 0, slack_rows + 1)
    pair_moves = pair_moves.at[0].set(slack_rows)
    offsets = jnp.zeros((N_SEQ,), jnp.int32).at[shuffled[0::2]].set(pair_moves).at[shuffled[1::2]].set(-pair_moves)
    weights = MEAN + offsets
    loader_ids = jnp.arange(N_SEQ)[:, None]
    owner_ids = jnp.arange(N_SEQ)[None, :]
    counts = weights[(owner_ids - loader_ids) % N_SEQ]
    send_start = jnp.cumsum(counts, axis=1) - counts
    land_start = jnp.cumsum(counts, axis=0) - counts
    slot_ids = jnp.arange(CAP)
    valid_slot = slot_ids[None, None, :] < counts[:, :, None]
    send_perm = jax.vmap(lambda sub_key: jax.random.permutation(sub_key, TOK_DEV))(jax.random.split(send_key, N_SEQ))
    land_perm = jax.vmap(lambda sub_key: jax.random.permutation(sub_key, TOK_DEV))(jax.random.split(land_key, N_SEQ))
    send_at = jnp.minimum(send_start[:, :, None] + slot_ids[None, None, :], TOK_DEV - 1)
    land_at = jnp.minimum(land_start[:, :, None] + slot_ids[None, None, :], TOK_DEV - 1)
    loader_all = jnp.broadcast_to(jnp.arange(N_SEQ)[:, None, None], send_at.shape)
    owner_all = jnp.broadcast_to(jnp.arange(N_SEQ)[None, :, None], land_at.shape)
    send_lists = jnp.where(valid_slot, send_perm[loader_all, send_at], -1)
    land_lists = jnp.where(valid_slot, land_perm[owner_all, land_at], -1)
    return (send_lists.astype(jnp.int32), jnp.transpose(land_lists, (1, 0, 2)).astype(jnp.int32))


def draw_send_rows(key, part):
    return route_tables(key)[0]


def draw_recv_pos(key, part):
    return route_tables(key)[1]


def block_scale(stream_key, extent, cuts, smallest, largest):
    loudness, own = 1.0, jax.random.fold_in(stream_key, 6)
    for position, shards_of in cuts:
        heights = jnp.exp(jax.random.uniform(jax.random.fold_in(own, position), (shards_of,), jnp.float32, smallest / len(cuts), largest / len(cuts)))
        loudness = loudness * jnp.repeat(heights, extent[position] // shards_of).reshape([-1 if axis == position else 1 for axis in range(len(extent))])
    return loudness


def split_up(count, total, bound, slope):
    portions = [(1 << 20) // math.isqrt(standing ** slope) + 1 for standing in range(2, count + 1)]
    rest, holding = total - bound - (count - 1), [1] * (count - 1)
    while rest > 0:
        candidates = [i for i in range(count - 1) if holding[i] < bound]
        mass, remaining = sum([portions[i] for i in candidates]), rest
        for i in candidates:
            extra = min(bound - holding[i], max(1, remaining * portions[i] // mass), rest)
            holding[i] = holding[i] + extra
            rest = rest - extra
    return np.array([bound] + holding)


def ragged_sizes(own_key, number_of, total, bound, lean):
    if number_of == 2:
        one = jax.random.randint(own_key, (), max(1, total - bound), min(bound, total - 1) + 1)
        return jnp.stack([one, total - one])
    sizes = jnp.asarray(split_up(number_of, total, bound, lean), jnp.int32)
    couples = (number_of - 1) // 2
    donor, taker = sizes[1:1 + 2 * couples:2], sizes[2:2 + 2 * couples:2]
    margin = jnp.minimum(donor - 1, bound - taker)
    moved = jax.random.randint(jax.random.fold_in(own_key, 1), (couples,), 0, 1 << 20) % (margin + 1)
    sizes = sizes.at[1:1 + 2 * couples:2].set(donor - moved).at[2:2 + 2 * couples:2].set(taker + moved)
    return sizes[jax.random.permutation(jax.random.fold_in(own_key, 2), number_of)]


def gaussian(stream_key, extent, deviation, most, shards=(), held_as=jnp.bfloat16):
    level = block_scale(stream_key, extent, shards, -0.22, 0.18) if shards else 1.0
    array = jax.random.normal(stream_key, extent, jnp.float32) * deviation * level
    return jnp.minimum(jnp.maximum(array, -most), most).astype(held_as)


def setup_inputs(seed: int = 0) -> dict:
    key_list = jax.random.split(jax.random.key(seed), 6)
    qkv = gaussian(key_list[0], (3, TOKENS, HD), 1.0, 6.0, ((1, 32),))
    send_rows = draw_send_rows(jax.random.fold_in(key_list[5], 71), 0)
    recv_pos = draw_recv_pos(jax.random.fold_in(key_list[5], 71), 0)
    req_lengths = ragged_sizes(key_list[3], REQS, TOKENS, LONGEST, 2).astype(jnp.int32)
    norm_gain = jnp.clip(1.0 + 0.1 * jax.random.normal(key_list[4], (HD,), jnp.float32), 0.5, 1.5)
    return dict(qkv=qkv, send_rows=send_rows, recv_pos=recv_pos, req_lengths=req_lengths, norm_gain=norm_gain)


norm_eps = 1e-06

def packed_source(send_rows, recv_pos):
    loader_ids = jnp.arange(N_SEQ, dtype=jnp.int32)[:, None, None]
    owner_ids = jnp.arange(N_SEQ, dtype=jnp.int32)[None, :, None]
    source_rows = loader_ids * TOK_DEV + jnp.maximum(send_rows, 0)
    target_rows = owner_ids * TOK_DEV + jnp.transpose(recv_pos, (1, 0, 2))
    target_rows = jnp.where(send_rows >= 0, target_rows, TOKENS).astype(jnp.int32)
    blank_rows = jnp.zeros((TOKENS,), jnp.int32)
    return blank_rows.at[target_rows.reshape(-1)].set(source_rows.reshape(-1).astype(jnp.int32), mode='drop')

def reference(qkv, send_rows, recv_pos, req_lengths, norm_gain):
    source_of = packed_source(send_rows, recv_pos)
    req_ends = jnp.cumsum(req_lengths).astype(jnp.int32)
    req_starts = (req_ends - req_lengths).astype(jnp.int32)
    gain_f32 = norm_gain.astype(jnp.float32).reshape(HEADS, HEAD_DIM)

    def block_step(carry, block_id):
        carry_state, prev_segment = carry
        row_ids = lax.dynamic_slice_in_dim(source_of, (block_id * TOK_DEV).astype(jnp.int32), TOK_DEV)
        positions = (block_id * TOK_DEV + jnp.arange(TOK_DEV, dtype=jnp.int32)).astype(jnp.int32)
        segment = (lax.optimization_barrier(jnp.sum((req_starts[None, :] <= positions[:, None]).astype(jnp.int32), axis=1)) - 1).astype(jnp.int32)
        block_data = qkv[:, row_ids, :].astype(jnp.float32).reshape(3, TOK_DEV, HEADS, HEAD_DIM)
        query, keys, values = (block_data[0], block_data[1], block_data[2])
        scores = jnp.einsum('thd,shd->hts', query, keys)
        same_req = (positions[None, :] <= positions[:, None]) & (segment[None, :] == segment[:, None])
        weights = jnp.where(same_req[None], scores, 0.0).astype(jnp.bfloat16)
        weights = lax.optimization_barrier(weights).astype(jnp.float32)
        local_term = jnp.einsum('hts,shd->thd', weights, values)
        tail_mask = segment == segment[TOK_DEV - 1]
        tail_keys = jnp.where(tail_mask[:, None, None], keys, 0.0)
        update = jnp.einsum('shd,she->hde', tail_keys, values)
        carried_term = jnp.einsum('thd,hde->the', query, carry_state, precision=lax.Precision.HIGHEST)
        carried_term = jnp.where((segment == prev_segment)[:, None, None], carried_term, 0.0)
        raw_out = local_term + carried_term
        inv_rms = lax.rsqrt(lax.optimization_barrier(jnp.mean(raw_out * raw_out, axis=2, keepdims=True)) + norm_eps)
        normed = (raw_out * inv_rms * gain_f32[None]).reshape(TOK_DEV, HD).astype(jnp.bfloat16)
        has_start = jnp.any((req_starts >= block_id * TOK_DEV) & (req_starts < block_id * TOK_DEV + TOK_DEV))
        next_state = (update + jnp.where(has_start, jnp.zeros_like(carry_state), carry_state)).astype(carry_state.dtype)
        return ((next_state, segment[TOK_DEV - 1].astype(jnp.int32)), normed)
    start_state = jnp.zeros((HEADS, HEAD_DIM, HEAD_DIM), jnp.float32)
    block_ids = jnp.arange(TOKENS // TOK_DEV, dtype=jnp.int32)
    final_carry, blocks_out = lax.scan(block_step, (start_state, jnp.int32(-1)), block_ids)
    return blocks_out.reshape(TOKENS, HD)
```

```python
import functools

import jax
import jax.numpy as jnp
from jax import lax
from jax.experimental import pallas as pl
from jax.experimental.pallas import tpu as pltpu
from jax.sharding import PartitionSpec as P

HEAD_DIM = 128

norm_eps = 1e-06

QUERY, KEYS, VALUES = 0, 1, 2


def pack_kernel(place_ref, *refs):
    count = (len(refs) - 1) // 3
    picks, sources = refs[:count], refs[count : 2 * count]
    out_ref, chosen = refs[2 * count], refs[2 * count + 1 :]

    @pl.when((pl.program_id(0) == 0) & (pl.program_id(1) == 0))
    def _():
        for pick, onehot in zip(picks, chosen):
            rows = lax.broadcasted_iota(jnp.int32, onehot.shape, 1)
            onehot[...] = jnp.where(pick[...] == rows, 1.0, 0.0).astype(onehot.dtype)

    total = None
    for source, onehot in zip(sources, chosen):
        part = jnp.dot(onehot[...], source[0], preferred_element_type=jnp.float32)
        total = part if total is None else total + part
    out_ref[...] = total.astype(out_ref.dtype)


def pack_rows(place, picks, sources, planes, columns):
    slots = picks[0].shape[0]
    width = min(columns, 512)
    blocks = columns // width
    lens = [array.shape[1] for array, _, _ in sources]

    def source_spec(array, plane_start, first):
        return pl.BlockSpec(
            (1, array.shape[1], width),
            lambda p, j, place_ref: (plane_start + p, 0, first(place_ref[0], width) + j),
        )

    return pl.pallas_call(
        pack_kernel,
        out_shape=jax.ShapeDtypeStruct((slots, planes * columns), jnp.bfloat16),
        grid_spec=pltpu.PrefetchScalarGridSpec(
            num_scalar_prefetch=1,
            grid=(planes, blocks),
            in_specs=[pl.BlockSpec((slots, 1), lambda p, j, place_ref: (0, 0)) for _ in picks]
            + [source_spec(*source) for source in sources],
            out_specs=pl.BlockSpec((slots, width), lambda p, j, place_ref: (0, p * blocks + j)),
            scratch_shapes=[pltpu.VMEM((slots, length), jnp.bfloat16) for length in lens],
        ),
        cost_estimate=pl.CostEstimate(
            flops=2 * slots * sum(lens) * planes * columns,
            bytes_accessed=2 * planes * columns * (slots + sum(lens)),
            transcendentals=0,
        ),
        name="pack_rows",
    )(place, *picks, *[array for array, _, _ in sources])


def unpack_kernel(land_ref, tail_ref, keys_ref, values_ref, keys_out, values_out, update_ref, order):
    @pl.when(pl.program_id(0) == 0)
    def _():
        rows = lax.broadcasted_iota(jnp.int32, order.shape, 0)
        order[...] = jnp.where(land_ref[...] == rows, 1.0, 0.0).astype(order.dtype)

    keys = jnp.dot(order[...], keys_ref[...], preferred_element_type=jnp.float32)
    keys_out[...] = keys.astype(keys_out.dtype)
    values = jnp.dot(order[...], values_ref[...], preferred_element_type=jnp.float32).astype(
        values_out.dtype
    )
    values_out[...] = values
    tail_keys = jnp.where(tail_ref[...] != 0, keys, 0.0).astype(values.dtype)
    for part in range(keys.shape[1] // HEAD_DIM):
        columns = slice(part * HEAD_DIM, (part + 1) * HEAD_DIM)
        update_ref[columns, :] = lax.dot_general(
            tail_keys[:, columns],
            values[:, columns],
            (((0,), (0,)), ((), ())),
            preferred_element_type=jnp.float32,
        ).astype(update_ref.dtype)


def unpack_keys_values(arrived, land_row, tail, tok_rows):
    slots, columns = arrived.shape[0], arrived.shape[1] // 2
    width = min(columns, 2 * HEAD_DIM)
    blocks = columns // width
    packed = jax.ShapeDtypeStruct((tok_rows, columns), arrived.dtype)
    column_spec = pl.BlockSpec((tok_rows, width), lambda j: (0, j))
    return pl.pallas_call(
        unpack_kernel,
        out_shape=(packed, packed, jax.ShapeDtypeStruct((columns, HEAD_DIM), jnp.bfloat16)),
        grid=(blocks,),
        in_specs=[
            pl.BlockSpec((1, slots), lambda j: (0, 0)),
            pl.BlockSpec((tok_rows, 1), lambda j: (0, 0)),
            pl.BlockSpec((slots, width), lambda j: (0, j)),
            pl.BlockSpec((slots, width), lambda j: (0, blocks + j)),
        ],
        out_specs=(column_spec, column_spec, pl.BlockSpec((width, HEAD_DIM), lambda j: (j, 0))),
        scratch_shapes=[pltpu.VMEM((tok_rows, slots), jnp.bfloat16)],
        cost_estimate=pl.CostEstimate(
            flops=2 * tok_rows * columns * (2 * slots + HEAD_DIM),
            bytes_accessed=4 * columns * (slots + tok_rows),
            transcendentals=0,
        ),
        name="unpack_keys_values",
    )(land_row, tail, arrived, arrived)


def carry_kernel(keep_ref, updates_ref, carried_ref):
    count = updates_ref.shape[0]
    state = jnp.zeros(updates_ref.shape[1:], jnp.float32)
    carried_ref[0] = state.astype(carried_ref.dtype)
    for block in range(1, count):
        state = jnp.where(keep_ref[block] != 0, state, 0.0) + updates_ref[block - 1].astype(jnp.float32)
        carried_ref[block] = state.astype(carried_ref.dtype)


def carry_states(update, keep):
    seq_count = lax.axis_size("seq")
    share = update.shape[0] // seq_count
    updates = lax.all_to_all(update, "seq", split_axis=0, concat_axis=0, tiled=True)
    states = pl.pallas_call(
        carry_kernel,
        out_shape=jax.ShapeDtypeStruct((seq_count, share, HEAD_DIM), update.dtype),
        grid_spec=pltpu.PrefetchScalarGridSpec(
            num_scalar_prefetch=1,
            grid=(1,),
            in_specs=[pl.BlockSpec((seq_count, share, HEAD_DIM), lambda i, keep_ref: (0, 0, 0))],
            out_specs=pl.BlockSpec((seq_count, share, HEAD_DIM), lambda i, keep_ref: (0, 0, 0)),
        ),
        cost_estimate=pl.CostEstimate(
            flops=2 * update.size, bytes_accessed=4 * update.size, transcendentals=0
        ),
        name="carry_states",
    )(keep, updates.reshape(seq_count, share, HEAD_DIM))
    return lax.all_to_all(
        states.reshape(seq_count * share, HEAD_DIM), "seq", split_axis=0, concat_axis=0, tiled=True
    )


def attend_kernel(
    land_ref, seg_col_ref, seg_row_ref, carried_mask_ref, gain_ref, query_ref, keys_ref, values_ref,
    states_ref, out_ref, order, causal,
):
    tok_rows = order.shape[0]

    @pl.when(pl.program_id(0) == 0)
    def _():
        rows = lax.broadcasted_iota(jnp.int32, order.shape, 0)
        order[...] = jnp.where(land_ref[...] == rows, 1.0, 0.0).astype(order.dtype)
        later = lax.broadcasted_iota(jnp.int32, causal.shape, 0)
        earlier = lax.broadcasted_iota(jnp.int32, causal.shape, 1)
        open_pair = (earlier <= later) & (seg_col_ref[...] == seg_row_ref[...])
        causal[...] = jnp.where(open_pair, 1.0, 0.0)

    query = jnp.dot(order[...], query_ref[...], preferred_element_type=jnp.float32).astype(
        keys_ref.dtype
    )
    half = tok_rows // 2
    for part in range(query.shape[1] // HEAD_DIM):
        columns = slice(part * HEAD_DIM, (part + 1) * HEAD_DIM)
        for rows, reach in ((slice(0, half), half), (slice(half, tok_rows), tok_rows)):
            queries = query[rows, columns]
            scores = lax.dot_general(
                queries,
                keys_ref[:reach, columns],
                (((1,), (1,)), ((), ())),
                preferred_element_type=jnp.float32,
            )
            weights = jnp.where(causal[rows, :reach] != 0.0, scores, 0.0).astype(keys_ref.dtype)
            local_term = jnp.dot(
                weights, values_ref[:reach, columns], preferred_element_type=jnp.float32
            )
            carried_term = jnp.dot(
                queries, states_ref[columns, :], preferred_element_type=jnp.float32
            )
            raw_out = local_term + jnp.where(carried_mask_ref[rows, :] != 0, carried_term, 0.0)
            inv_rms = lax.rsqrt(jnp.mean(raw_out * raw_out, axis=1, keepdims=True) + norm_eps)
            out_ref[rows, columns] = (raw_out * inv_rms * gain_ref[:, columns]).astype(out_ref.dtype)


def attend(arrived, keys, values, states, land_row, seg_col, seg_row, carried_mask, gain):
    slots, columns = arrived.shape
    tok_rows = keys.shape[0]
    width = min(columns, 2 * HEAD_DIM)
    column_spec = pl.BlockSpec((tok_rows, width), lambda j: (0, j))
    return pl.pallas_call(
        attend_kernel,
        out_shape=jax.ShapeDtypeStruct((tok_rows, columns), jnp.bfloat16),
        grid=(columns // width,),
        in_specs=[
            pl.BlockSpec((1, slots), lambda j: (0, 0)),
            pl.BlockSpec((tok_rows, 1), lambda j: (0, 0)),
            pl.BlockSpec((1, tok_rows), lambda j: (0, 0)),
            pl.BlockSpec((tok_rows, 1), lambda j: (0, 0)),
            pl.BlockSpec((1, width), lambda j: (0, j)),
            pl.BlockSpec((slots, width), lambda j: (0, j)),
            column_spec,
            column_spec,
            pl.BlockSpec((width, HEAD_DIM), lambda j: (j, 0)),
        ],
        out_specs=column_spec,
        scratch_shapes=[
            pltpu.VMEM((tok_rows, slots), jnp.bfloat16),
            pltpu.VMEM((tok_rows, tok_rows), jnp.float32),
        ],
        cost_estimate=pl.CostEstimate(
            flops=2 * tok_rows * columns * (slots + 2 * tok_rows + HEAD_DIM),
            bytes_accessed=2 * columns * (slots + 3 * tok_rows),
            transcendentals=0,
        ),
        name="attend",
    )(land_row, seg_col, seg_row, carried_mask, gain, arrived, keys, values, states)


def send_packed(qkv, send_rows, plane_start, planes, start, columns):
    head_count = lax.axis_size("head")
    place = lax.axis_index("head")
    rows = qkv.shape[1]
    mine = qkv.shape[2] // head_count
    slots = send_rows.reshape(-1, 1)
    part = lax.slice_in_dim(qkv, plane_start, plane_start + planes, axis=0)
    if head_count == 2:
        low = part[:, :, start : start + columns]
        high = part[:, :, mine + start : mine + start + columns]
        outgoing = jnp.where(place == 0, high, low)
        incoming = lax.ppermute(outgoing, "head", [(0, 1), (1, 0)])
        picks = (slots - place * rows, slots - (1 - place) * rows)
        sources = (
            (qkv, plane_start, lambda at, width: at * (mine // width) + start // width),
            (incoming, 0, lambda at, width: 0),
        )
    else:
        split = part.reshape(planes, rows, head_count, mine)[..., start : start + columns]
        incoming = lax.all_to_all(
            jnp.moveaxis(split, 2, 0), "head", split_axis=0, concat_axis=0, tiled=False
        )
        incoming = jnp.moveaxis(incoming, 0, 1).reshape(planes, head_count * rows, columns)
        picks = (slots,)
        sources = ((incoming, 0, lambda at, width: 0),)
    outgoing = pack_rows(
        jnp.reshape(place, (1,)).astype(jnp.int32), picks, sources, planes, columns
    )
    return lax.all_to_all(outgoing, "seq", split_axis=0, concat_axis=0, tiled=True)


def on_device(qkv, send_rows, recv_pos, req_lengths, norm_gain):
    seq_count, head_count = lax.axis_size("seq"), lax.axis_size("head")
    block = lax.axis_index("seq")
    tok_rows = qkv.shape[1] * head_count
    columns = qkv.shape[2] // head_count
    half = columns // 2

    req_ends = jnp.cumsum(req_lengths)
    req_starts = req_ends - req_lengths
    first_row = block * tok_rows
    positions = first_row + jnp.arange(tok_rows, dtype=jnp.int32)
    segment = jnp.sum((req_starts[None, :] <= positions[:, None]).astype(jnp.int32), axis=1) - 1
    last_rows = (jnp.arange(seq_count, dtype=jnp.int32) + 1) * tok_rows - 1
    last_segment = jnp.sum((req_starts[None, :] <= last_rows[:, None]).astype(jnp.int32), axis=1) - 1
    prev_segment = jnp.sum((req_starts < first_row).astype(jnp.int32)) - 1
    keep = jnp.concatenate(
        [jnp.zeros((2,), jnp.int32), (last_segment[1:-1] == last_segment[:-2]).astype(jnp.int32)]
    )
    carried_mask = (segment == prev_segment).astype(jnp.int32)[:, None]
    tail = (segment == segment[tok_rows - 1]).astype(jnp.int32)[:, None]
    land_row = recv_pos[0].reshape(1, -1)
    gain = norm_gain.reshape(1, -1)

    arrived = [send_packed(qkv, send_rows[0], KEYS, 2, start, half) for start in (0, half)]
    query = send_packed(qkv, send_rows[0], QUERY, 1, 0, columns)
    keys, values, updates = zip(*[unpack_keys_values(part, land_row, tail, tok_rows) for part in arrived])
    states = carry_states(jnp.concatenate(updates, axis=0), keep)
    return attend(
        query,
        jnp.concatenate(keys, axis=1),
        jnp.concatenate(values, axis=1),
        states,
        land_row,
        segment[:, None],
        segment[None, :],
        carried_mask,
        gain,
    )


def solution(mesh):
    return jax.shard_map(
        on_device,
        mesh=mesh,
        in_specs=(
            P(None, ("seq", "head"), None),
            P("seq", None, None),
            P("seq", None, None),
            P(),
            P("head"),
        ),
        out_specs=P("seq", "head"),
        check_vma=False,
    )
```

```python
import math

import jax
import jax.numpy as jnp
from jax import lax
from jax.experimental import pallas as pl
from jax.experimental.pallas import tpu as pltpu
from jax.sharding import PartitionSpec as P

HEAD_DIM = 128

norm_eps = 1e-06

QUERY, KEYS, VALUES = 0, 1, 2


def pack_kernel(place_ref, *refs):
    count = (len(refs) - 1) // 3
    picks, sources = refs[:count], refs[count : 2 * count]
    out_ref, chosen = refs[2 * count], refs[2 * count + 1 :]

    @pl.when((pl.program_id(0) == 0) & (pl.program_id(1) == 0))
    def _():
        for pick, onehot in zip(picks, chosen):
            rows = lax.broadcasted_iota(jnp.int32, onehot.shape, 1)
            onehot[...] = jnp.where(pick[...] == rows, 1.0, 0.0).astype(onehot.dtype)

    total = None
    for source, onehot in zip(sources, chosen):
        part = jnp.dot(onehot[...], source[0], preferred_element_type=jnp.float32)
        total = part if total is None else total + part
    out_ref[...] = total.astype(out_ref.dtype)


def pack_rows(place, picks, sources, planes, columns, width):
    slots = picks[0].shape[0]
    blocks = columns // width
    lens = [array.shape[1] for array, _, _ in sources]

    def source_spec(array, plane_start, first):
        return pl.BlockSpec(
            (1, array.shape[1], width),
            lambda p, j, place_ref: (plane_start + p, 0, first(place_ref[0], width) + j),
        )

    return pl.pallas_call(
        pack_kernel,
        out_shape=jax.ShapeDtypeStruct((slots, planes * columns), jnp.bfloat16),
        grid_spec=pltpu.PrefetchScalarGridSpec(
            num_scalar_prefetch=1,
            grid=(planes, blocks),
            in_specs=[pl.BlockSpec((slots, 1), lambda p, j, place_ref: (0, 0)) for _ in picks]
            + [source_spec(*source) for source in sources],
            out_specs=pl.BlockSpec((slots, width), lambda p, j, place_ref: (0, p * blocks + j)),
            scratch_shapes=[pltpu.VMEM((slots, length), jnp.bfloat16) for length in lens],
        ),
        cost_estimate=pl.CostEstimate(
            flops=2 * slots * sum(lens) * planes * columns,
            bytes_accessed=2 * planes * columns * (slots + sum(lens)),
            transcendentals=0,
        ),
        name="pack_rows",
    )(place, *picks, *[array for array, _, _ in sources])


def unpack_kernel(land_ref, tail_ref, keys_ref, values_ref, *refs):
    keys_out, values_out, update_ref, order = refs[-4:]

    @pl.when(pl.program_id(0) == 0)
    def _():
        rows = lax.broadcasted_iota(jnp.int32, order.shape, 0)
        order[...] = jnp.where(land_ref[...] == rows, 1.0, 0.0).astype(order.dtype)

    keys = jnp.dot(order[...], keys_ref[...], preferred_element_type=jnp.float32)
    keys_out[...] = keys.astype(keys_out.dtype)
    values = jnp.dot(order[...], values_ref[...], preferred_element_type=jnp.float32).astype(
        values_out.dtype
    )
    values_out[...] = values
    tail_keys = jnp.where(tail_ref[...] != 0, keys, 0.0).astype(values.dtype)
    for part in range(keys.shape[1] // HEAD_DIM):
        columns = slice(part * HEAD_DIM, (part + 1) * HEAD_DIM)
        update_ref[columns, :] = lax.dot_general(
            tail_keys[:, columns],
            values[:, columns],
            (((0,), (0,)), ((), ())),
            preferred_element_type=jnp.float32,
        )


def unpack_keys_values(arrived, land_row, tail, tok_rows, start, mine, filled):
    slots, columns = arrived.shape[0], arrived.shape[1] // 2
    width = min(columns, 2 * HEAD_DIM)
    blocks, first = columns // width, start // width
    packed = jax.ShapeDtypeStruct((tok_rows, mine), arrived.dtype)
    column_spec = pl.BlockSpec((tok_rows, width), lambda j: (0, first + j))
    return pl.pallas_call(
        unpack_kernel,
        out_shape=(packed, packed, jax.ShapeDtypeStruct((mine, HEAD_DIM), jnp.float32)),
        grid=(blocks,),
        in_specs=[
            pl.BlockSpec((1, slots), lambda j: (0, 0)),
            pl.BlockSpec((tok_rows, 1), lambda j: (0, 0)),
            pl.BlockSpec((slots, width), lambda j: (0, j)),
            pl.BlockSpec((slots, width), lambda j: (0, blocks + j)),
        ]
        + [pl.BlockSpec(memory_space=pl.ANY) for _ in filled],
        out_specs=(
            column_spec,
            column_spec,
            pl.BlockSpec((width, HEAD_DIM), lambda j: (first + j, 0)),
        ),
        scratch_shapes=[pltpu.VMEM((tok_rows, slots), jnp.bfloat16)],
        input_output_aliases={4 + number: number for number in range(len(filled))},
        cost_estimate=pl.CostEstimate(
            flops=2 * tok_rows * columns * (2 * slots + HEAD_DIM),
            bytes_accessed=4 * columns * (slots + tok_rows),
            transcendentals=0,
        ),
        name="unpack_keys_values",
    )(land_row, tail, arrived, arrived, *filled)


def sum_kernel(take_ref, *refs):
    count = take_ref.shape[1]
    pieces, outs = refs[:count], refs[count:]
    number = 0
    for out in outs:
        for part in range(out.shape[0]):
            total = jnp.zeros(out.shape[1:], jnp.float32)
            for piece in range(count):
                wanted = take_ref[number, piece] != 0
                total = total + jnp.where(wanted, pieces[piece][...], 0.0)
            out[part] = total
            number += 1


def sum_pieces(take, pieces, counts):
    rows = pieces[0].shape[0]
    step = math.gcd(rows, 128)
    return pl.pallas_call(
        sum_kernel,
        out_shape=tuple(jax.ShapeDtypeStruct((n, rows, HEAD_DIM), jnp.float32) for n in counts),
        grid_spec=pltpu.PrefetchScalarGridSpec(
            num_scalar_prefetch=1,
            grid=(rows // step,),
            in_specs=[pl.BlockSpec((step, HEAD_DIM), lambda i, take_ref: (i, 0)) for _ in pieces],
            out_specs=tuple(
                pl.BlockSpec((n, step, HEAD_DIM), lambda i, take_ref: (0, i, 0)) for n in counts
            ),
        ),
        cost_estimate=pl.CostEstimate(
            flops=sum(counts) * len(pieces) * rows * HEAD_DIM,
            bytes_accessed=4 * (len(pieces) + sum(counts)) * rows * HEAD_DIM,
            transcendentals=0,
        ),
        name="sum_pieces",
    )(take.astype(jnp.int32), *pieces)


def carry_states(update, last_segment):
    seq_count, block = lax.axis_size("seq"), lax.axis_index("seq")
    near = math.gcd(seq_count, 4)
    far = seq_count // near
    share = update.shape[0] // near
    place, run = block % near, block // near
    base = run * near

    def swap(value, k):
        return lax.ppermute(value, "seq", [(i, i ^ k) for i in range(seq_count)])

    pieces = [lax.dynamic_slice_in_dim(update, place * share, share, axis=0)]
    for k in range(1, near):
        mine = lax.dynamic_slice_in_dim(update, (place ^ k) * share, share, axis=0)
        pieces.append(swap(mine, k))
    source = base + (place ^ jnp.arange(near))
    before = jnp.maximum(source - 1, 0)
    inside = (source[None, :] < source[:, None]) & (
        last_segment[source][None, :] == last_segment[before][:, None]
    )
    whole = last_segment[source] == last_segment[base + near - 1]
    inner, total = sum_pieces(jnp.concatenate([inside, whole[None]]), pieces, (near, 1))
    total = total[0]

    def ends(run_number):
        return last_segment[jnp.maximum(run_number, 0) * near + near - 1]

    entering, window, reach = None, total, 1
    while reach < far:
        shifted = lax.ppermute(
            window, "seq", [(i, i + reach * near) for i in range(seq_count - reach * near)]
        )
        same_start = (run >= reach) & (ends(run - reach) == ends(run - 1))
        same_end = (run >= reach) & (ends(run - reach) == ends(run))
        shifted_in = jnp.where(same_start, shifted, 0.0)
        entering = shifted_in if entering is None else entering + shifted_in
        window = window + jnp.where(same_end, shifted, 0.0)
        reach *= 2
    handed = []
    for k in range(near):
        state = inner[k]
        if entering is not None:
            same = (run >= 1) & (last_segment[before[k]] == ends(run - 1))
            state = state + jnp.where(same, entering, 0.0)
        handed.append(state if k == 0 else swap(state, k))
    stacked = jnp.stack(handed)
    return [
        lax.dynamic_index_in_dim(stacked, place ^ number, axis=0, keepdims=False)
        for number in range(near)
    ]


def attend_kernel(
    land_ref, seg_col_ref, seg_row_ref, carried_mask_ref, gain_ref, query_ref, keys_ref, values_ref,
    states_ref, out_ref, order, causal,
):
    tok_rows = order.shape[0]

    @pl.when(pl.program_id(0) == 0)
    def _():
        rows = lax.broadcasted_iota(jnp.int32, order.shape, 0)
        order[...] = jnp.where(land_ref[...] == rows, 1.0, 0.0).astype(order.dtype)
        later = lax.broadcasted_iota(jnp.int32, causal.shape, 0)
        earlier = lax.broadcasted_iota(jnp.int32, causal.shape, 1)
        open_pair = (earlier <= later) & (seg_col_ref[...] == seg_row_ref[...])
        causal[...] = jnp.where(open_pair, 1.0, 0.0)

    query = jnp.dot(order[...], query_ref[...], preferred_element_type=jnp.float32).astype(
        keys_ref.dtype
    )
    state_high = states_ref[...].astype(query.dtype)
    state_low = (states_ref[...] - state_high.astype(jnp.float32)).astype(query.dtype)
    half = tok_rows // 2
    for part in range(query.shape[1] // HEAD_DIM):
        columns = slice(part * HEAD_DIM, (part + 1) * HEAD_DIM)
        for rows, reach in ((slice(0, half), half), (slice(half, tok_rows), tok_rows)):
            queries = query[rows, columns]
            scores = lax.dot_general(
                queries,
                keys_ref[:reach, columns],
                (((1,), (1,)), ((), ())),
                preferred_element_type=jnp.float32,
            )
            weights = jnp.where(causal[rows, :reach] != 0.0, scores, 0.0).astype(keys_ref.dtype)
            local_term = jnp.dot(
                weights, values_ref[:reach, columns], preferred_element_type=jnp.float32
            )
            carried_term = jnp.dot(
                queries, state_high[columns], preferred_element_type=jnp.float32
            ) + jnp.dot(queries, state_low[columns], preferred_element_type=jnp.float32)
            raw_out = local_term + jnp.where(carried_mask_ref[rows, :] != 0, carried_term, 0.0)
            inv_rms = lax.rsqrt(jnp.mean(raw_out * raw_out, axis=1, keepdims=True) + norm_eps)
            out_ref[rows, columns] = (raw_out * inv_rms * gain_ref[:, columns]).astype(out_ref.dtype)


def attend(arrived, keys, values, states, land_row, seg_col, seg_row, carried_mask, gain):
    slots, columns = arrived.shape
    tok_rows = keys.shape[0]
    width = min(columns, 2 * HEAD_DIM)
    column_spec = pl.BlockSpec((tok_rows, width), lambda j: (0, j))
    return pl.pallas_call(
        attend_kernel,
        out_shape=jax.ShapeDtypeStruct((tok_rows, columns), jnp.bfloat16),
        grid=(columns // width,),
        in_specs=[
            pl.BlockSpec((1, slots), lambda j: (0, 0)),
            pl.BlockSpec((tok_rows, 1), lambda j: (0, 0)),
            pl.BlockSpec((1, tok_rows), lambda j: (0, 0)),
            pl.BlockSpec((tok_rows, 1), lambda j: (0, 0)),
            pl.BlockSpec((1, width), lambda j: (0, j)),
            pl.BlockSpec((slots, width), lambda j: (0, j)),
            column_spec,
            column_spec,
            pl.BlockSpec((width, HEAD_DIM), lambda j: (j, 0)),
        ],
        out_specs=column_spec,
        scratch_shapes=[
            pltpu.VMEM((tok_rows, slots), jnp.bfloat16),
            pltpu.VMEM((tok_rows, tok_rows), jnp.float32),
        ],
        cost_estimate=pl.CostEstimate(
            flops=2 * tok_rows * columns * (slots + 2 * tok_rows + HEAD_DIM),
            bytes_accessed=2 * columns * (slots + 3 * tok_rows),
            transcendentals=0,
        ),
        name="attend",
    )(land_row, seg_col, seg_row, carried_mask, gain, arrived, keys, values, states)


def send_packed(qkv, send_rows, plane_start, planes, start, columns):
    head_count = lax.axis_size("head")
    place = lax.axis_index("head")
    rows = qkv.shape[1]
    mine = qkv.shape[2] // head_count
    slots = send_rows.reshape(-1, 1)
    width = math.gcd(math.gcd(columns, start), math.gcd(mine, 512))
    part = lax.slice_in_dim(qkv, plane_start, plane_start + planes, axis=0)
    if head_count == 2:
        low = part[:, :, start : start + columns]
        high = part[:, :, mine + start : mine + start + columns]
        outgoing = jnp.where(place == 0, high, low)
        incoming = lax.ppermute(outgoing, "head", [(0, 1), (1, 0)])
        picks = (slots - place * rows, slots - (1 - place) * rows)
        sources = (
            (qkv, plane_start, lambda at, width: at * (mine // width) + start // width),
            (incoming, 0, lambda at, width: 0),
        )
    else:
        split = part.reshape(planes, rows, head_count, mine)[..., start : start + columns]
        incoming = lax.all_to_all(
            jnp.moveaxis(split, 2, 0), "head", split_axis=0, concat_axis=0, tiled=False
        )
        incoming = jnp.moveaxis(incoming, 0, 1).reshape(planes, head_count * rows, columns)
        picks = (slots,)
        sources = ((incoming, 0, lambda at, width: 0),)
    outgoing = pack_rows(
        jnp.reshape(place, (1,)).astype(jnp.int32), picks, sources, planes, columns, width
    )
    return lax.all_to_all(outgoing, "seq", split_axis=0, concat_axis=0, tiled=True)


def on_device(qkv, send_rows, recv_pos, req_lengths, norm_gain):
    seq_count, head_count = lax.axis_size("seq"), lax.axis_size("head")
    block = lax.axis_index("seq")
    tok_rows = qkv.shape[1] * head_count
    columns = qkv.shape[2] // head_count

    req_ends = jnp.cumsum(req_lengths)
    req_starts = req_ends - req_lengths
    first_row = block * tok_rows
    positions = first_row + jnp.arange(tok_rows, dtype=jnp.int32)
    segment = jnp.sum((req_starts[None, :] <= positions[:, None]).astype(jnp.int32), axis=1) - 1
    last_rows = (jnp.arange(seq_count, dtype=jnp.int32) + 1) * tok_rows - 1
    last_segment = jnp.sum((req_starts[None, :] <= last_rows[:, None]).astype(jnp.int32), axis=1) - 1
    prev_segment = jnp.sum((req_starts < first_row).astype(jnp.int32)) - 1
    carried_mask = (segment == prev_segment).astype(jnp.int32)[:, None]
    tail = (segment == segment[tok_rows - 1]).astype(jnp.int32)[:, None]
    land_row = recv_pos[0].reshape(1, -1)
    gain = norm_gain.reshape(1, -1)

    head_share = columns // HEAD_DIM
    first = max(1, 3 * head_share // 16) * 2 * HEAD_DIM
    arrived = []
    for start, size in ((0, first), (first, columns - first)):
        arrived.append((start, send_packed(qkv, send_rows[0], KEYS, 2, start, size)))
    query = send_packed(qkv, send_rows[0], QUERY, 1, 0, columns)
    filled = ()
    for start, part in arrived:
        filled = unpack_keys_values(part, land_row, tail, tok_rows, start, columns, filled)
    keys, values, update = filled
    states = jnp.concatenate(carry_states(update, last_segment), axis=0)
    return attend(
        query, keys, values, states, land_row, segment[:, None], segment[None, :], carried_mask, gain
    )


def solution(mesh):
    return jax.shard_map(
        on_device,
        mesh=mesh,
        in_specs=(
            P(None, ("seq", "head"), None),
            P("seq", None, None),
            P("seq", None, None),
            P(),
            P("head"),
        ),
        out_specs=P("seq", "head"),
        check_vma=False,
    )
```

```python
import math

import jax
import jax.numpy as jnp
from jax import lax
from jax.experimental import pallas as pl
from jax.experimental.pallas import tpu as pltpu
from jax.sharding import PartitionSpec as P

HEAD_DIM = 128

norm_eps = 1e-06

QUERY, KEYS, VALUES = 0, 1, 2


def pack_kernel(place_ref, *refs):
    count = (len(refs) - 1) // 3
    picks, sources = refs[:count], refs[count : 2 * count]
    out_ref, chosen = refs[2 * count], refs[2 * count + 1 :]

    @pl.when((pl.program_id(0) == 0) & (pl.program_id(1) == 0))
    def _():
        for pick, onehot in zip(picks, chosen):
            rows = lax.broadcasted_iota(jnp.int32, onehot.shape, 1)
            onehot[...] = jnp.where(pick[...] == rows, 1.0, 0.0).astype(onehot.dtype)

    total = None
    for source, onehot in zip(sources, chosen):
        part = jnp.dot(onehot[...], source[0], preferred_element_type=jnp.float32)
        total = part if total is None else total + part
    out_ref[...] = total.astype(out_ref.dtype)


def pack_rows(place, picks, sources, planes, columns, width):
    slots = picks[0].shape[0]
    blocks = columns // width
    lens = [array.shape[1] for array, _, _ in sources]

    def source_spec(array, plane_start, first):
        return pl.BlockSpec(
            (1, array.shape[1], width),
            lambda p, j, place_ref: (plane_start + p, 0, first(place_ref[0], width) + j),
        )

    return pl.pallas_call(
        pack_kernel,
        out_shape=jax.ShapeDtypeStruct((slots, planes * columns), jnp.bfloat16),
        grid_spec=pltpu.PrefetchScalarGridSpec(
            num_scalar_prefetch=1,
            grid=(planes, blocks),
            in_specs=[pl.BlockSpec((slots, 1), lambda p, j, place_ref: (0, 0)) for _ in picks]
            + [source_spec(*source) for source in sources],
            out_specs=pl.BlockSpec((slots, width), lambda p, j, place_ref: (0, p * blocks + j)),
            scratch_shapes=[pltpu.VMEM((slots, length), jnp.bfloat16) for length in lens],
        ),
        cost_estimate=pl.CostEstimate(
            flops=2 * slots * sum(lens) * planes * columns,
            bytes_accessed=2 * planes * columns * (slots + sum(lens)),
            transcendentals=0,
        ),
        name="pack_rows",
    )(place, *picks, *[array for array, _, _ in sources])


def update_kernel(tail_ref, keys_ref, values_ref, update_ref):
    tail = tail_ref[...] != 0
    for part in range(keys_ref.shape[1] // HEAD_DIM):
        columns = slice(part * HEAD_DIM, (part + 1) * HEAD_DIM)
        keys = keys_ref[:, columns]
        update_ref[columns, :] = lax.dot_general(
            jnp.where(tail, keys, jnp.zeros_like(keys)),
            values_ref[:, columns],
            (((0,), (0,)), ((), ())),
            preferred_element_type=jnp.float32,
        )


def block_update(arrived, tail_slots):
    slots, columns = arrived.shape[0], arrived.shape[1] // 2
    width = min(columns, 2 * HEAD_DIM)
    blocks = columns // width
    return pl.pallas_call(
        update_kernel,
        out_shape=jax.ShapeDtypeStruct((columns, HEAD_DIM), jnp.float32),
        grid=(blocks,),
        in_specs=[
            pl.BlockSpec((slots, 1), lambda j: (0, 0)),
            pl.BlockSpec((slots, width), lambda j: (0, j)),
            pl.BlockSpec((slots, width), lambda j: (0, blocks + j)),
        ],
        out_specs=pl.BlockSpec((width, HEAD_DIM), lambda j: (j, 0)),
        cost_estimate=pl.CostEstimate(
            flops=2 * slots * columns * HEAD_DIM,
            bytes_accessed=4 * columns * (slots + HEAD_DIM),
            transcendentals=0,
        ),
        name="block_update",
    )(tail_slots, arrived, arrived)


def unpack_kernel(land_ref, keys_ref, values_ref, *refs):
    keys_out, values_out, order = refs[-3:]

    @pl.when(pl.program_id(0) == 0)
    def _():
        rows = lax.broadcasted_iota(jnp.int32, order.shape, 0)
        order[...] = jnp.where(land_ref[...] == rows, 1.0, 0.0).astype(order.dtype)

    for source, out in ((keys_ref, keys_out), (values_ref, values_out)):
        out[...] = jnp.dot(
            order[...], source[...], preferred_element_type=jnp.float32
        ).astype(out.dtype)


def unpack_keys_values(arrived, land_row, tok_rows, start, mine, filled):
    slots, columns = arrived.shape[0], arrived.shape[1] // 2
    width = min(columns, 2 * HEAD_DIM)
    blocks, first = columns // width, start // width
    packed = jax.ShapeDtypeStruct((tok_rows, mine), arrived.dtype)
    column_spec = pl.BlockSpec((tok_rows, width), lambda j: (0, first + j))
    return pl.pallas_call(
        unpack_kernel,
        out_shape=(packed, packed),
        grid=(blocks,),
        in_specs=[
            pl.BlockSpec((1, slots), lambda j: (0, 0)),
            pl.BlockSpec((slots, width), lambda j: (0, j)),
            pl.BlockSpec((slots, width), lambda j: (0, blocks + j)),
        ]
        + [pl.BlockSpec(memory_space=pl.ANY) for _ in filled],
        out_specs=(column_spec, column_spec),
        scratch_shapes=[pltpu.VMEM((tok_rows, slots), jnp.bfloat16)],
        input_output_aliases={3 + number: number for number in range(len(filled))},
        cost_estimate=pl.CostEstimate(
            flops=4 * tok_rows * columns * slots,
            bytes_accessed=4 * columns * (slots + tok_rows),
            transcendentals=0,
        ),
        name="unpack_keys_values",
    )(land_row, arrived, arrived, *filled)


def sum_kernel(take_ref, *refs):
    count = take_ref.shape[1]
    pieces, outs = refs[:count], refs[count:]
    number = 0
    for out in outs:
        for part in range(out.shape[0]):
            total = jnp.zeros(out.shape[1:], jnp.float32)
            for piece in range(count):
                wanted = take_ref[number, piece] != 0
                total = total + jnp.where(wanted, pieces[piece][...], 0.0)
            out[part] = total
            number += 1


def sum_pieces(take, pieces, counts):
    rows = pieces[0].shape[0]
    step = rows // 2
    return pl.pallas_call(
        sum_kernel,
        out_shape=tuple(jax.ShapeDtypeStruct((n, rows, HEAD_DIM), jnp.float32) for n in counts),
        grid_spec=pltpu.PrefetchScalarGridSpec(
            num_scalar_prefetch=1,
            grid=(rows // step,),
            in_specs=[pl.BlockSpec((step, HEAD_DIM), lambda i, take_ref: (i, 0)) for _ in pieces],
            out_specs=tuple(
                pl.BlockSpec((n, step, HEAD_DIM), lambda i, take_ref: (0, i, 0)) for n in counts
            ),
        ),
        cost_estimate=pl.CostEstimate(
            flops=sum(counts) * len(pieces) * rows * HEAD_DIM,
            bytes_accessed=4 * (len(pieces) + sum(counts)) * rows * HEAD_DIM,
            transcendentals=0,
        ),
        name="sum_pieces",
    )(take.astype(jnp.int32), *pieces)


def carry_states(update, last_segment):
    seq_count, block = lax.axis_size("seq"), lax.axis_index("seq")
    near = math.gcd(seq_count, 4)
    far = seq_count // near
    share = update.shape[0] // near
    place, run = block % near, block // near
    base = run * near

    def swap(value, k):
        return lax.ppermute(value, "seq", [(i, i ^ k) for i in range(seq_count)])

    pieces = [lax.dynamic_slice_in_dim(update, place * share, share, axis=0)]
    for k in range(1, near):
        mine = lax.dynamic_slice_in_dim(update, (place ^ k) * share, share, axis=0)
        pieces.append(swap(mine, k))
    source = base + (place ^ jnp.arange(near))
    before = jnp.maximum(source - 1, 0)
    inside = (source[None, :] < source[:, None]) & (
        last_segment[source][None, :] == last_segment[before][:, None]
    )
    whole = last_segment[source] == last_segment[base + near - 1]
    inner, total = sum_pieces(jnp.concatenate([inside, whole[None]]), pieces, (near, 1))
    total = total[0]

    def ends(run_number):
        return last_segment[jnp.maximum(run_number, 0) * near + near - 1]

    entering, window, reach = None, total, 1
    while reach < far:
        shifted = lax.ppermute(
            window, "seq", [(i, i + reach * near) for i in range(seq_count - reach * near)]
        )
        same_start = (run >= reach) & (ends(run - reach) == ends(run - 1))
        same_end = (run >= reach) & (ends(run - reach) == ends(run))
        shifted_in = jnp.where(same_start, shifted, 0.0)
        entering = shifted_in if entering is None else entering + shifted_in
        window = window + jnp.where(same_end, shifted, 0.0)
        reach *= 2
    handed = []
    for k in range(near):
        state = inner[k]
        if entering is not None:
            same = (run >= 1) & (last_segment[before[k]] == ends(run - 1))
            state = state + jnp.where(same, entering, 0.0)
        handed.append(state if k == 0 else swap(state, k))
    stacked = jnp.stack(handed)
    return [
        lax.dynamic_index_in_dim(stacked, place ^ number, axis=0, keepdims=False)
        for number in range(near)
    ]


def attend_kernel(
    land_ref, seg_col_ref, seg_row_ref, carried_mask_ref, gain_ref, query_ref, keys_ref, values_ref,
    states_ref, out_ref, order, causal,
):
    tok_rows = order.shape[0]

    @pl.when(pl.program_id(0) == 0)
    def _():
        rows = lax.broadcasted_iota(jnp.int32, order.shape, 0)
        order[...] = jnp.where(land_ref[...] == rows, 1.0, 0.0).astype(order.dtype)
        later = lax.broadcasted_iota(jnp.int32, causal.shape, 0)
        earlier = lax.broadcasted_iota(jnp.int32, causal.shape, 1)
        open_pair = (earlier <= later) & (seg_col_ref[...] == seg_row_ref[...])
        causal[...] = jnp.where(open_pair, 1.0, 0.0)

    query = jnp.dot(order[...], query_ref[...], preferred_element_type=jnp.float32).astype(
        keys_ref.dtype
    )
    state_high = states_ref[...].astype(query.dtype)
    state_low = (states_ref[...] - state_high.astype(jnp.float32)).astype(query.dtype)
    half = tok_rows // 2
    for part in range(query.shape[1] // HEAD_DIM):
        columns = slice(part * HEAD_DIM, (part + 1) * HEAD_DIM)
        for rows, reach in ((slice(0, half), half), (slice(half, tok_rows), tok_rows)):
            queries = query[rows, columns]
            scores = lax.dot_general(
                queries,
                keys_ref[:reach, columns],
                (((1,), (1,)), ((), ())),
                preferred_element_type=jnp.float32,
            )
            weights = jnp.where(causal[rows, :reach] != 0.0, scores, 0.0).astype(keys_ref.dtype)
            local_term = jnp.dot(
                weights, values_ref[:reach, columns], preferred_element_type=jnp.float32
            )
            carried_term = jnp.dot(
                queries, state_high[columns], preferred_element_type=jnp.float32
            ) + jnp.dot(queries, state_low[columns], preferred_element_type=jnp.float32)
            raw_out = local_term + jnp.where(carried_mask_ref[rows, :] != 0, carried_term, 0.0)
            inv_rms = lax.rsqrt(jnp.mean(raw_out * raw_out, axis=1, keepdims=True) + norm_eps)
            out_ref[rows, columns] = (raw_out * inv_rms * gain_ref[:, columns]).astype(out_ref.dtype)


def attend(arrived, keys, values, states, land_row, seg_col, seg_row, carried_mask, gain):
    slots, columns = arrived.shape
    tok_rows = keys.shape[0]
    width = min(columns, 2 * HEAD_DIM)
    column_spec = pl.BlockSpec((tok_rows, width), lambda j: (0, j))
    return pl.pallas_call(
        attend_kernel,
        out_shape=jax.ShapeDtypeStruct((tok_rows, columns), jnp.bfloat16),
        grid=(columns // width,),
        in_specs=[
            pl.BlockSpec((1, slots), lambda j: (0, 0)),
            pl.BlockSpec((tok_rows, 1), lambda j: (0, 0)),
            pl.BlockSpec((1, tok_rows), lambda j: (0, 0)),
            pl.BlockSpec((tok_rows, 1), lambda j: (0, 0)),
            pl.BlockSpec((1, width), lambda j: (0, j)),
            pl.BlockSpec((slots, width), lambda j: (0, j)),
            column_spec,
            column_spec,
            pl.BlockSpec((width, HEAD_DIM), lambda j: (j, 0)),
        ],
        out_specs=column_spec,
        scratch_shapes=[
            pltpu.VMEM((tok_rows, slots), jnp.bfloat16),
            pltpu.VMEM((tok_rows, tok_rows), jnp.float32),
        ],
        cost_estimate=pl.CostEstimate(
            flops=2 * tok_rows * columns * (slots + 2 * tok_rows + HEAD_DIM),
            bytes_accessed=2 * columns * (slots + 3 * tok_rows),
            transcendentals=0,
        ),
        name="attend",
    )(land_row, seg_col, seg_row, carried_mask, gain, arrived, keys, values, states)


def swap_heads(qkv, plane_start, planes, start, columns):
    head_count = lax.axis_size("head")
    rows = qkv.shape[1]
    mine = qkv.shape[2] // head_count
    part = lax.slice_in_dim(qkv, plane_start, plane_start + planes, axis=0)
    if head_count == 2:
        low = part[:, :, start : start + columns]
        high = part[:, :, mine + start : mine + start + columns]
        outgoing = jnp.where(lax.axis_index("head") == 0, high, low)
        return lax.ppermute(outgoing, "head", [(0, 1), (1, 0)])
    split = part.reshape(planes, rows, head_count, mine)[..., start : start + columns]
    incoming = lax.all_to_all(
        jnp.moveaxis(split, 2, 0), "head", split_axis=0, concat_axis=0, tiled=False
    )
    return jnp.moveaxis(incoming, 0, 1).reshape(planes, head_count * rows, columns)


def send_packed(qkv, incoming, send_rows, plane_start, planes, start, columns):
    head_count = lax.axis_size("head")
    place = lax.axis_index("head")
    rows = qkv.shape[1]
    mine = qkv.shape[2] // head_count
    slots = send_rows.reshape(-1, 1)
    width = math.gcd(math.gcd(columns, start), math.gcd(mine, 512))
    picks, sources = (slots,), ((incoming, 0, lambda at, width: 0),)
    if head_count == 2:
        picks = (slots - place * rows, slots - (1 - place) * rows)
        sources = (
            (qkv, plane_start, lambda at, width: at * (mine // width) + start // width),
        ) + sources
    outgoing = pack_rows(
        jnp.reshape(place, (1,)).astype(jnp.int32), picks, sources, planes, columns, width
    )
    return lax.all_to_all(outgoing, "seq", split_axis=0, concat_axis=0, tiled=True)


def on_device(qkv, send_rows, recv_pos, req_lengths, norm_gain):
    seq_count, head_count = lax.axis_size("seq"), lax.axis_size("head")
    block = lax.axis_index("seq")
    tok_rows = qkv.shape[1] * head_count
    columns = qkv.shape[2] // head_count

    req_ends = jnp.cumsum(req_lengths)
    req_starts = req_ends - req_lengths
    first_row = block * tok_rows
    positions = first_row + jnp.arange(tok_rows, dtype=jnp.int32)
    segment = jnp.sum((req_starts[None, :] <= positions[:, None]).astype(jnp.int32), axis=1) - 1
    last_rows = (jnp.arange(seq_count, dtype=jnp.int32) + 1) * tok_rows - 1
    last_segment = jnp.sum((req_starts[None, :] <= last_rows[:, None]).astype(jnp.int32), axis=1) - 1
    prev_segment = jnp.sum((req_starts < first_row).astype(jnp.int32)) - 1
    carried_mask = (segment == prev_segment).astype(jnp.int32)[:, None]
    land_row = recv_pos[0].reshape(1, -1)
    landing = first_row + land_row.reshape(-1, 1)
    landing_segment = jnp.sum((req_starts[None, :] <= landing).astype(jnp.int32), axis=1, keepdims=True) - 1
    in_tail = (land_row.reshape(-1, 1) >= 0) & (landing_segment == last_segment[block])
    tail_slots = in_tail.astype(jnp.int32)
    gain = norm_gain.reshape(1, -1)

    rows = send_rows[0]
    head_share = columns // HEAD_DIM
    first = max(1, 3 * head_share // 16) * 2 * HEAD_DIM
    second = columns - first
    arrived = send_packed(
        qkv, swap_heads(qkv, KEYS, 2, 0, first), rows, KEYS, 2, 0, first
    )
    arrived_next = send_packed(
        qkv, swap_heads(qkv, KEYS, 2, first, second), rows, KEYS, 2, first, second
    )
    states = carry_states(block_update(arrived, tail_slots), last_segment)
    filled = unpack_keys_values(arrived, land_row, tok_rows, 0, columns, ())
    incoming = swap_heads(qkv, QUERY, 1, 0, columns)
    incoming, states, filled, tail_slots, last_segment, segment, carried_mask = lax.optimization_barrier(
        (incoming, states, filled, tail_slots, last_segment, segment, carried_mask)
    )
    query = send_packed(qkv, incoming, rows, QUERY, 1, 0, columns)
    states += carry_states(block_update(arrived_next, tail_slots), last_segment)
    keys, values = unpack_keys_values(arrived_next, land_row, tok_rows, first, columns, filled)
    return attend(
        query,
        keys,
        values,
        jnp.concatenate(states, axis=0),
        land_row,
        segment[:, None],
        segment[None, :],
        carried_mask,
        gain,
    )


def solution(mesh):
    return jax.shard_map(
        on_device,
        mesh=mesh,
        in_specs=(
            P(None, ("seq", "head"), None),
            P("seq", None, None),
            P("seq", None, None),
            P(),
            P("head"),
        ),
        out_specs=P("seq", "head"),
        check_vma=False,
    )
```

```python
import math

import jax
import jax.numpy as jnp
from jax import lax
from jax.experimental import pallas as pl
from jax.experimental.pallas import tpu as pltpu
from jax.sharding import PartitionSpec as P

HEAD_DIM = 128

norm_eps = 1e-06

QUERY, KEYS, VALUES = 0, 1, 2


def pack_kernel(place_ref, *refs):
    count = (len(refs) - 1) // 3
    picks, sources = refs[:count], refs[count : 2 * count]
    out_ref, chosen = refs[2 * count], refs[2 * count + 1 :]

    @pl.when((pl.program_id(0) == 0) & (pl.program_id(1) == 0))
    def _():
        for pick, onehot in zip(picks, chosen):
            rows = lax.broadcasted_iota(jnp.int32, onehot.shape, 1)
            onehot[...] = jnp.where(pick[...] == rows, 1.0, 0.0).astype(onehot.dtype)

    total = None
    for source, onehot in zip(sources, chosen):
        part = jnp.dot(onehot[...], source[0], preferred_element_type=jnp.float32)
        total = part if total is None else total + part
    out_ref[...] = total.astype(out_ref.dtype)


def pack_rows(place, picks, sources, planes, columns, width):
    slots = picks[0].shape[0]
    blocks = columns // width
    lens = [array.shape[1] for array, _, _ in sources]

    def source_spec(array, plane_start, first):
        return pl.BlockSpec(
            (1, array.shape[1], width),
            lambda p, j, place_ref: (plane_start + p, 0, first(place_ref[0], width) + j),
        )

    return pl.pallas_call(
        pack_kernel,
        out_shape=jax.ShapeDtypeStruct((slots, planes * columns), jnp.bfloat16),
        grid_spec=pltpu.PrefetchScalarGridSpec(
            num_scalar_prefetch=1,
            grid=(planes, blocks),
            in_specs=[pl.BlockSpec((slots, 1), lambda p, j, place_ref: (0, 0)) for _ in picks]
            + [source_spec(*source) for source in sources],
            out_specs=pl.BlockSpec((slots, width), lambda p, j, place_ref: (0, p * blocks + j)),
            scratch_shapes=[pltpu.VMEM((slots, length), jnp.bfloat16) for length in lens],
        ),
        cost_estimate=pl.CostEstimate(
            flops=2 * slots * sum(lens) * planes * columns,
            bytes_accessed=2 * planes * columns * (slots + sum(lens)),
            transcendentals=0,
        ),
        name="pack_rows",
    )(place, *picks, *[array for array, _, _ in sources])


def update_kernel(tail_ref, keys_ref, values_ref, update_ref):
    tail = tail_ref[...] != 0
    for part in range(keys_ref.shape[1] // HEAD_DIM):
        columns = slice(part * HEAD_DIM, (part + 1) * HEAD_DIM)
        keys = keys_ref[:, columns]
        update_ref[columns, :] = lax.dot_general(
            jnp.where(tail, keys, jnp.zeros_like(keys)),
            values_ref[:, columns],
            (((0,), (0,)), ((), ())),
            preferred_element_type=jnp.float32,
        )


def block_update(arrived, tail_slots):
    slots, columns = arrived.shape[0], arrived.shape[1] // 2
    width = min(columns, 2 * HEAD_DIM)
    blocks = columns // width
    return pl.pallas_call(
        update_kernel,
        out_shape=jax.ShapeDtypeStruct((columns, HEAD_DIM), jnp.float32),
        grid=(blocks,),
        in_specs=[
            pl.BlockSpec((slots, 1), lambda j: (0, 0)),
            pl.BlockSpec((slots, width), lambda j: (0, j)),
            pl.BlockSpec((slots, width), lambda j: (0, blocks + j)),
        ],
        out_specs=pl.BlockSpec((width, HEAD_DIM), lambda j: (j, 0)),
        cost_estimate=pl.CostEstimate(
            flops=2 * slots * columns * HEAD_DIM,
            bytes_accessed=4 * columns * (slots + HEAD_DIM),
            transcendentals=0,
        ),
        name="block_update",
    )(tail_slots, arrived, arrived)


def unpack_kernel(land_ref, keys_ref, values_ref, *refs):
    keys_out, values_out, order = refs[-3:]

    @pl.when(pl.program_id(0) == 0)
    def _():
        rows = lax.broadcasted_iota(jnp.int32, order.shape, 0)
        order[...] = jnp.where(land_ref[...] == rows, 1.0, 0.0).astype(order.dtype)

    for source, out in ((keys_ref, keys_out), (values_ref, values_out)):
        out[...] = jnp.dot(
            order[...], source[...], preferred_element_type=jnp.float32
        ).astype(out.dtype)


def unpack_keys_values(arrived, land_row, tok_rows, start, mine, filled):
    slots, columns = arrived.shape[0], arrived.shape[1] // 2
    width = min(columns, 2 * HEAD_DIM)
    blocks, first = columns // width, start // width
    packed = jax.ShapeDtypeStruct((tok_rows, mine), arrived.dtype)
    column_spec = pl.BlockSpec((tok_rows, width), lambda j: (0, first + j))
    return pl.pallas_call(
        unpack_kernel,
        out_shape=(packed, packed),
        grid=(blocks,),
        in_specs=[
            pl.BlockSpec((1, slots), lambda j: (0, 0)),
            pl.BlockSpec((slots, width), lambda j: (0, j)),
            pl.BlockSpec((slots, width), lambda j: (0, blocks + j)),
        ]
        + [pl.BlockSpec(memory_space=pl.ANY) for _ in filled],
        out_specs=(column_spec, column_spec),
        scratch_shapes=[pltpu.VMEM((tok_rows, slots), jnp.bfloat16)],
        input_output_aliases={3 + number: number for number in range(len(filled))},
        cost_estimate=pl.CostEstimate(
            flops=4 * tok_rows * columns * slots,
            bytes_accessed=4 * columns * (slots + tok_rows),
            transcendentals=0,
        ),
        name="unpack_keys_values",
    )(land_row, arrived, arrived, *filled)


def sum_kernel(take_ref, *refs):
    count = take_ref.shape[1]
    pieces, outs = refs[:count], refs[count:]
    for number, out in enumerate(outs):
        total = jnp.zeros(out.shape, jnp.float32)
        for piece in range(count):
            total = total + jnp.where(take_ref[number, piece] != 0, pieces[piece][...], 0.0)
        out[...] = total


def sum_pieces(take, pieces):
    rows = pieces[0].shape[0]
    step = rows // 2
    spec = pl.BlockSpec((step, HEAD_DIM), lambda i, take_ref: (i, 0))
    count = take.shape[0]
    return pl.pallas_call(
        sum_kernel,
        out_shape=(jax.ShapeDtypeStruct((rows, HEAD_DIM), jnp.float32),) * count,
        grid_spec=pltpu.PrefetchScalarGridSpec(
            num_scalar_prefetch=1,
            grid=(rows // step,),
            in_specs=[spec] * len(pieces),
            out_specs=(spec,) * count,
        ),
        cost_estimate=pl.CostEstimate(
            flops=count * len(pieces) * rows * HEAD_DIM,
            bytes_accessed=4 * (len(pieces) + count) * rows * HEAD_DIM,
            transcendentals=0,
        ),
        name="sum_pieces",
    )(take.astype(jnp.int32), *pieces)


def run_of_blocks():
    seq_count, block = lax.axis_size("seq"), lax.axis_index("seq")
    near = math.gcd(seq_count, 4)
    return near, seq_count // near, block % near, block // near


def swap_places(value, k):
    seq_count = lax.axis_size("seq")
    return lax.ppermute(value, "seq", [(i, i ^ k) for i in range(seq_count)])


def carry_tables(last_segment):
    near, far, place, run = run_of_blocks()
    base = run * near
    source = base + (place ^ jnp.arange(near))
    before = last_segment[jnp.maximum(source - 1, 0)]
    of_source = last_segment[source]
    inside = (source[None, :] < source[:, None]) & (of_source[None, :] == before[:, None])
    whole = of_source == last_segment[base + near - 1]
    within = jnp.concatenate([inside, whole[None]])
    shifts = jnp.arange(1, far // 2 + 1)
    ends = last_segment[jnp.maximum(run - shifts, 0) * near + near - 1]
    across = (run >= shifts)[None, :] & (ends[None, :] == before[:, None])
    own = jnp.arange(near)[:, None] == jnp.arange(near)[None, :]
    return within, jnp.concatenate([own, across], axis=1)


def carry_within(update, within):
    near, _, place, _ = run_of_blocks()
    share = update.shape[0] // near
    pieces = []
    for k in range(near):
        mine = lax.dynamic_slice_in_dim(update, (place ^ k) * share, share, axis=0)
        pieces.append(mine if k == 0 else swap_places(mine, k))
    return sum_pieces(within, pieces)


def pass_totals(sums):
    seq_count = lax.axis_size("seq")
    near, far, _, _ = run_of_blocks()
    pieces = list(sums[:near])
    for shift in range(1, far // 2 + 1):
        step = shift * near
        pieces.append(
            lax.ppermute(sums[near], "seq", [(i, i + step) for i in range(seq_count - step)])
        )
    return pieces


def hand_back(pieces, across):
    near, _, place, _ = run_of_blocks()
    handed = sum_pieces(across, pieces)
    stacked = jnp.stack([handed[0]] + [swap_places(handed[k], k) for k in range(1, near)])
    return [
        lax.dynamic_index_in_dim(stacked, place ^ number, axis=0, keepdims=False)
        for number in range(near)
    ]


def local_kernel(
    land_ref, seg_col_ref, seg_row_ref, arrived_ref, keys_ref, values_ref, query_out, local_out,
    order, causal,
):
    tok_rows = order.shape[0]

    @pl.when(pl.program_id(0) == 0)
    def _():
        rows = lax.broadcasted_iota(jnp.int32, order.shape, 0)
        order[...] = jnp.where(land_ref[...] == rows, 1.0, 0.0).astype(order.dtype)
        later = lax.broadcasted_iota(jnp.int32, causal.shape, 0)
        earlier = lax.broadcasted_iota(jnp.int32, causal.shape, 1)
        open_pair = (earlier <= later) & (seg_col_ref[...] == seg_row_ref[...])
        causal[...] = jnp.where(open_pair, 1.0, 0.0)

    query = jnp.dot(order[...], arrived_ref[...], preferred_element_type=jnp.float32).astype(
        keys_ref.dtype
    )
    query_out[...] = query
    half = tok_rows // 2
    for part in range(query.shape[1] // HEAD_DIM):
        columns = slice(part * HEAD_DIM, (part + 1) * HEAD_DIM)
        for rows, reach in ((slice(0, half), half), (slice(half, tok_rows), tok_rows)):
            scores = lax.dot_general(
                query[rows, columns],
                keys_ref[:reach, columns],
                (((1,), (1,)), ((), ())),
                preferred_element_type=jnp.float32,
            )
            weights = jnp.where(causal[rows, :reach] != 0.0, scores, 0.0).astype(keys_ref.dtype)
            local_out[rows, columns] = jnp.dot(
                weights, values_ref[:reach, columns], preferred_element_type=jnp.float32
            )


def attend_locally(arrived, keys, values, land_row, seg_col, seg_row):
    slots, columns = arrived.shape
    tok_rows = keys.shape[0]
    width = min(columns, 2 * HEAD_DIM)
    column_spec = pl.BlockSpec((tok_rows, width), lambda j: (0, j))
    return pl.pallas_call(
        local_kernel,
        out_shape=(
            jax.ShapeDtypeStruct((tok_rows, columns), jnp.bfloat16),
            jax.ShapeDtypeStruct((tok_rows, columns), jnp.float32),
        ),
        grid=(columns // width,),
        in_specs=[
            pl.BlockSpec((1, slots), lambda j: (0, 0)),
            pl.BlockSpec((tok_rows, 1), lambda j: (0, 0)),
            pl.BlockSpec((1, tok_rows), lambda j: (0, 0)),
            pl.BlockSpec((slots, width), lambda j: (0, j)),
            column_spec,
            column_spec,
        ],
        out_specs=(column_spec, column_spec),
        scratch_shapes=[
            pltpu.VMEM((tok_rows, slots), jnp.bfloat16),
            pltpu.VMEM((tok_rows, tok_rows), jnp.float32),
        ],
        cost_estimate=pl.CostEstimate(
            flops=2 * tok_rows * columns * (slots + 2 * tok_rows),
            bytes_accessed=2 * columns * (slots + 5 * tok_rows),
            transcendentals=0,
        ),
        name="attend_locally",
    )(land_row, seg_col, seg_row, arrived, keys, values)


def finish_kernel(mask_ref, gain_ref, query_ref, local_ref, states_ref, out_ref):
    states = states_ref[...]
    high = states.astype(query_ref.dtype)
    low = (states - high.astype(jnp.float32)).astype(query_ref.dtype)
    for part in range(out_ref.shape[1] // HEAD_DIM):
        columns = slice(part * HEAD_DIM, (part + 1) * HEAD_DIM)
        query = query_ref[:, columns]
        carried_term = jnp.dot(
            query, high[columns], preferred_element_type=jnp.float32
        ) + jnp.dot(query, low[columns], preferred_element_type=jnp.float32)
        raw_out = local_ref[:, columns] + jnp.where(mask_ref[...] != 0, carried_term, 0.0)
        inv_rms = lax.rsqrt(jnp.mean(raw_out * raw_out, axis=1, keepdims=True) + norm_eps)
        out_ref[:, columns] = (raw_out * inv_rms * gain_ref[:, columns]).astype(out_ref.dtype)


def finish(query, local_term, states, carried_mask, gain):
    tok_rows, columns = query.shape
    width = min(columns, 4 * HEAD_DIM)
    column_spec = pl.BlockSpec((tok_rows, width), lambda j: (0, j))
    return pl.pallas_call(
        finish_kernel,
        out_shape=jax.ShapeDtypeStruct((tok_rows, columns), jnp.bfloat16),
        grid=(columns // width,),
        in_specs=[
            pl.BlockSpec((tok_rows, 1), lambda j: (0, 0)),
            pl.BlockSpec((1, width), lambda j: (0, j)),
            column_spec,
            column_spec,
            pl.BlockSpec((width, HEAD_DIM), lambda j: (j, 0)),
        ],
        out_specs=column_spec,
        cost_estimate=pl.CostEstimate(
            flops=4 * tok_rows * columns * HEAD_DIM,
            bytes_accessed=8 * columns * tok_rows,
            transcendentals=0,
        ),
        name="finish",
    )(carried_mask, gain, query, local_term, states)


def swap_heads(qkv, plane_start, planes, start, columns):
    head_count = lax.axis_size("head")
    rows = qkv.shape[1]
    mine = qkv.shape[2] // head_count
    part = lax.slice_in_dim(qkv, plane_start, plane_start + planes, axis=0)
    if head_count == 2:
        low = part[:, :, start : start + columns]
        high = part[:, :, mine + start : mine + start + columns]
        outgoing = jnp.where(lax.axis_index("head") == 0, high, low)
        return lax.ppermute(outgoing, "head", [(0, 1), (1, 0)])
    split = part.reshape(planes, rows, head_count, mine)[..., start : start + columns]
    incoming = lax.all_to_all(
        jnp.moveaxis(split, 2, 0), "head", split_axis=0, concat_axis=0, tiled=False
    )
    return jnp.moveaxis(incoming, 0, 1).reshape(planes, head_count * rows, columns)


def pack_chunk(qkv, incoming, send_rows, plane_start, planes, start, columns):
    head_count = lax.axis_size("head")
    place = lax.axis_index("head")
    rows = qkv.shape[1]
    mine = qkv.shape[2] // head_count
    slots = send_rows.reshape(-1, 1)
    width = math.gcd(math.gcd(columns, start), math.gcd(mine, 512))
    picks, sources = (slots,), ((incoming, 0, lambda at, width: 0),)
    if head_count == 2:
        picks = (slots - place * rows, slots - (1 - place) * rows)
        sources = (
            (qkv, plane_start, lambda at, width: at * (mine // width) + start // width),
        ) + sources
    return pack_rows(
        jnp.reshape(place, (1,)).astype(jnp.int32), picks, sources, planes, columns, width
    )


def to_owners(outgoing):
    return lax.all_to_all(outgoing, "seq", split_axis=0, concat_axis=0, tiled=True)


def on_device(qkv, send_rows, recv_pos, req_lengths, norm_gain):
    seq_count, head_count = lax.axis_size("seq"), lax.axis_size("head")
    block = lax.axis_index("seq")
    tok_rows = qkv.shape[1] * head_count
    columns = qkv.shape[2] // head_count

    req_ends = jnp.cumsum(req_lengths)
    req_starts = req_ends - req_lengths
    first_row = block * tok_rows
    positions = first_row + jnp.arange(tok_rows, dtype=jnp.int32)
    segment = jnp.sum((req_starts[None, :] <= positions[:, None]).astype(jnp.int32), axis=1) - 1
    last_rows = (jnp.arange(seq_count, dtype=jnp.int32) + 1) * tok_rows - 1
    last_segment = jnp.sum((req_starts[None, :] <= last_rows[:, None]).astype(jnp.int32), axis=1) - 1
    prev_segment = jnp.sum((req_starts < first_row).astype(jnp.int32)) - 1
    carried_mask = (segment == prev_segment).astype(jnp.int32)[:, None]
    land_row = recv_pos[0].reshape(1, -1)
    landing = first_row + land_row.reshape(-1, 1)
    landing_segment = jnp.sum((req_starts[None, :] <= landing).astype(jnp.int32), axis=1, keepdims=True) - 1
    in_tail = (land_row.reshape(-1, 1) >= 0) & (landing_segment == last_segment[block])
    tail_slots = in_tail.astype(jnp.int32)
    gain = norm_gain.reshape(1, -1)

    rows = send_rows[0]
    head_share = columns // HEAD_DIM
    first = max(1, 3 * head_share // 16) * 2 * HEAD_DIM
    second = columns - first
    outgoing = pack_chunk(qkv, swap_heads(qkv, KEYS, 2, 0, first), rows, KEYS, 2, 0, first)
    arrived = to_owners(outgoing)
    outgoing = pack_chunk(
        qkv, swap_heads(qkv, KEYS, 2, first, second), rows, KEYS, 2, first, second
    )
    arrived_next = to_owners(outgoing)
    within, across = carry_tables(last_segment)
    sums = carry_within(block_update(arrived, tail_slots), within)
    filled = unpack_keys_values(arrived, land_row, tok_rows, 0, columns, ())
    incoming = swap_heads(qkv, QUERY, 1, 0, columns)
    incoming, sums, filled, tables = lax.optimization_barrier(
        (incoming, sums, filled, (tail_slots, within, across, segment, carried_mask))
    )
    tail_slots, within, across, segment, carried_mask = tables
    outgoing = pack_chunk(qkv, incoming, rows, QUERY, 1, 0, columns)
    outgoing, pieces = lax.optimization_barrier((outgoing, pass_totals(sums)))
    query = to_owners(outgoing)
    sums = carry_within(block_update(arrived_next, tail_slots), within)
    states = hand_back(pieces, across)
    filled = unpack_keys_values(arrived_next, land_row, tok_rows, first, columns, filled)
    pieces, (keys, values) = lax.optimization_barrier((pass_totals(sums), filled))
    states += hand_back(pieces, across)
    query, local_term = attend_locally(
        query, keys, values, land_row, segment[:, None], segment[None, :]
    )
    return finish(query, local_term, jnp.concatenate(states, axis=0), carried_mask, gain)


def solution(mesh):
    return jax.shard_map(
        on_device,
        mesh=mesh,
        in_specs=(
            P(None, ("seq", "head"), None),
            P("seq", None, None),
            P("seq", None, None),
            P(),
            P("head"),
        ),
        out_specs=P("seq", "head"),
        check_vma=False,
    )
```

```python
import math

import jax
import jax.numpy as jnp
from jax import lax
from jax.experimental import pallas as pl
from jax.experimental.pallas import tpu as pltpu
from jax.sharding import PartitionSpec as P

HEAD_DIM = 128

norm_eps = 1e-06

QUERY, KEYS, VALUES = 0, 1, 2


def pack_kernel(place_ref, *refs):
    count = (len(refs) - 1) // 3
    picks, sources = refs[:count], refs[count : 2 * count]
    out_ref, chosen = refs[2 * count], refs[2 * count + 1 :]

    @pl.when((pl.program_id(0) == 0) & (pl.program_id(1) == 0))
    def _():
        for pick, onehot in zip(picks, chosen):
            rows = lax.broadcasted_iota(jnp.int32, onehot.shape, 1)
            onehot[...] = jnp.where(pick[...] == rows, 1.0, 0.0).astype(onehot.dtype)

    total = None
    for source, onehot in zip(sources, chosen):
        part = jnp.dot(onehot[...], source[0], preferred_element_type=jnp.float32)
        total = part if total is None else total + part
    out_ref[...] = total.astype(out_ref.dtype)


def pack_rows(place, picks, sources, planes, columns, width):
    slots = picks[0].shape[0]
    blocks = columns // width
    lens = [array.shape[1] for array, _, _ in sources]

    def source_spec(array, plane_start, first):
        return pl.BlockSpec(
            (1, array.shape[1], width),
            lambda p, j, place_ref: (plane_start + p, 0, first(place_ref[0], width) + j),
        )

    return pl.pallas_call(
        pack_kernel,
        out_shape=jax.ShapeDtypeStruct((slots, planes * columns), jnp.bfloat16),
        grid_spec=pltpu.PrefetchScalarGridSpec(
            num_scalar_prefetch=1,
            grid=(planes, blocks),
            in_specs=[pl.BlockSpec((slots, 1), lambda p, j, place_ref: (0, 0)) for _ in picks]
            + [source_spec(*source) for source in sources],
            out_specs=pl.BlockSpec((slots, width), lambda p, j, place_ref: (0, p * blocks + j)),
            scratch_shapes=[pltpu.VMEM((slots, length), jnp.bfloat16) for length in lens],
        ),
        cost_estimate=pl.CostEstimate(
            flops=2 * slots * sum(lens) * planes * columns,
            bytes_accessed=2 * planes * columns * (slots + sum(lens)),
            transcendentals=0,
        ),
        name="pack_rows",
    )(place, *picks, *[array for array, _, _ in sources])


def update_kernel(tail_ref, keys_ref, values_ref, update_ref):
    tail = tail_ref[...] != 0
    for part in range(keys_ref.shape[1] // HEAD_DIM):
        columns = slice(part * HEAD_DIM, (part + 1) * HEAD_DIM)
        keys = keys_ref[:, columns]
        update_ref[columns, :] = lax.dot_general(
            jnp.where(tail, keys, jnp.zeros_like(keys)),
            values_ref[:, columns],
            (((0,), (0,)), ((), ())),
            preferred_element_type=jnp.float32,
        )


def block_update(arrived, tail_slots):
    slots, columns = arrived.shape[0], arrived.shape[1] // 2
    width = math.gcd(columns, 4 * HEAD_DIM)
    blocks = columns // width
    return pl.pallas_call(
        update_kernel,
        out_shape=jax.ShapeDtypeStruct((columns, HEAD_DIM), jnp.float32),
        grid=(blocks,),
        in_specs=[
            pl.BlockSpec((slots, 1), lambda j: (0, 0)),
            pl.BlockSpec((slots, width), lambda j: (0, j)),
            pl.BlockSpec((slots, width), lambda j: (0, blocks + j)),
        ],
        out_specs=pl.BlockSpec((width, HEAD_DIM), lambda j: (j, 0)),
        cost_estimate=pl.CostEstimate(
            flops=2 * slots * columns * HEAD_DIM,
            bytes_accessed=4 * columns * (slots + HEAD_DIM),
            transcendentals=0,
        ),
        name="block_update",
    )(tail_slots, arrived, arrived)


def unpack_kernel(land_ref, keys_ref, values_ref, *refs):
    keys_out, values_out, order = refs[-3:]

    @pl.when(pl.program_id(0) == 0)
    def _():
        rows = lax.broadcasted_iota(jnp.int32, order.shape, 0)
        order[...] = jnp.where(land_ref[...] == rows, 1.0, 0.0).astype(order.dtype)

    for source, out in ((keys_ref, keys_out), (values_ref, values_out)):
        out[...] = jnp.dot(
            order[...], source[...], preferred_element_type=jnp.float32
        ).astype(out.dtype)


def unpack_keys_values(arrived, land_row, tok_rows, start, mine, filled):
    slots, columns = arrived.shape[0], arrived.shape[1] // 2
    width = math.gcd(math.gcd(columns, start), 4 * HEAD_DIM)
    blocks, first = columns // width, start // width
    packed = jax.ShapeDtypeStruct((tok_rows, mine), arrived.dtype)
    column_spec = pl.BlockSpec((tok_rows, width), lambda j: (0, first + j))
    return pl.pallas_call(
        unpack_kernel,
        out_shape=(packed, packed),
        grid=(blocks,),
        in_specs=[
            pl.BlockSpec((1, slots), lambda j: (0, 0)),
            pl.BlockSpec((slots, width), lambda j: (0, j)),
            pl.BlockSpec((slots, width), lambda j: (0, blocks + j)),
        ]
        + [pl.BlockSpec(memory_space=pl.ANY) for _ in filled],
        out_specs=(column_spec, column_spec),
        scratch_shapes=[pltpu.VMEM((tok_rows, slots), jnp.bfloat16)],
        input_output_aliases={3 + number: number for number in range(len(filled))},
        cost_estimate=pl.CostEstimate(
            flops=4 * tok_rows * columns * slots,
            bytes_accessed=4 * columns * (slots + tok_rows),
            transcendentals=0,
        ),
        name="unpack_keys_values",
    )(land_row, arrived, arrived, *filled)


def sum_kernel(take_ref, *refs):
    count = take_ref.shape[1]
    pieces, outs = refs[:count], refs[count:]
    for number, out in enumerate(outs):
        total = jnp.zeros(out.shape, jnp.float32)
        for piece in range(count):
            total = total + jnp.where(take_ref[number, piece] != 0, pieces[piece][...], 0.0)
        out[...] = total


def sum_pieces(take, pieces):
    rows = pieces[0].shape[0]
    step = rows // 2
    spec = pl.BlockSpec((step, HEAD_DIM), lambda i, take_ref: (i, 0))
    count = take.shape[0]
    return pl.pallas_call(
        sum_kernel,
        out_shape=(jax.ShapeDtypeStruct((rows, HEAD_DIM), jnp.float32),) * count,
        grid_spec=pltpu.PrefetchScalarGridSpec(
            num_scalar_prefetch=1,
            grid=(rows // step,),
            in_specs=[spec] * len(pieces),
            out_specs=(spec,) * count,
        ),
        cost_estimate=pl.CostEstimate(
            flops=count * len(pieces) * rows * HEAD_DIM,
            bytes_accessed=4 * (len(pieces) + count) * rows * HEAD_DIM,
            transcendentals=0,
        ),
        name="sum_pieces",
    )(take.astype(jnp.int32), *pieces)


def run_of_blocks():
    seq_count, block = lax.axis_size("seq"), lax.axis_index("seq")
    near = math.gcd(seq_count, 4)
    return near, seq_count // near, block % near, block // near


def swap_places(value, k):
    seq_count = lax.axis_size("seq")
    return lax.ppermute(value, "seq", [(i, i ^ k) for i in range(seq_count)])


def carry_tables(last_segment):
    near, far, place, run = run_of_blocks()
    base = run * near
    source = base + (place ^ jnp.arange(near))
    before = last_segment[jnp.maximum(source - 1, 0)]
    of_source = last_segment[source]
    inside = (source[None, :] < source[:, None]) & (of_source[None, :] == before[:, None])
    whole = of_source == last_segment[base + near - 1]
    within = jnp.concatenate([inside, whole[None]])
    shifts = jnp.arange(1, far // 2 + 1)
    ends = last_segment[jnp.maximum(run - shifts, 0) * near + near - 1]
    across = (run >= shifts)[None, :] & (ends[None, :] == before[:, None])
    own = jnp.arange(near)[:, None] == jnp.arange(near)[None, :]
    return within, jnp.concatenate([own, across], axis=1)


def carry_within(update, within):
    near, _, place, _ = run_of_blocks()
    share = update.shape[0] // near
    pieces = []
    for k in range(near):
        mine = lax.dynamic_slice_in_dim(update, (place ^ k) * share, share, axis=0)
        pieces.append(mine if k == 0 else swap_places(mine, k))
    return sum_pieces(within, pieces)


def pass_totals(sums):
    seq_count = lax.axis_size("seq")
    near, far, _, _ = run_of_blocks()
    pieces = list(sums[:near])
    for shift in range(1, far // 2 + 1):
        step = shift * near
        pieces.append(
            lax.ppermute(sums[near], "seq", [(i, i + step) for i in range(seq_count - step)])
        )
    return pieces


def hand_back(pieces, across):
    near, _, place, _ = run_of_blocks()
    handed = sum_pieces(across, pieces)
    stacked = jnp.stack([handed[0]] + [swap_places(handed[k], k) for k in range(1, near)])
    return [
        lax.dynamic_index_in_dim(stacked, place ^ number, axis=0, keepdims=False)
        for number in range(near)
    ]


def local_kernel(
    land_ref, seg_col_ref, seg_row_ref, mask_ref, arrived_ref, keys_ref, values_ref, query_out,
    local_out, order, causal, carried,
):
    tok_rows = order.shape[0]

    @pl.when(pl.program_id(0) == 0)
    def _():
        rows = lax.broadcasted_iota(jnp.int32, order.shape, 0)
        order[...] = jnp.where(land_ref[...] == rows, 1.0, 0.0).astype(order.dtype)
        later = lax.broadcasted_iota(jnp.int32, causal.shape, 0)
        earlier = lax.broadcasted_iota(jnp.int32, causal.shape, 1)
        open_pair = (earlier <= later) & (seg_col_ref[...] == seg_row_ref[...])
        causal[...] = jnp.where(open_pair, 1.0, 0.0).astype(causal.dtype)
        carried[...] = jnp.broadcast_to(
            jnp.where(mask_ref[...] != 0, 1.0, 0.0).astype(carried.dtype), carried.shape
        )

    query = jnp.dot(order[...], arrived_ref[...], preferred_element_type=jnp.float32).astype(
        keys_ref.dtype
    )
    half = tok_rows // 2
    for part in range(query.shape[1] // HEAD_DIM):
        columns = slice(part * HEAD_DIM, (part + 1) * HEAD_DIM)
        query_out[:, columns] = query[:, columns] * carried[...]
        for rows, reach in ((slice(0, half), half), (slice(half, tok_rows), tok_rows)):
            scores = lax.dot_general(
                query[rows, columns],
                keys_ref[:reach, columns],
                (((1,), (1,)), ((), ())),
                preferred_element_type=jnp.float32,
            )
            weights = scores.astype(keys_ref.dtype) * causal[rows, :reach]
            local_out[rows, columns] = jnp.dot(
                weights, values_ref[:reach, columns], preferred_element_type=jnp.float32
            )


def attend_locally(arrived, keys, values, land_row, seg_col, seg_row, carried_mask):
    slots, columns = arrived.shape
    tok_rows = keys.shape[0]
    width = math.gcd(columns, 4 * HEAD_DIM)
    column_spec = pl.BlockSpec((tok_rows, width), lambda j: (0, j))
    return pl.pallas_call(
        local_kernel,
        out_shape=(
            jax.ShapeDtypeStruct((tok_rows, columns), jnp.bfloat16),
            jax.ShapeDtypeStruct((tok_rows, columns), jnp.float32),
        ),
        grid=(columns // width,),
        in_specs=[
            pl.BlockSpec((1, slots), lambda j: (0, 0)),
            pl.BlockSpec((tok_rows, 1), lambda j: (0, 0)),
            pl.BlockSpec((1, tok_rows), lambda j: (0, 0)),
            pl.BlockSpec((tok_rows, 1), lambda j: (0, 0)),
            pl.BlockSpec((slots, width), lambda j: (0, j)),
            column_spec,
            column_spec,
        ],
        out_specs=(column_spec, column_spec),
        scratch_shapes=[
            pltpu.VMEM((tok_rows, slots), jnp.bfloat16),
            pltpu.VMEM((tok_rows, tok_rows), jnp.bfloat16),
            pltpu.VMEM((tok_rows, HEAD_DIM), jnp.bfloat16),
        ],
        cost_estimate=pl.CostEstimate(
            flops=2 * tok_rows * columns * (slots + 2 * tok_rows),
            bytes_accessed=2 * columns * (slots + 5 * tok_rows),
            transcendentals=0,
        ),
        name="attend_locally",
    )(land_row, seg_col, seg_row, carried_mask, arrived, keys, values)


def two_terms(value):
    high = value.astype(jnp.bfloat16)
    return high, (value - high.astype(jnp.float32)).astype(jnp.bfloat16)


def finish_kernel(gain_ref, query_ref, local_ref, states_ref, out_ref):
    ones = jnp.full((HEAD_DIM, HEAD_DIM), 1.0, jnp.bfloat16)

    def product(left, right):
        return jnp.dot(left, right, preferred_element_type=jnp.float32)

    for part in range(out_ref.shape[1] // HEAD_DIM):
        columns = slice(part * HEAD_DIM, (part + 1) * HEAD_DIM)
        high, low = two_terms(states_ref[columns, :])
        query = query_ref[:, columns]
        raw_out = local_ref[:, columns] + (product(query, high) + product(query, low))
        high, low = two_terms(raw_out * raw_out)
        mean = (product(high, ones) + product(low, ones)) * (1.0 / HEAD_DIM)
        out_ref[:, columns] = (raw_out * lax.rsqrt(mean + norm_eps) * gain_ref[:, columns]).astype(
            out_ref.dtype
        )


def finish(query, local_term, states, gain):
    tok_rows, columns = query.shape
    width = math.gcd(columns, 4 * HEAD_DIM)
    column_spec = pl.BlockSpec((tok_rows, width), lambda j: (0, j))
    return pl.pallas_call(
        finish_kernel,
        out_shape=jax.ShapeDtypeStruct((tok_rows, columns), jnp.bfloat16),
        grid=(columns // width,),
        in_specs=[
            pl.BlockSpec((1, width), lambda j: (0, j)),
            column_spec,
            column_spec,
            pl.BlockSpec((width, HEAD_DIM), lambda j: (j, 0)),
        ],
        out_specs=column_spec,
        cost_estimate=pl.CostEstimate(
            flops=8 * tok_rows * columns * HEAD_DIM,
            bytes_accessed=8 * columns * tok_rows,
            transcendentals=0,
        ),
        name="finish",
    )(gain, query, local_term, states)


def swap_heads(qkv, plane_start, planes, start, columns):
    head_count = lax.axis_size("head")
    rows = qkv.shape[1]
    mine = qkv.shape[2] // head_count
    part = lax.slice_in_dim(qkv, plane_start, plane_start + planes, axis=0)
    if head_count == 2:
        low = part[:, :, start : start + columns]
        high = part[:, :, mine + start : mine + start + columns]
        outgoing = jnp.where(lax.axis_index("head") == 0, high, low)
        return lax.ppermute(outgoing, "head", [(0, 1), (1, 0)])
    split = part.reshape(planes, rows, head_count, mine)[..., start : start + columns]
    incoming = lax.all_to_all(
        jnp.moveaxis(split, 2, 0), "head", split_axis=0, concat_axis=0, tiled=False
    )
    return jnp.moveaxis(incoming, 0, 1).reshape(planes, head_count * rows, columns)


def pack_chunk(qkv, incoming, send_rows, plane_start, planes, start, columns):
    head_count = lax.axis_size("head")
    place = lax.axis_index("head")
    rows = qkv.shape[1]
    mine = qkv.shape[2] // head_count
    slots = send_rows.reshape(-1, 1)
    width = math.gcd(math.gcd(columns, start), math.gcd(mine, 512))
    picks, sources = (slots,), ((incoming, 0, lambda at, width: 0),)
    if head_count == 2:
        picks = (slots - place * rows, slots - (1 - place) * rows)
        sources = (
            (qkv, plane_start, lambda at, width: at * (mine // width) + start // width),
        ) + sources
    return pack_rows(
        jnp.reshape(place, (1,)).astype(jnp.int32), picks, sources, planes, columns, width
    )


def to_owners(outgoing):
    return lax.all_to_all(outgoing, "seq", split_axis=0, concat_axis=0, tiled=True)


def on_device(qkv, send_rows, recv_pos, req_lengths, norm_gain):
    seq_count, head_count = lax.axis_size("seq"), lax.axis_size("head")
    block = lax.axis_index("seq")
    tok_rows = qkv.shape[1] * head_count
    columns = qkv.shape[2] // head_count

    req_ends = jnp.cumsum(req_lengths)
    req_starts = req_ends - req_lengths
    first_row = block * tok_rows
    positions = first_row + jnp.arange(tok_rows, dtype=jnp.int32)
    segment = jnp.sum((req_starts[None, :] <= positions[:, None]).astype(jnp.int32), axis=1) - 1
    last_rows = (jnp.arange(seq_count, dtype=jnp.int32) + 1) * tok_rows - 1
    last_segment = jnp.sum((req_starts[None, :] <= last_rows[:, None]).astype(jnp.int32), axis=1) - 1
    prev_segment = jnp.sum((req_starts < first_row).astype(jnp.int32)) - 1
    carried_mask = (segment == prev_segment).astype(jnp.int32)[:, None]
    land_row = recv_pos[0].reshape(1, -1)
    landing = first_row + land_row.reshape(-1, 1)
    landing_segment = jnp.sum((req_starts[None, :] <= landing).astype(jnp.int32), axis=1, keepdims=True) - 1
    in_tail = (land_row.reshape(-1, 1) >= 0) & (landing_segment == last_segment[block])
    tail_slots = in_tail.astype(jnp.int32)
    gain = norm_gain.reshape(1, -1)

    rows = send_rows[0]
    head_share = columns // HEAD_DIM
    first = max(2, head_share // 4) * HEAD_DIM
    second = columns - first
    outgoing = pack_chunk(qkv, swap_heads(qkv, KEYS, 2, 0, first), rows, KEYS, 2, 0, first)
    arrived = to_owners(outgoing)
    outgoing = pack_chunk(
        qkv, swap_heads(qkv, KEYS, 2, first, second), rows, KEYS, 2, first, second
    )
    arrived_next = to_owners(outgoing)
    within, across = carry_tables(last_segment)
    sums = carry_within(block_update(arrived, tail_slots), within)
    filled = unpack_keys_values(arrived, land_row, tok_rows, 0, columns, ())
    incoming = swap_heads(qkv, QUERY, 1, 0, columns)
    incoming, sums, filled, tables = lax.optimization_barrier(
        (incoming, sums, filled, (tail_slots, within, across, segment, carried_mask))
    )
    tail_slots, within, across, segment, carried_mask = tables
    outgoing = pack_chunk(qkv, incoming, rows, QUERY, 1, 0, columns)
    outgoing, pieces = lax.optimization_barrier((outgoing, pass_totals(sums)))
    query = to_owners(outgoing)
    sums = carry_within(block_update(arrived_next, tail_slots), within)
    pieces, sums = lax.optimization_barrier((pieces, sums))
    states = hand_back(pieces, across)
    filled = unpack_keys_values(arrived_next, land_row, tok_rows, first, columns, filled)
    local = attend_locally(
        query, *filled, land_row, segment[:, None], segment[None, :], carried_mask
    )
    pieces, (query, local_term) = lax.optimization_barrier((pass_totals(sums), local))
    states += hand_back(pieces, across)
    return finish(query, local_term, jnp.concatenate(states, axis=0), gain)


def solution(mesh):
    return jax.shard_map(
        on_device,
        mesh=mesh,
        in_specs=(
            P(None, ("seq", "head"), None),
            P("seq", None, None),
            P("seq", None, None),
            P(),
            P("head"),
        ),
        out_specs=P("seq", "head"),
        check_vma=False,
    )
```

```python
import math

import jax
import jax.numpy as jnp
from jax import lax
from jax.experimental import pallas as pl
from jax.experimental.pallas import tpu as pltpu
from jax.sharding import PartitionSpec as P

HEAD_DIM = 128

norm_eps = 1e-06

QUERY, KEYS, VALUES = 0, 1, 2

PACK_WEIGHT = 20
ATTEND_WEIGHT = 7


def pack_kernel(place_ref, *refs):
    count = (len(refs) - 1) // 3
    picks, sources = refs[:count], refs[count : 2 * count]
    out_ref, chosen = refs[2 * count], refs[2 * count + 1 :]

    @pl.when((pl.program_id(0) == 0) & (pl.program_id(1) == 0))
    def _():
        for pick, onehot in zip(picks, chosen):
            rows = lax.broadcasted_iota(jnp.int32, onehot.shape, 1)
            onehot[...] = jnp.where(pick[...] == rows, 1.0, 0.0).astype(onehot.dtype)

    total = None
    for source, onehot in zip(sources, chosen):
        part = jnp.dot(onehot[...], source[0], preferred_element_type=jnp.float32)
        total = part if total is None else total + part
    out_ref[...] = total.astype(out_ref.dtype)


def pack_rows(place, picks, sources, planes, columns, width):
    slots = picks[0].shape[0]
    blocks = columns // width
    lens = [array.shape[1] for array, _, _ in sources]

    def source_spec(array, plane_start, first):
        return pl.BlockSpec(
            (1, array.shape[1], width),
            lambda p, j, place_ref: (plane_start + p, 0, first(place_ref[0], width) + j),
        )

    return pl.pallas_call(
        pack_kernel,
        out_shape=jax.ShapeDtypeStruct((slots, planes * columns), jnp.bfloat16),
        grid_spec=pltpu.PrefetchScalarGridSpec(
            num_scalar_prefetch=1,
            grid=(planes, blocks),
            in_specs=[pl.BlockSpec((slots, 1), lambda p, j, place_ref: (0, 0)) for _ in picks]
            + [source_spec(*source) for source in sources],
            out_specs=pl.BlockSpec((slots, width), lambda p, j, place_ref: (0, p * blocks + j)),
            scratch_shapes=[pltpu.VMEM((slots, length), jnp.bfloat16) for length in lens],
        ),
        cost_estimate=pl.CostEstimate(
            flops=PACK_WEIGHT * 2 * slots * sum(lens) * planes * columns,
            bytes_accessed=2 * planes * columns * (slots + sum(lens)),
            transcendentals=0,
        ),
        name="pack_rows",
    )(place, *picks, *[array for array, _, _ in sources])


def update_kernel(tail_ref, keys_ref, values_ref, update_ref):
    tail = tail_ref[...] != 0
    for part in range(keys_ref.shape[1] // HEAD_DIM):
        columns = slice(part * HEAD_DIM, (part + 1) * HEAD_DIM)
        keys = keys_ref[:, columns]
        update_ref[columns, :] = lax.dot_general(
            jnp.where(tail, keys, jnp.zeros_like(keys)),
            values_ref[:, columns],
            (((0,), (0,)), ((), ())),
            preferred_element_type=jnp.float32,
        )


def block_update(arrived, tail_slots):
    slots, columns = arrived.shape[0], arrived.shape[1] // 2
    width = math.gcd(columns, 4 * HEAD_DIM)
    blocks = columns // width
    return pl.pallas_call(
        update_kernel,
        out_shape=jax.ShapeDtypeStruct((columns, HEAD_DIM), jnp.float32),
        grid=(blocks,),
        in_specs=[
            pl.BlockSpec((slots, 1), lambda j: (0, 0)),
            pl.BlockSpec((slots, width), lambda j: (0, j)),
            pl.BlockSpec((slots, width), lambda j: (0, blocks + j)),
        ],
        out_specs=pl.BlockSpec((width, HEAD_DIM), lambda j: (j, 0)),
        cost_estimate=pl.CostEstimate(
            flops=2 * slots * columns * HEAD_DIM,
            bytes_accessed=4 * columns * (slots + HEAD_DIM),
            transcendentals=0,
        ),
        name="block_update",
    )(tail_slots, arrived, arrived)


def unpack_kernel(land_ref, keys_ref, values_ref, *refs):
    keys_out, values_out, order = refs[-3:]

    @pl.when(pl.program_id(0) == 0)
    def _():
        rows = lax.broadcasted_iota(jnp.int32, order.shape, 0)
        order[...] = jnp.where(land_ref[...] == rows, 1.0, 0.0).astype(order.dtype)

    for source, out in ((keys_ref, keys_out), (values_ref, values_out)):
        out[...] = jnp.dot(
            order[...], source[...], preferred_element_type=jnp.float32
        ).astype(out.dtype)


def unpack_keys_values(arrived, land_row, tok_rows, start, mine, filled):
    slots, columns = arrived.shape[0], arrived.shape[1] // 2
    width = math.gcd(math.gcd(columns, start), 4 * HEAD_DIM)
    blocks, first = columns // width, start // width
    packed = jax.ShapeDtypeStruct((tok_rows, mine), arrived.dtype)
    column_spec = pl.BlockSpec((tok_rows, width), lambda j: (0, first + j))
    return pl.pallas_call(
        unpack_kernel,
        out_shape=(packed, packed),
        grid=(blocks,),
        in_specs=[
            pl.BlockSpec((1, slots), lambda j: (0, 0)),
            pl.BlockSpec((slots, width), lambda j: (0, j)),
            pl.BlockSpec((slots, width), lambda j: (0, blocks + j)),
        ]
        + [pl.BlockSpec(memory_space=pl.ANY) for _ in filled],
        out_specs=(column_spec, column_spec),
        scratch_shapes=[pltpu.VMEM((tok_rows, slots), jnp.bfloat16)],
        input_output_aliases={3 + number: number for number in range(len(filled))},
        cost_estimate=pl.CostEstimate(
            flops=4 * tok_rows * columns * slots,
            bytes_accessed=4 * columns * (slots + tok_rows),
            transcendentals=0,
        ),
        name="unpack_keys_values",
    )(land_row, arrived, arrived, *filled)


def sum_kernel(take_ref, *refs):
    count = take_ref.shape[1]
    pieces, outs = refs[:count], refs[count:]
    for number, out in enumerate(outs):
        total = jnp.zeros(out.shape, jnp.float32)
        for piece in range(count):
            total = total + jnp.where(take_ref[number, piece] != 0, pieces[piece][...], 0.0)
        out[...] = total


def sum_pieces(take, pieces):
    rows = pieces[0].shape[0]
    step = rows // 2
    spec = pl.BlockSpec((step, HEAD_DIM), lambda i, take_ref: (i, 0))
    count = take.shape[0]
    return pl.pallas_call(
        sum_kernel,
        out_shape=(jax.ShapeDtypeStruct((rows, HEAD_DIM), jnp.float32),) * count,
        grid_spec=pltpu.PrefetchScalarGridSpec(
            num_scalar_prefetch=1,
            grid=(rows // step,),
            in_specs=[spec] * len(pieces),
            out_specs=(spec,) * count,
        ),
        cost_estimate=pl.CostEstimate(
            flops=count * len(pieces) * rows * HEAD_DIM,
            bytes_accessed=4 * (len(pieces) + count) * rows * HEAD_DIM,
            transcendentals=0,
        ),
        name="sum_pieces",
    )(take.astype(jnp.int32), *pieces)


def run_of_blocks():
    seq_count, block = lax.axis_size("seq"), lax.axis_index("seq")
    near = math.gcd(seq_count, 4)
    return near, seq_count // near, block % near, block // near


def swap_places(value, k):
    seq_count = lax.axis_size("seq")
    return lax.ppermute(value, "seq", [(i, i ^ k) for i in range(seq_count)])


def carry_tables(last_segment):
    near, far, place, run = run_of_blocks()
    base = run * near
    source = base + (place ^ jnp.arange(near))
    before = last_segment[jnp.maximum(source - 1, 0)]
    of_source = last_segment[source]
    inside = (source[None, :] < source[:, None]) & (of_source[None, :] == before[:, None])
    whole = of_source == last_segment[base + near - 1]
    within = jnp.concatenate([inside, whole[None]])
    shifts = jnp.arange(1, far // 2 + 1)
    ends = last_segment[jnp.maximum(run - shifts, 0) * near + near - 1]
    across = (run >= shifts)[None, :] & (ends[None, :] == before[:, None])
    own = jnp.arange(near)[:, None] == jnp.arange(near)[None, :]
    return within, jnp.concatenate([own, across], axis=1)


def carry_within(update, within):
    near, _, place, _ = run_of_blocks()
    share = update.shape[0] // near
    pieces = []
    for k in range(near):
        mine = lax.dynamic_slice_in_dim(update, (place ^ k) * share, share, axis=0)
        pieces.append(mine if k == 0 else swap_places(mine, k))
    return sum_pieces(within, pieces)


def pass_totals(sums):
    seq_count = lax.axis_size("seq")
    near, far, _, _ = run_of_blocks()
    pieces = list(sums[:near])
    for shift in range(1, far // 2 + 1):
        step = shift * near
        pieces.append(
            lax.ppermute(sums[near], "seq", [(i, i + step) for i in range(seq_count - step)])
        )
    return pieces


def hand_back(pieces, across):
    near, _, place, _ = run_of_blocks()
    handed = sum_pieces(across, pieces)
    stacked = jnp.stack([handed[0]] + [swap_places(handed[k], k) for k in range(1, near)])
    return [
        lax.dynamic_index_in_dim(stacked, place ^ number, axis=0, keepdims=False)
        for number in range(near)
    ]


def two_terms(value):
    high = value.astype(jnp.bfloat16)
    return high, (value - high.astype(jnp.float32)).astype(jnp.bfloat16)


def attend_kernel(
    land_ref, seg_col_ref, seg_row_ref, mask_ref, gain_ref, arrived_ref, keys_ref, values_ref,
    states_ref, *refs,
):
    out_ref, order, causal, carried = refs[-4:]
    tok_rows = order.shape[0]

    @pl.when(pl.program_id(0) == 0)
    def _():
        rows = lax.broadcasted_iota(jnp.int32, order.shape, 0)
        order[...] = jnp.where(land_ref[...] == rows, 1.0, 0.0).astype(order.dtype)
        later = lax.broadcasted_iota(jnp.int32, causal.shape, 0)
        earlier = lax.broadcasted_iota(jnp.int32, causal.shape, 1)
        open_pair = (earlier <= later) & (seg_col_ref[...] == seg_row_ref[...])
        causal[...] = jnp.where(open_pair, 1.0, 0.0).astype(causal.dtype)
        carried[...] = jnp.broadcast_to(
            jnp.where(mask_ref[...] != 0, 1.0, 0.0).astype(carried.dtype), carried.shape
        )

    def product(left, right):
        return jnp.dot(left, right, preferred_element_type=jnp.float32)

    ones = jnp.full((HEAD_DIM, HEAD_DIM), 1.0, jnp.bfloat16)
    query = product(order[...], arrived_ref[...]).astype(keys_ref.dtype)
    half = tok_rows // 2
    for part in range(query.shape[1] // HEAD_DIM):
        columns = slice(part * HEAD_DIM, (part + 1) * HEAD_DIM)
        state_high, state_low = two_terms(states_ref[columns, :])
        for rows, reach in ((slice(0, half), half), (slice(half, tok_rows), tok_rows)):
            queries = query[rows, columns]
            scores = lax.dot_general(
                queries,
                keys_ref[:reach, columns],
                (((1,), (1,)), ((), ())),
                preferred_element_type=jnp.float32,
            )
            weights = scores.astype(keys_ref.dtype) * causal[rows, :reach]
            carrying = queries * carried[rows, :]
            raw_out = product(weights, values_ref[:reach, columns]) + (
                product(carrying, state_high) + product(carrying, state_low)
            )
            square_high, square_low = two_terms(raw_out * raw_out)
            mean = (product(square_high, ones) + product(square_low, ones)) * (1.0 / HEAD_DIM)
            out_ref[rows, columns] = (
                raw_out * lax.rsqrt(mean + norm_eps) * gain_ref[:, columns]
            ).astype(out_ref.dtype)


def attend(arrived, keys, values, states, tables, gain, start, filled):
    slots, columns = arrived.shape
    tok_rows, mine = keys.shape
    width = math.gcd(math.gcd(columns, start), 4 * HEAD_DIM)
    first = start // width
    column_spec = pl.BlockSpec((tok_rows, width), lambda j: (0, first + j))
    return pl.pallas_call(
        attend_kernel,
        out_shape=jax.ShapeDtypeStruct((tok_rows, mine), jnp.bfloat16),
        grid=(columns // width,),
        in_specs=[
            pl.BlockSpec((1, slots), lambda j: (0, 0)),
            pl.BlockSpec((tok_rows, 1), lambda j: (0, 0)),
            pl.BlockSpec((1, tok_rows), lambda j: (0, 0)),
            pl.BlockSpec((tok_rows, 1), lambda j: (0, 0)),
            pl.BlockSpec((1, width), lambda j: (0, first + j)),
            pl.BlockSpec((slots, width), lambda j: (0, j)),
            column_spec,
            column_spec,
            pl.BlockSpec((width, HEAD_DIM), lambda j: (first + j, 0)),
        ]
        + [pl.BlockSpec(memory_space=pl.ANY) for _ in filled],
        out_specs=column_spec,
        scratch_shapes=[
            pltpu.VMEM((tok_rows, slots), jnp.bfloat16),
            pltpu.VMEM((tok_rows, tok_rows), jnp.bfloat16),
            pltpu.VMEM((tok_rows, HEAD_DIM), jnp.bfloat16),
        ],
        input_output_aliases={9: 0} if filled else {},
        cost_estimate=pl.CostEstimate(
            flops=ATTEND_WEIGHT * 2 * tok_rows * columns * (slots + 2 * tok_rows + 4 * HEAD_DIM),
            bytes_accessed=2 * columns * (slots + 4 * tok_rows),
            transcendentals=0,
        ),
        name="attend",
    )(*tables, gain, arrived, keys, values, states, *filled)


def swap_heads(qkv, plane_start, planes, start, columns):
    head_count = lax.axis_size("head")
    rows = qkv.shape[1]
    mine = qkv.shape[2] // head_count
    part = lax.slice_in_dim(qkv, plane_start, plane_start + planes, axis=0)
    if head_count == 2:
        low = part[:, :, start : start + columns]
        high = part[:, :, mine + start : mine + start + columns]
        outgoing = jnp.where(lax.axis_index("head") == 0, high, low)
        return lax.ppermute(outgoing, "head", [(0, 1), (1, 0)])
    split = part.reshape(planes, rows, head_count, mine)[..., start : start + columns]
    incoming = lax.all_to_all(
        jnp.moveaxis(split, 2, 0), "head", split_axis=0, concat_axis=0, tiled=False
    )
    return jnp.moveaxis(incoming, 0, 1).reshape(planes, head_count * rows, columns)


def pack_chunk(qkv, incoming, send_rows, plane_start, planes, start, columns, offset=0):
    head_count = lax.axis_size("head")
    place = lax.axis_index("head")
    rows = qkv.shape[1]
    mine = qkv.shape[2] // head_count
    slots = send_rows.reshape(-1, 1)
    width = math.gcd(math.gcd(columns, start), math.gcd(mine, 512))
    picks, sources = (slots,), ((incoming, 0, lambda at, width: offset // width),)
    if head_count == 2:
        picks = (slots - place * rows, slots - (1 - place) * rows)
        sources = (
            (qkv, plane_start, lambda at, width: at * (mine // width) + start // width),
        ) + sources
    return pack_rows(
        jnp.reshape(place, (1,)).astype(jnp.int32), picks, sources, planes, columns, width
    )


def to_owners(outgoing):
    return lax.all_to_all(outgoing, "seq", split_axis=0, concat_axis=0, tiled=True)


def on_device(qkv, send_rows, recv_pos, req_lengths, norm_gain):
    seq_count, head_count = lax.axis_size("seq"), lax.axis_size("head")
    block = lax.axis_index("seq")
    tok_rows = qkv.shape[1] * head_count
    columns = qkv.shape[2] // head_count

    req_ends = jnp.cumsum(req_lengths)
    req_starts = req_ends - req_lengths
    first_row = block * tok_rows
    positions = first_row + jnp.arange(tok_rows, dtype=jnp.int32)
    segment = jnp.sum((req_starts[None, :] <= positions[:, None]).astype(jnp.int32), axis=1) - 1
    last_rows = (jnp.arange(seq_count, dtype=jnp.int32) + 1) * tok_rows - 1
    last_segment = jnp.sum((req_starts[None, :] <= last_rows[:, None]).astype(jnp.int32), axis=1) - 1
    prev_segment = jnp.sum((req_starts < first_row).astype(jnp.int32)) - 1
    carried_mask = (segment == prev_segment).astype(jnp.int32)[:, None]
    land_row = recv_pos[0].reshape(1, -1)
    landing = first_row + land_row.reshape(-1, 1)
    landing_segment = jnp.sum((req_starts[None, :] <= landing).astype(jnp.int32), axis=1, keepdims=True) - 1
    in_tail = (land_row.reshape(-1, 1) >= 0) & (landing_segment == last_segment[block])
    tail_slots = in_tail.astype(jnp.int32)
    gain = norm_gain.reshape(1, -1)

    rows = send_rows[0]
    head_share = columns // HEAD_DIM
    first = max(2, head_share // 4) * HEAD_DIM
    second = columns - first
    outgoing = pack_chunk(qkv, swap_heads(qkv, KEYS, 2, 0, first), rows, KEYS, 2, 0, first)
    arrived = to_owners(outgoing)
    outgoing = pack_chunk(
        qkv, swap_heads(qkv, KEYS, 2, first, second), rows, KEYS, 2, first, second
    )
    arrived_next = to_owners(outgoing)
    within, across = carry_tables(last_segment)
    sums = carry_within(block_update(arrived, tail_slots), within)
    filled = unpack_keys_values(arrived, land_row, tok_rows, 0, columns, ())
    incoming = swap_heads(qkv, QUERY, 1, 0, columns)
    incoming, sums, filled, tables = lax.optimization_barrier(
        (incoming, sums, filled, (tail_slots, within, across, segment, carried_mask))
    )
    tail_slots, within, across, segment, carried_mask = tables
    part = max(2, head_share // 2) * HEAD_DIM
    outgoing, outgoing_next = (
        pack_chunk(qkv, incoming, rows, QUERY, 1, start, size, start)
        for start, size in ((0, part), (part, columns - part))
    )
    outgoing, pieces = lax.optimization_barrier((outgoing, pass_totals(sums)))
    query = to_owners(outgoing)
    sums = carry_within(block_update(arrived_next, tail_slots), within)
    states = hand_back(pieces, across)
    keys, values = unpack_keys_values(arrived_next, land_row, tok_rows, first, columns, filled)
    outgoing_next, sums, states, keys, values = lax.optimization_barrier(
        (outgoing_next, sums, states, keys, values)
    )
    pieces = pass_totals(sums)
    query_next = to_owners(outgoing_next)
    states = jnp.concatenate(states + hand_back(pieces, across), axis=0)
    tables = (land_row, segment[:, None], segment[None, :], carried_mask)
    out = attend(query, keys, values, states, tables, gain, 0, ())
    return attend(query_next, keys, values, states, tables, gain, part, (out,))


def solution(mesh):
    return jax.shard_map(
        on_device,
        mesh=mesh,
        in_specs=(
            P(None, ("seq", "head"), None),
            P("seq", None, None),
            P("seq", None, None),
            P(),
            P("head"),
        ),
        out_specs=P("seq", "head"),
        check_vma=False,
    )
```

```python
import math

import jax
import jax.numpy as jnp
from jax import lax
from jax.experimental import pallas as pl
from jax.experimental.pallas import tpu as pltpu
from jax.sharding import PartitionSpec as P

HEAD_DIM = 128

norm_eps = 1e-06

QUERY, KEYS, VALUES = 0, 1, 2

PACK_WEIGHT = 20
ATTEND_WEIGHT = 20


def pack_kernel(place_ref, *refs):
    count = (len(refs) - 1) // 3
    picks, sources = refs[:count], refs[count : 2 * count]
    out_ref, chosen = refs[2 * count], refs[2 * count + 1 :]

    @pl.when((pl.program_id(0) == 0) & (pl.program_id(1) == 0))
    def _():
        for pick, onehot in zip(picks, chosen):
            rows = lax.broadcasted_iota(jnp.int32, onehot.shape, 1)
            onehot[...] = jnp.where(pick[...] == rows, 1.0, 0.0).astype(onehot.dtype)

    total = None
    for source, onehot in zip(sources, chosen):
        part = jnp.dot(onehot[...], source[0], preferred_element_type=jnp.float32)
        total = part if total is None else total + part
    out_ref[...] = total.astype(out_ref.dtype)


def pack_rows(place, picks, sources, planes, columns, width):
    slots = picks[0].shape[0]
    blocks = columns // width
    lens = [array.shape[1] for array, _, _ in sources]

    def source_spec(array, plane_start, first):
        return pl.BlockSpec(
            (1, array.shape[1], width),
            lambda p, j, place_ref: (plane_start + p, 0, first(place_ref[0], width) + j),
        )

    return pl.pallas_call(
        pack_kernel,
        out_shape=jax.ShapeDtypeStruct((slots, planes * columns), jnp.bfloat16),
        grid_spec=pltpu.PrefetchScalarGridSpec(
            num_scalar_prefetch=1,
            grid=(planes, blocks),
            in_specs=[pl.BlockSpec((slots, 1), lambda p, j, place_ref: (0, 0)) for _ in picks]
            + [source_spec(*source) for source in sources],
            out_specs=pl.BlockSpec((slots, width), lambda p, j, place_ref: (0, p * blocks + j)),
            scratch_shapes=[pltpu.VMEM((slots, length), jnp.bfloat16) for length in lens],
        ),
        cost_estimate=pl.CostEstimate(
            flops=PACK_WEIGHT * 2 * slots * sum(lens) * planes * columns,
            bytes_accessed=2 * planes * columns * (slots + sum(lens)),
            transcendentals=0,
        ),
        name="pack_rows",
    )(place, *picks, *[array for array, _, _ in sources])


def update_kernel(place_ref, tail_ref, keys_ref, values_ref, *outs):
    tail = tail_ref[...] != 0
    for number, out in enumerate(outs):

        @pl.when(pl.program_id(0) == number)
        def _():
            for part in range(keys_ref.shape[1] // HEAD_DIM):
                columns = slice(part * HEAD_DIM, (part + 1) * HEAD_DIM)
                keys = keys_ref[:, columns]
                out[columns, :] = lax.dot_general(
                    jnp.where(tail, keys, jnp.zeros_like(keys)),
                    values_ref[:, columns],
                    (((0,), (0,)), ((), ())),
                    preferred_element_type=jnp.float32,
                )


def block_update(arrived, tail_slots):
    near, _, place, _ = run_of_blocks()
    slots, columns = arrived.shape[0], arrived.shape[1] // 2
    share = columns // near
    direct = share % HEAD_DIM == 0
    width, blocks = (share, near) if direct else (columns, 1)

    def column_spec(first):
        return pl.BlockSpec((slots, width), lambda j, place_ref: (0, first + (j ^ place_ref[0])))

    updates = pl.pallas_call(
        update_kernel,
        out_shape=(jax.ShapeDtypeStruct((width, HEAD_DIM), jnp.float32),) * blocks,
        grid_spec=pltpu.PrefetchScalarGridSpec(
            num_scalar_prefetch=1,
            grid=(blocks,),
            in_specs=[
                pl.BlockSpec((slots, 1), lambda j, place_ref: (0, 0)),
                column_spec(0),
                column_spec(blocks),
            ],
            out_specs=(pl.BlockSpec((width, HEAD_DIM), lambda j, place_ref: (0, 0)),) * blocks,
        ),
        cost_estimate=pl.CostEstimate(
            flops=2 * slots * columns * HEAD_DIM,
            bytes_accessed=4 * columns * (slots + HEAD_DIM),
            transcendentals=0,
        ),
        name="block_update",
    )(jnp.reshape(place if direct else 0 * place, (1,)), tail_slots, arrived, arrived)
    if direct:
        return list(updates)
    return [
        lax.dynamic_slice_in_dim(updates[0], (place ^ k) * share, share, axis=0)
        for k in range(near)
    ]


def tables_kernel(land_ref, seg_col_ref, seg_row_ref, mask_ref, order, causal, carried):
    rows = lax.broadcasted_iota(jnp.int32, order.shape, 0)
    order[...] = jnp.where(land_ref[...] == rows, 1.0, 0.0).astype(order.dtype)
    later = lax.broadcasted_iota(jnp.int32, causal.shape, 0)
    earlier = lax.broadcasted_iota(jnp.int32, causal.shape, 1)
    open_pair = (earlier <= later) & (seg_col_ref[...] == seg_row_ref[...])
    causal[...] = jnp.where(open_pair, 1.0, 0.0).astype(causal.dtype)
    carried[...] = jnp.broadcast_to(
        jnp.where(mask_ref[...] != 0, 1.0, 0.0).astype(carried.dtype), carried.shape
    )


def block_tables(land_row, segment, carried_mask):
    slots, tok_rows = land_row.shape[1], segment.shape[0]
    return pl.pallas_call(
        tables_kernel,
        out_shape=tuple(
            jax.ShapeDtypeStruct((tok_rows, n), jnp.bfloat16) for n in (slots, tok_rows, HEAD_DIM)
        ),
        cost_estimate=pl.CostEstimate(
            flops=8 * tok_rows * (slots + tok_rows),
            bytes_accessed=2 * tok_rows * (slots + tok_rows),
            transcendentals=0,
        ),
        name="block_tables",
    )(land_row, segment[:, None], segment[None, :], carried_mask)


def unpack_kernel(order_ref, keys_ref, values_ref, *refs):
    for source, out in zip((keys_ref, values_ref), refs[-2:]):
        out[...] = jnp.dot(
            order_ref[...], source[...], preferred_element_type=jnp.float32
        ).astype(out.dtype)


def unpack_keys_values(arrived, order, start, mine, filled):
    slots, columns = arrived.shape[0], arrived.shape[1] // 2
    tok_rows = order.shape[0]
    width = math.gcd(math.gcd(columns, start), 4 * HEAD_DIM)
    blocks, first = columns // width, start // width
    packed = jax.ShapeDtypeStruct((tok_rows, mine), arrived.dtype)
    column_spec = pl.BlockSpec((tok_rows, width), lambda j: (0, first + j))
    return pl.pallas_call(
        unpack_kernel,
        out_shape=(packed, packed),
        grid=(blocks,),
        in_specs=[
            pl.BlockSpec((tok_rows, slots), lambda j: (0, 0)),
            pl.BlockSpec((slots, width), lambda j: (0, j)),
            pl.BlockSpec((slots, width), lambda j: (0, blocks + j)),
        ]
        + [pl.BlockSpec(memory_space=pl.ANY) for _ in filled],
        out_specs=(column_spec, column_spec),
        input_output_aliases={3 + number: number for number in range(len(filled))},
        cost_estimate=pl.CostEstimate(
            flops=4 * tok_rows * columns * slots,
            bytes_accessed=4 * columns * (slots + tok_rows),
            transcendentals=0,
        ),
        name="unpack_keys_values",
    )(order, arrived, arrived, *filled)


def sum_kernel(take_ref, *refs):
    count = take_ref.shape[1]
    pieces, outs = refs[:count], refs[count:]
    for number, out in enumerate(outs):
        total = jnp.zeros(out.shape, jnp.float32)
        for piece in range(count):
            total = total + jnp.where(take_ref[number, piece] != 0, pieces[piece][...], 0.0)
        out[...] = total


def sum_pieces(take, pieces):
    rows = pieces[0].shape[0]
    count = take.shape[0]
    whole = pl.BlockSpec(memory_space=pltpu.VMEM)
    return pl.pallas_call(
        sum_kernel,
        out_shape=(jax.ShapeDtypeStruct((rows, HEAD_DIM), jnp.float32),) * count,
        in_specs=[pl.BlockSpec(memory_space=pltpu.SMEM)] + [whole] * len(pieces),
        out_specs=(whole,) * count,
        cost_estimate=pl.CostEstimate(
            flops=count * len(pieces) * rows * HEAD_DIM,
            bytes_accessed=4 * (len(pieces) + count) * rows * HEAD_DIM,
            transcendentals=0,
        ),
        name="sum_pieces",
    )(take.astype(jnp.int32), *pieces)


def run_of_blocks():
    seq_count, block = lax.axis_size("seq"), lax.axis_index("seq")
    near = run_size()
    return near, seq_count // near, block % near, block // near


def swap_places(value, k):
    seq_count = lax.axis_size("seq")
    return lax.ppermute(value, "seq", [(i, i ^ k) for i in range(seq_count)])


def carry_tables(last_segment):
    near, far, place, run = run_of_blocks()
    base = run * near
    source = base + (place ^ jnp.arange(near))
    before = last_segment[jnp.maximum(source - 1, 0)]
    of_source = last_segment[source]
    inside = (source[None, :] < source[:, None]) & (of_source[None, :] == before[:, None])
    whole = of_source == last_segment[base + near - 1]
    within = jnp.concatenate([inside, whole[None]])
    shifts = jnp.arange(1, far // 2 + 1)
    ends = last_segment[jnp.maximum(run - shifts, 0) * near + near - 1]
    across = (run >= shifts)[None, :] & (ends[None, :] == before[:, None])
    own = jnp.arange(near)[:, None] == jnp.arange(near)[None, :]
    return within, jnp.concatenate([own, across], axis=1)


def carry_within(shares, within):
    return sum_pieces(within, [shares[0]] + [swap_places(shares[k], k) for k in range(1, len(shares))])


def pass_totals(sums):
    seq_count = lax.axis_size("seq")
    near, far, _, _ = run_of_blocks()
    pieces = list(sums[:near])
    for shift in range(1, far // 2 + 1):
        step = shift * near
        pieces.append(
            lax.ppermute(sums[near], "seq", [(i, i + step) for i in range(seq_count - step)])
        )
    return pieces


def hand_back(pieces, across):
    handed = sum_pieces(across, pieces)
    return [handed[0]] + [swap_places(handed[k], k) for k in range(1, len(handed))]


def two_terms(value):
    high = value.astype(jnp.bfloat16)
    return high, (value - high.astype(jnp.float32)).astype(jnp.bfloat16)


def assemble_kernel(place_ref, *refs):
    pieces, out = refs[:-1], refs[-1]
    near = run_size()
    number = 0
    for chunk in range(0, len(pieces), near):
        share = pieces[chunk].shape[0]
        step = math.gcd(share, HEAD_DIM)
        for place in range(near):
            for row in range(0, share, step):
                value = pieces[chunk + place][row : row + step, :]
                for other in range(1, near):
                    piece = pieces[chunk + (place ^ other)]
                    value = jnp.where(place_ref[0] == other, piece[row : row + step, :], value)
                head, within = divmod(number, HEAD_DIM)
                for term, part in enumerate(two_terms(value)):
                    first = (2 * head + term) * HEAD_DIM + within
                    out[first : first + step, :] = part
                number += step


def run_size():
    return math.gcd(lax.axis_size("seq"), 4)


def assemble_states(pieces):
    _, _, place, _ = run_of_blocks()
    rows = sum(piece.shape[0] for piece in pieces)
    whole = pl.BlockSpec(memory_space=pltpu.VMEM)
    return pl.pallas_call(
        assemble_kernel,
        out_shape=jax.ShapeDtypeStruct((2 * rows, HEAD_DIM), jnp.bfloat16),
        in_specs=[pl.BlockSpec(memory_space=pltpu.SMEM)] + [whole] * len(pieces),
        out_specs=whole,
        cost_estimate=pl.CostEstimate(
            flops=8 * rows * HEAD_DIM, bytes_accessed=8 * rows * HEAD_DIM, transcendentals=0
        ),
        name="assemble_states",
    )(jnp.reshape(place, (1,)), *pieces)


def attend_kernel(
    order_ref, causal_ref, carried_ref, gain_ref, arrived_ref, keys_ref, values_ref, states_ref, *refs
):
    out_ref = refs[-1]
    tok_rows = order_ref.shape[0]
    half = tok_rows // 2

    def product(left, right):
        return jnp.dot(left, right, preferred_element_type=jnp.float32)

    ones = jnp.full((2 * HEAD_DIM, HEAD_DIM), 1.0, jnp.bfloat16)
    query = product(order_ref[...], arrived_ref[...]).astype(keys_ref.dtype)
    heads = query.shape[1] // HEAD_DIM
    together = math.gcd(heads, 2)
    for group in range(0, heads, together):
        tiles = []
        for part in range(group, group + together):
            columns = slice(part * HEAD_DIM, (part + 1) * HEAD_DIM)
            for rows, reach in ((slice(0, half), half), (slice(half, tok_rows), tok_rows)):
                scores = lax.dot_general(
                    query[rows, columns],
                    keys_ref[:reach, columns],
                    (((1,), (1,)), ((), ())),
                    preferred_element_type=jnp.float32,
                )
                weights = scores.astype(keys_ref.dtype) * causal_ref[rows, :reach]
                tiles.append((part, columns, rows, reach, weights))
        raws = []
        for part, columns, rows, reach, weights in tiles:
            carrying = query[rows, columns] * carried_ref[rows, :]
            states = states_ref[2 * part * HEAD_DIM : 2 * (part + 1) * HEAD_DIM, :]
            raws.append(
                product(
                    jnp.concatenate([weights, carrying, carrying], axis=1),
                    jnp.concatenate([values_ref[:reach, columns], states], axis=0),
                )
            )
        for (part, columns, rows, reach, weights), raw_out in zip(tiles, raws):
            square = jnp.concatenate(two_terms(raw_out * raw_out), axis=1)
            mean = product(square, ones) * (1.0 / HEAD_DIM)
            out_ref[rows, columns] = (
                raw_out * lax.rsqrt(mean + norm_eps) * gain_ref[:, columns]
            ).astype(out_ref.dtype)


def attend(arrived, keys, values, states, tables, gain, start, filled):
    slots, columns = arrived.shape
    tok_rows, mine = keys.shape
    width = math.gcd(math.gcd(columns, start), 4 * HEAD_DIM)
    first = start // width
    column_spec = pl.BlockSpec((tok_rows, width), lambda j: (0, first + j))
    return pl.pallas_call(
        attend_kernel,
        out_shape=jax.ShapeDtypeStruct((tok_rows, mine), jnp.bfloat16),
        grid=(columns // width,),
        in_specs=[pl.BlockSpec(table.shape, lambda j: (0, 0)) for table in tables]
        + [
            pl.BlockSpec((1, width), lambda j: (0, first + j)),
            pl.BlockSpec((slots, width), lambda j: (0, j)),
            column_spec,
            column_spec,
            pl.BlockSpec((2 * width, HEAD_DIM), lambda j: (first + j, 0)),
        ]
        + [pl.BlockSpec(memory_space=pl.ANY) for _ in filled],
        out_specs=column_spec,
        input_output_aliases={8: 0} if filled else {},
        cost_estimate=pl.CostEstimate(
            flops=ATTEND_WEIGHT * tok_rows * columns * (slots + 2 * tok_rows + 4 * HEAD_DIM),
            bytes_accessed=2 * columns * (slots + 4 * tok_rows),
            transcendentals=0,
        ),
        name="attend",
    )(*tables, gain, arrived, keys, values, states, *filled)


def swap_heads(qkv, plane_start, planes, start, columns):
    head_count = lax.axis_size("head")
    rows = qkv.shape[1]
    mine = qkv.shape[2] // head_count
    part = lax.slice_in_dim(qkv, plane_start, plane_start + planes, axis=0)
    if head_count == 2:
        low = part[:, :, start : start + columns]
        high = part[:, :, mine + start : mine + start + columns]
        outgoing = jnp.where(lax.axis_index("head") == 0, high, low)
        return lax.ppermute(outgoing, "head", [(0, 1), (1, 0)])
    split = part.reshape(planes, rows, head_count, mine)[..., start : start + columns]
    incoming = lax.all_to_all(
        jnp.moveaxis(split, 2, 0), "head", split_axis=0, concat_axis=0, tiled=False
    )
    return jnp.moveaxis(incoming, 0, 1).reshape(planes, head_count * rows, columns)


def pack_chunk(qkv, incoming, send_rows, plane_start, planes, start, columns, offset=0):
    head_count = lax.axis_size("head")
    place = lax.axis_index("head")
    rows = qkv.shape[1]
    mine = qkv.shape[2] // head_count
    slots = send_rows.reshape(-1, 1)
    width = math.gcd(math.gcd(columns, start), math.gcd(mine, 512))
    picks, sources = (slots,), ((incoming, 0, lambda at, width: offset // width),)
    if head_count == 2:
        picks = (slots - place * rows, slots - (1 - place) * rows)
        sources = (
            (qkv, plane_start, lambda at, width: at * (mine // width) + start // width),
        ) + sources
    return pack_rows(
        jnp.reshape(place, (1,)).astype(jnp.int32), picks, sources, planes, columns, width
    )


def to_owners(outgoing):
    return lax.all_to_all(outgoing, "seq", split_axis=0, concat_axis=0, tiled=True)


def on_device(qkv, send_rows, recv_pos, req_lengths, norm_gain):
    seq_count, head_count = lax.axis_size("seq"), lax.axis_size("head")
    block = lax.axis_index("seq")
    tok_rows = qkv.shape[1] * head_count
    columns = qkv.shape[2] // head_count

    req_ends = jnp.cumsum(req_lengths)
    req_starts = req_ends - req_lengths
    first_row = block * tok_rows
    positions = first_row + jnp.arange(tok_rows, dtype=jnp.int32)
    segment = jnp.sum((req_starts[None, :] <= positions[:, None]).astype(jnp.int32), axis=1) - 1
    last_rows = (jnp.arange(seq_count, dtype=jnp.int32) + 1) * tok_rows - 1
    last_segment = jnp.sum((req_starts[None, :] <= last_rows[:, None]).astype(jnp.int32), axis=1) - 1
    prev_segment = jnp.sum((req_starts < first_row).astype(jnp.int32)) - 1
    carried_mask = (segment == prev_segment).astype(jnp.int32)[:, None]
    land_row = recv_pos[0].reshape(1, -1)
    landing = first_row + land_row.reshape(-1, 1)
    landing_segment = jnp.sum((req_starts[None, :] <= landing).astype(jnp.int32), axis=1, keepdims=True) - 1
    in_tail = (land_row.reshape(-1, 1) >= 0) & (landing_segment == last_segment[block])
    tail_slots = in_tail.astype(jnp.int32)
    gain = norm_gain.reshape(1, -1)

    rows = send_rows[0]
    head_share = columns // HEAD_DIM
    first = max(2, head_share // 4) * HEAD_DIM
    second = columns - first
    outgoing = pack_chunk(qkv, swap_heads(qkv, KEYS, 2, 0, first), rows, KEYS, 2, 0, first)
    arrived = to_owners(outgoing)
    outgoing = pack_chunk(
        qkv, swap_heads(qkv, KEYS, 2, first, second), rows, KEYS, 2, first, second
    )
    arrived_next = to_owners(outgoing)
    within, across = carry_tables(last_segment)
    sums = carry_within(block_update(arrived, tail_slots), within)
    tables = block_tables(land_row, segment, carried_mask)
    filled = unpack_keys_values(arrived, tables[0], 0, columns, ())
    incoming = swap_heads(qkv, QUERY, 1, 0, columns)
    incoming, sums, filled, tables, small = lax.optimization_barrier(
        (incoming, sums, filled, tables, (tail_slots, within, across))
    )
    tail_slots, within, across = small
    part = max(2, head_share // 2) * HEAD_DIM
    outgoing, outgoing_next = (
        pack_chunk(qkv, incoming, rows, QUERY, 1, start, size, start)
        for start, size in ((0, part), (part, columns - part))
    )
    outgoing, outgoing_next, pieces = lax.optimization_barrier(
        (outgoing, outgoing_next, pass_totals(sums))
    )
    query = to_owners(outgoing)
    shares, pieces = lax.optimization_barrier((block_update(arrived_next, tail_slots), pieces))
    states = hand_back(pieces, across)
    sums = carry_within(shares, within)
    filled = unpack_keys_values(arrived_next, tables[0], first, columns, filled)
    outgoing_next, sums, states, filled = lax.optimization_barrier(
        (outgoing_next, sums, states, filled)
    )
    pieces = pass_totals(sums)
    query_next = to_owners(outgoing_next)
    states = assemble_states(states + hand_back(pieces, across))
    out = attend(query, *filled, states, tables, gain, 0, ())
    return attend(query_next, *filled, states, tables, gain, part, (out,))


def solution(mesh):
    return jax.shard_map(
        on_device,
        mesh=mesh,
        in_specs=(
            P(None, ("seq", "head"), None),
            P("seq", None, None),
            P("seq", None, None),
            P(),
            P("head"),
        ),
        out_specs=P("seq", "head"),
        check_vma=False,
    )
```

```python
import math

import jax
import jax.numpy as jnp
from jax import lax
from jax.experimental import pallas as pl
from jax.experimental.pallas import tpu as pltpu
from jax.sharding import PartitionSpec as P

HEAD_DIM = 128

norm_eps = 1e-06

QUERY, KEYS, VALUES = 0, 1, 2

PACK_WEIGHT = 20
FINISH_WEIGHT = 1
ATTEND_WEIGHT = 143


def pack_kernel(place_ref, *refs):
    count = (len(refs) - 1) // 3
    picks, sources = refs[:count], refs[count : 2 * count]
    out_ref, chosen = refs[2 * count], refs[2 * count + 1 :]

    @pl.when((pl.program_id(0) == 0) & (pl.program_id(1) == 0))
    def _():
        for pick, onehot in zip(picks, chosen):
            rows = lax.broadcasted_iota(jnp.int32, onehot.shape, 1)
            onehot[...] = jnp.where(pick[...] == rows, 1.0, 0.0).astype(onehot.dtype)

    total = None
    for source, onehot in zip(sources, chosen):
        part = jnp.dot(onehot[...], source[0], preferred_element_type=jnp.float32)
        total = part if total is None else total + part
    out_ref[...] = total.astype(out_ref.dtype)


def pack_rows(place, picks, sources, planes, columns, width):
    slots = picks[0].shape[0]
    blocks = columns // width
    lens = [array.shape[1] for array, _, _ in sources]

    def source_spec(array, plane_start, first):
        return pl.BlockSpec(
            (1, array.shape[1], width),
            lambda p, j, place_ref: (plane_start + p, 0, first(place_ref[0], width) + j),
        )

    return pl.pallas_call(
        pack_kernel,
        out_shape=jax.ShapeDtypeStruct((slots, planes * columns), jnp.bfloat16),
        grid_spec=pltpu.PrefetchScalarGridSpec(
            num_scalar_prefetch=1,
            grid=(planes, blocks),
            in_specs=[pl.BlockSpec((slots, 1), lambda p, j, place_ref: (0, 0)) for _ in picks]
            + [source_spec(*source) for source in sources],
            out_specs=pl.BlockSpec((slots, width), lambda p, j, place_ref: (0, p * blocks + j)),
            scratch_shapes=[pltpu.VMEM((slots, length), jnp.bfloat16) for length in lens],
        ),
        cost_estimate=pl.CostEstimate(
            flops=PACK_WEIGHT * 2 * slots * sum(lens) * planes * columns,
            bytes_accessed=2 * planes * columns * (slots + sum(lens)),
            transcendentals=0,
        ),
        name="pack_rows",
    )(place, *picks, *[array for array, _, _ in sources])


def update_kernel(place_ref, tail_ref, keys_ref, values_ref, *outs):
    for number, out in enumerate(outs):

        @pl.when(pl.program_id(0) == number)
        def _():
            for part in range(keys_ref.shape[1] // HEAD_DIM):
                columns = slice(part * HEAD_DIM, (part + 1) * HEAD_DIM)
                out[columns, :] = lax.dot_general(
                    keys_ref[:, columns] * tail_ref[...],
                    values_ref[:, columns],
                    (((0,), (0,)), ((), ())),
                    preferred_element_type=jnp.float32,
                )


def block_update(arrived, tail_slots):
    near, _, place, _ = run_of_blocks()
    slots, columns = arrived.shape[0], arrived.shape[1] // 2
    share = columns // near
    direct = share % HEAD_DIM == 0
    width, blocks = (share, near) if direct else (columns, 1)

    def column_spec(first):
        return pl.BlockSpec((slots, width), lambda j, place_ref: (0, first + (j ^ place_ref[0])))

    updates = pl.pallas_call(
        update_kernel,
        out_shape=(jax.ShapeDtypeStruct((width, HEAD_DIM), jnp.float32),) * blocks,
        grid_spec=pltpu.PrefetchScalarGridSpec(
            num_scalar_prefetch=1,
            grid=(blocks,),
            in_specs=[
                pl.BlockSpec((slots, HEAD_DIM), lambda j, place_ref: (0, 0)),
                column_spec(0),
                column_spec(blocks),
            ],
            out_specs=(pl.BlockSpec((width, HEAD_DIM), lambda j, place_ref: (0, 0)),) * blocks,
        ),
        cost_estimate=pl.CostEstimate(
            flops=2 * slots * columns * HEAD_DIM,
            bytes_accessed=4 * columns * (slots + HEAD_DIM),
            transcendentals=0,
        ),
        name="block_update",
    )(jnp.reshape(place if direct else 0 * place, (1,)), tail_slots, arrived, arrived)
    if direct:
        return list(updates)
    return [
        lax.dynamic_slice_in_dim(updates[0], (place ^ k) * share, share, axis=0)
        for k in range(near)
    ]


def tables_kernel(land_ref, seg_col_ref, seg_row_ref, mask_ref, order, causal, carried):
    rows = lax.broadcasted_iota(jnp.int32, order.shape, 0)
    order[...] = jnp.where(land_ref[...] == rows, 1.0, 0.0).astype(order.dtype)
    later = lax.broadcasted_iota(jnp.int32, causal.shape, 0)
    earlier = lax.broadcasted_iota(jnp.int32, causal.shape, 1)
    open_pair = (earlier <= later) & (seg_col_ref[...] == seg_row_ref[...])
    causal[...] = jnp.where(open_pair, 1.0, 0.0).astype(causal.dtype)
    carried[...] = jnp.broadcast_to(
        jnp.where(mask_ref[...] != 0, 1.0, 0.0).astype(carried.dtype), carried.shape
    )


def block_tables(land_row, segment, carried_mask):
    slots, tok_rows = land_row.shape[1], segment.shape[0]
    return pl.pallas_call(
        tables_kernel,
        out_shape=tuple(
            jax.ShapeDtypeStruct((tok_rows, n), jnp.bfloat16) for n in (slots, tok_rows, HEAD_DIM)
        ),
        cost_estimate=pl.CostEstimate(
            flops=8 * tok_rows * (slots + tok_rows),
            bytes_accessed=2 * tok_rows * (slots + tok_rows),
            transcendentals=0,
        ),
        name="block_tables",
    )(land_row, segment[:, None], segment[None, :], carried_mask)


def unpack_kernel(order_ref, keys_ref, values_ref, *refs):
    for source, out in zip((keys_ref, values_ref), refs[-2:]):
        out[...] = jnp.dot(
            order_ref[...], source[...], preferred_element_type=jnp.float32
        ).astype(out.dtype)


def unpack_keys_values(arrived, order, start, mine, filled):
    slots, columns = arrived.shape[0], arrived.shape[1] // 2
    tok_rows = order.shape[0]
    width = math.gcd(math.gcd(columns, start), 4 * HEAD_DIM)
    blocks, first = columns // width, start // width
    packed = jax.ShapeDtypeStruct((tok_rows, mine), arrived.dtype)
    column_spec = pl.BlockSpec((tok_rows, width), lambda j: (0, first + j))
    return pl.pallas_call(
        unpack_kernel,
        out_shape=(packed, packed),
        grid=(blocks,),
        in_specs=[
            pl.BlockSpec((tok_rows, slots), lambda j: (0, 0)),
            pl.BlockSpec((slots, width), lambda j: (0, j)),
            pl.BlockSpec((slots, width), lambda j: (0, blocks + j)),
        ]
        + [pl.BlockSpec(memory_space=pl.ANY) for _ in filled],
        out_specs=(column_spec, column_spec),
        input_output_aliases={3 + number: number for number in range(len(filled))},
        cost_estimate=pl.CostEstimate(
            flops=4 * tok_rows * columns * slots,
            bytes_accessed=4 * columns * (slots + tok_rows),
            transcendentals=0,
        ),
        name="unpack_keys_values",
    )(order, arrived, arrived, *filled)


def sum_kernel(take_ref, *refs):
    count = take_ref.shape[1]
    pieces, outs = refs[:count], refs[count:]
    for number, out in enumerate(outs):
        total = jnp.zeros(out.shape, jnp.float32)
        for piece in range(count):
            total = total + jnp.where(take_ref[number, piece] != 0, pieces[piece][...], 0.0)
        out[...] = total


def sum_pieces(take, pieces):
    rows = pieces[0].shape[0]
    count = take.shape[0]
    whole = pl.BlockSpec(memory_space=pltpu.VMEM)
    return pl.pallas_call(
        sum_kernel,
        out_shape=(jax.ShapeDtypeStruct((rows, HEAD_DIM), jnp.float32),) * count,
        in_specs=[pl.BlockSpec(memory_space=pltpu.SMEM)] + [whole] * len(pieces),
        out_specs=(whole,) * count,
        cost_estimate=pl.CostEstimate(
            flops=count * len(pieces) * rows * HEAD_DIM,
            bytes_accessed=4 * (len(pieces) + count) * rows * HEAD_DIM,
            transcendentals=0,
        ),
        name="sum_pieces",
    )(take.astype(jnp.int32), *pieces)


def run_of_blocks():
    seq_count, block = lax.axis_size("seq"), lax.axis_index("seq")
    near = run_size()
    return near, seq_count // near, block % near, block // near


def swap_places(value, k):
    seq_count = lax.axis_size("seq")
    return lax.ppermute(value, "seq", [(i, i ^ k) for i in range(seq_count)])


def carry_tables(last_segment):
    near, far, place, run = run_of_blocks()
    base = run * near
    source = base + (place ^ jnp.arange(near))
    before = last_segment[jnp.maximum(source - 1, 0)]
    of_source = last_segment[source]
    inside = (source[None, :] < source[:, None]) & (of_source[None, :] == before[:, None])
    whole = of_source == last_segment[base + near - 1]
    within = jnp.concatenate([inside, whole[None]])
    shifts = jnp.arange(1, far // 2 + 1)
    ends = last_segment[jnp.maximum(run - shifts, 0) * near + near - 1]
    across = (run >= shifts)[None, :] & (ends[None, :] == before[:, None])
    own = jnp.arange(near)[:, None] == jnp.arange(near)[None, :]
    return within, jnp.concatenate([own, across], axis=1)


def carry_within(shares, within):
    return sum_pieces(within, [shares[0]] + [swap_places(shares[k], k) for k in range(1, len(shares))])


def pass_totals(sums):
    seq_count = lax.axis_size("seq")
    near, far, _, _ = run_of_blocks()
    pieces = list(sums[:near])
    for shift in range(1, far // 2 + 1):
        step = shift * near
        pieces.append(
            lax.ppermute(sums[near], "seq", [(i, i + step) for i in range(seq_count - step)])
        )
    return pieces


def hand_back(pieces, across):
    handed = sum_pieces(across, pieces)
    return [handed[0]] + [swap_places(handed[k], k) for k in range(1, len(handed))]


def two_terms(value):
    high = value.astype(jnp.bfloat16)
    return high, (value - high.astype(jnp.float32)).astype(jnp.bfloat16)


def assemble_kernel(place_ref, *refs):
    pieces, out = refs[:-1], refs[-1]
    near = run_size()
    number = 0
    for chunk in range(0, len(pieces), near):
        share = pieces[chunk].shape[0]
        step = math.gcd(share, HEAD_DIM)
        for place in range(near):
            for row in range(0, share, step):
                value = pieces[chunk + place][row : row + step, :]
                for other in range(1, near):
                    piece = pieces[chunk + (place ^ other)]
                    value = jnp.where(place_ref[0] == other, piece[row : row + step, :], value)
                head, within = divmod(number, HEAD_DIM)
                for term, part in enumerate(two_terms(value)):
                    first = (2 * head + term) * HEAD_DIM + within
                    out[first : first + step, :] = part
                number += step


def run_size():
    return math.gcd(lax.axis_size("seq"), 4)


def assemble_states(pieces):
    _, _, place, _ = run_of_blocks()
    rows = sum(piece.shape[0] for piece in pieces)
    whole = pl.BlockSpec(memory_space=pltpu.VMEM)
    return pl.pallas_call(
        assemble_kernel,
        out_shape=jax.ShapeDtypeStruct((2 * rows, HEAD_DIM), jnp.bfloat16),
        in_specs=[pl.BlockSpec(memory_space=pltpu.SMEM)] + [whole] * len(pieces),
        out_specs=whole,
        cost_estimate=pl.CostEstimate(
            flops=8 * rows * HEAD_DIM, bytes_accessed=8 * rows * HEAD_DIM, transcendentals=0
        ),
        name="assemble_states",
    )(jnp.reshape(place, (1,)), *pieces)


def product(left, right):
    return jnp.dot(left, right, preferred_element_type=jnp.float32)


def attend_kernel(
    order_ref, causal_ref, carried_ref, gain_ref, arrived_ref, keys_ref, values_ref, states_ref, *refs
):
    out_ref = refs[-1]
    tok_rows = order_ref.shape[0]
    half = tok_rows // 2

    ones = jnp.full((2 * HEAD_DIM, HEAD_DIM), 1.0, jnp.bfloat16)
    query = product(order_ref[...], arrived_ref[...]).astype(keys_ref.dtype)
    heads = query.shape[1] // HEAD_DIM
    together = math.gcd(heads, 2)
    for group in range(0, heads, together):
        tiles = []
        for part in range(group, group + together):
            columns = slice(part * HEAD_DIM, (part + 1) * HEAD_DIM)
            for rows, reach in ((slice(0, half), half), (slice(half, tok_rows), tok_rows)):
                scores = lax.dot_general(
                    query[rows, columns],
                    keys_ref[:reach, columns],
                    (((1,), (1,)), ((), ())),
                    preferred_element_type=jnp.float32,
                )
                weights = scores.astype(keys_ref.dtype) * causal_ref[rows, :reach]
                tiles.append((part, columns, rows, reach, weights))
        raws = []
        for part, columns, rows, reach, weights in tiles:
            carrying = query[rows, columns] * carried_ref[rows, :]
            states = states_ref[2 * part * HEAD_DIM : 2 * (part + 1) * HEAD_DIM, :]
            raws.append(
                product(
                    jnp.concatenate([weights, carrying, carrying], axis=1),
                    jnp.concatenate([values_ref[:reach, columns], states], axis=0),
                )
            )
        for (part, columns, rows, reach, weights), raw_out in zip(tiles, raws):
            square = jnp.concatenate(two_terms(raw_out * raw_out), axis=1)
            mean = product(square, ones) * (1.0 / HEAD_DIM)
            out_ref[rows, columns] = (
                raw_out * lax.rsqrt(mean + norm_eps) * gain_ref[:, columns]
            ).astype(out_ref.dtype)


def attend(arrived, keys, values, states, tables, gain, start, filled):
    slots, columns = arrived.shape
    tok_rows, mine = keys.shape
    width = math.gcd(math.gcd(columns, start), 4 * HEAD_DIM)
    first = start // width
    column_spec = pl.BlockSpec((tok_rows, width), lambda j: (0, first + j))
    return pl.pallas_call(
        attend_kernel,
        out_shape=jax.ShapeDtypeStruct((tok_rows, mine), jnp.bfloat16),
        grid=(columns // width,),
        in_specs=[pl.BlockSpec(table.shape, lambda j: (0, 0)) for table in tables]
        + [
            pl.BlockSpec((1, width), lambda j: (0, first + j)),
            pl.BlockSpec((slots, width), lambda j: (0, j)),
            column_spec,
            column_spec,
            pl.BlockSpec((2 * width, HEAD_DIM), lambda j: (first + j, 0)),
        ]
        + [pl.BlockSpec(memory_space=pl.ANY) for _ in filled],
        out_specs=column_spec,
        input_output_aliases={8: 0} if filled else {},
        cost_estimate=pl.CostEstimate(
            flops=ATTEND_WEIGHT * tok_rows * columns * (slots + 2 * tok_rows + 4 * HEAD_DIM) // 5,
            bytes_accessed=2 * columns * (slots + 4 * tok_rows),
            transcendentals=0,
        ),
        name="attend",
    )(*tables, gain, arrived, keys, values, states, *filled)


def local_kernel(order_ref, causal_ref, carried_ref, arrived_ref, keys_ref, values_ref, *refs):
    query_out, local_out = refs[-2:]
    tok_rows = order_ref.shape[0]
    half = tok_rows // 2
    query = product(order_ref[...], arrived_ref[...]).astype(keys_ref.dtype)
    heads = query.shape[1] // HEAD_DIM
    together = math.gcd(heads, 2)
    for group in range(0, heads, together):
        tiles = []
        for part in range(group, group + together):
            columns = slice(part * HEAD_DIM, (part + 1) * HEAD_DIM)
            query_out[:, columns] = query[:, columns] * carried_ref[...]
            for rows, reach in ((slice(0, half), half), (slice(half, tok_rows), tok_rows)):
                scores = lax.dot_general(
                    query[rows, columns],
                    keys_ref[:reach, columns],
                    (((1,), (1,)), ((), ())),
                    preferred_element_type=jnp.float32,
                )
                weights = scores.astype(keys_ref.dtype) * causal_ref[rows, :reach]
                tiles.append((columns, rows, reach, weights))
        for columns, rows, reach, weights in tiles:
            local_out[rows, columns] = product(weights, values_ref[:reach, columns])


def attend_locally(arrived, keys, values, tables):
    slots, columns = arrived.shape
    tok_rows = keys.shape[0]
    width = math.gcd(columns, 4 * HEAD_DIM)
    column_spec = pl.BlockSpec((tok_rows, width), lambda j: (0, j))
    return pl.pallas_call(
        local_kernel,
        out_shape=tuple(
            jax.ShapeDtypeStruct((tok_rows, columns), dtype) for dtype in (jnp.bfloat16, jnp.float32)
        ),
        grid=(columns // width,),
        in_specs=[pl.BlockSpec(table.shape, lambda j: (0, 0)) for table in tables]
        + [pl.BlockSpec((slots, width), lambda j: (0, j)), column_spec, column_spec],
        out_specs=(column_spec, column_spec),
        cost_estimate=pl.CostEstimate(
            flops=ATTEND_WEIGHT * tok_rows * columns * (slots + 2 * tok_rows) // 5,
            bytes_accessed=2 * columns * (slots + 5 * tok_rows),
            transcendentals=0,
        ),
        name="attend_locally",
    )(*tables, arrived, keys, values)


def finish_kernel(gain_ref, query_ref, local_ref, states_ref, out_ref):
    ones = jnp.full((2 * HEAD_DIM, HEAD_DIM), 1.0, jnp.bfloat16)
    raws = []
    for part in range(out_ref.shape[1] // HEAD_DIM):
        columns = slice(part * HEAD_DIM, (part + 1) * HEAD_DIM)
        query = query_ref[:, columns]
        states = states_ref[2 * part * HEAD_DIM : 2 * (part + 1) * HEAD_DIM, :]
        carried_term = product(jnp.concatenate([query, query], axis=1), states)
        raws.append((columns, local_ref[:, columns] + carried_term))
    for columns, raw_out in raws:
        square = jnp.concatenate(two_terms(raw_out * raw_out), axis=1)
        mean = product(square, ones) * (1.0 / HEAD_DIM)
        out_ref[:, columns] = (raw_out * lax.rsqrt(mean + norm_eps) * gain_ref[:, columns]).astype(
            out_ref.dtype
        )


def finish(query, local_term, states, gain):
    tok_rows, columns = query.shape
    width = math.gcd(columns, 4 * HEAD_DIM)
    column_spec = pl.BlockSpec((tok_rows, width), lambda j: (0, j))
    return pl.pallas_call(
        finish_kernel,
        out_shape=jax.ShapeDtypeStruct((tok_rows, gain.shape[1]), jnp.bfloat16),
        grid=(columns // width,),
        in_specs=[
            pl.BlockSpec((1, width), lambda j: (0, j)),
            column_spec,
            column_spec,
            pl.BlockSpec((2 * width, HEAD_DIM), lambda j: (j, 0)),
        ],
        out_specs=column_spec,
        cost_estimate=pl.CostEstimate(
            flops=FINISH_WEIGHT * 8 * tok_rows * columns * HEAD_DIM,
            bytes_accessed=8 * columns * tok_rows,
            transcendentals=0,
        ),
        name="finish",
    )(gain, query, local_term, states)


def swap_heads(qkv, plane_start, planes, start, columns):
    head_count = lax.axis_size("head")
    rows = qkv.shape[1]
    mine = qkv.shape[2] // head_count
    part = lax.slice_in_dim(qkv, plane_start, plane_start + planes, axis=0)
    if head_count == 2:
        low = part[:, :, start : start + columns]
        high = part[:, :, mine + start : mine + start + columns]
        outgoing = jnp.where(lax.axis_index("head") == 0, high, low)
        return lax.ppermute(outgoing, "head", [(0, 1), (1, 0)])
    split = part.reshape(planes, rows, head_count, mine)[..., start : start + columns]
    incoming = lax.all_to_all(
        jnp.moveaxis(split, 2, 0), "head", split_axis=0, concat_axis=0, tiled=False
    )
    return jnp.moveaxis(incoming, 0, 1).reshape(planes, head_count * rows, columns)


def pack_chunk(qkv, incoming, send_rows, plane_start, planes, start, columns, offset=0):
    head_count = lax.axis_size("head")
    place = lax.axis_index("head")
    rows = qkv.shape[1]
    mine = qkv.shape[2] // head_count
    slots = send_rows.reshape(-1, 1)
    width = math.gcd(math.gcd(columns, start), math.gcd(mine, 512))
    picks, sources = (slots,), ((incoming, 0, lambda at, width: offset // width),)
    if head_count == 2:
        picks = (slots - place * rows, slots - (1 - place) * rows)
        sources = (
            (qkv, plane_start, lambda at, width: at * (mine // width) + start // width),
        ) + sources
    return pack_rows(
        jnp.reshape(place, (1,)).astype(jnp.int32), picks, sources, planes, columns, width
    )


def to_owners(outgoing):
    return lax.all_to_all(outgoing, "seq", split_axis=0, concat_axis=0, tiled=True)


def on_device(qkv, send_rows, recv_pos, req_lengths, norm_gain):
    seq_count, head_count = lax.axis_size("seq"), lax.axis_size("head")
    block = lax.axis_index("seq")
    tok_rows = qkv.shape[1] * head_count
    columns = qkv.shape[2] // head_count

    req_ends = jnp.cumsum(req_lengths)
    req_starts = req_ends - req_lengths
    first_row = block * tok_rows
    positions = first_row + jnp.arange(tok_rows, dtype=jnp.int32)
    segment = jnp.sum((req_starts[None, :] <= positions[:, None]).astype(jnp.int32), axis=1) - 1
    last_rows = (jnp.arange(seq_count, dtype=jnp.int32) + 1) * tok_rows - 1
    last_segment = jnp.sum((req_starts[None, :] <= last_rows[:, None]).astype(jnp.int32), axis=1) - 1
    prev_segment = jnp.sum((req_starts < first_row).astype(jnp.int32)) - 1
    carried_mask = (segment == prev_segment).astype(jnp.int32)[:, None]
    land_row = recv_pos[0].reshape(1, -1)
    landing = first_row + land_row.reshape(-1, 1)
    landing_segment = jnp.sum((req_starts[None, :] <= landing).astype(jnp.int32), axis=1, keepdims=True) - 1
    in_tail = (land_row.reshape(-1, 1) >= 0) & (landing_segment == last_segment[block])
    tail_slots = jnp.broadcast_to(in_tail.astype(jnp.bfloat16), (land_row.shape[1], HEAD_DIM))
    gain = norm_gain.reshape(1, -1)

    rows = send_rows[0]
    head_share = columns // HEAD_DIM
    first = max(2, head_share // 4) * HEAD_DIM
    second = columns - first
    outgoing = pack_chunk(qkv, swap_heads(qkv, KEYS, 2, 0, first), rows, KEYS, 2, 0, first)
    arrived = to_owners(outgoing)
    outgoing = pack_chunk(
        qkv, swap_heads(qkv, KEYS, 2, first, second), rows, KEYS, 2, first, second
    )
    arrived_next = to_owners(outgoing)
    within, across = carry_tables(last_segment)
    sums = carry_within(block_update(arrived, tail_slots), within)
    tables = block_tables(land_row, segment, carried_mask)
    filled = unpack_keys_values(arrived, tables[0], 0, columns, ())
    incoming = swap_heads(qkv, QUERY, 1, 0, columns)
    incoming, sums, filled, tables, small = lax.optimization_barrier(
        (incoming, sums, filled, tables, (tail_slots, within, across))
    )
    tail_slots, within, across = small
    part = max(2, head_share // 2) * HEAD_DIM
    outgoing, outgoing_next = (
        pack_chunk(qkv, incoming, rows, QUERY, 1, start, size, start)
        for start, size in ((0, part), (part, columns - part))
    )
    outgoing, outgoing_next, pieces = lax.optimization_barrier(
        (outgoing, outgoing_next, pass_totals(sums))
    )
    query = to_owners(outgoing)
    shares, pieces = lax.optimization_barrier((block_update(arrived_next, tail_slots), pieces))
    states = hand_back(pieces, across)
    sums = carry_within(shares, within)
    filled = unpack_keys_values(arrived_next, tables[0], first, columns, filled)
    outgoing_next, sums, states, filled = lax.optimization_barrier(
        (outgoing_next, sums, states, filled)
    )
    pieces = pass_totals(sums)
    query_next = to_owners(outgoing_next)
    states += hand_back(pieces, across)
    local = attend_locally(query, *filled, tables)
    states = assemble_states(states)
    out = finish(*local, states, gain)
    return attend(query_next, *filled, states, tables, gain, part, (out,))


def solution(mesh):
    return jax.shard_map(
        on_device,
        mesh=mesh,
        in_specs=(
            P(None, ("seq", "head"), None),
            P("seq", None, None),
            P("seq", None, None),
            P(),
            P("head"),
        ),
        out_specs=P("seq", "head"),
        check_vma=False,
    )
```

```python
import math

import jax
import jax.numpy as jnp
from jax import lax
from jax.experimental import pallas as pl
from jax.experimental.pallas import tpu as pltpu
from jax.sharding import PartitionSpec as P

HEAD_DIM = 128

norm_eps = 1e-06

QUERY, KEYS, VALUES = 0, 1, 2

PACK_WEIGHT = 20
FINISH_WEIGHT = 1
ATTEND_WEIGHT = 145


def pack_kernel(place_ref, *refs):
    count = (len(refs) - 1) // 3
    picks, sources = refs[:count], refs[count : 2 * count]
    out_ref, chosen = refs[2 * count], refs[2 * count + 1 :]

    @pl.when((pl.program_id(0) == 0) & (pl.program_id(1) == 0))
    def _():
        for pick, onehot in zip(picks, chosen):
            rows = lax.broadcasted_iota(jnp.int32, onehot.shape, 1)
            onehot[...] = jnp.where(pick[...] == rows, 1.0, 0.0).astype(onehot.dtype)

    total = None
    for source, onehot in zip(sources, chosen):
        part = jnp.dot(onehot[...], source[0], preferred_element_type=jnp.float32)
        total = part if total is None else total + part
    out_ref[...] = total.astype(out_ref.dtype)


def pack_rows(place, picks, sources, planes, columns, width):
    slots = picks[0].shape[0]
    blocks = columns // width
    lens = [array.shape[1] for array, _, _ in sources]

    def source_spec(array, plane_start, first):
        return pl.BlockSpec(
            (1, array.shape[1], width),
            lambda p, j, place_ref: (plane_start + p, 0, first(place_ref[0], width) + j),
        )

    return pl.pallas_call(
        pack_kernel,
        out_shape=jax.ShapeDtypeStruct((slots, planes * columns), jnp.bfloat16),
        grid_spec=pltpu.PrefetchScalarGridSpec(
            num_scalar_prefetch=1,
            grid=(planes, blocks),
            in_specs=[pl.BlockSpec((slots, 1), lambda p, j, place_ref: (0, 0)) for _ in picks]
            + [source_spec(*source) for source in sources],
            out_specs=pl.BlockSpec((slots, width), lambda p, j, place_ref: (0, p * blocks + j)),
            scratch_shapes=[pltpu.VMEM((slots, length), jnp.bfloat16) for length in lens],
        ),
        cost_estimate=pl.CostEstimate(
            flops=PACK_WEIGHT * 2 * slots * sum(lens) * planes * columns,
            bytes_accessed=2 * planes * columns * (slots + sum(lens)),
            transcendentals=0,
        ),
        name="pack_rows",
    )(place, *picks, *[array for array, _, _ in sources])


def update_kernel(place_ref, tail_ref, keys_ref, values_ref, *outs):
    for number, out in enumerate(outs):

        @pl.when(pl.program_id(0) == number)
        def _():
            for part in range(keys_ref.shape[1] // HEAD_DIM):
                columns = slice(part * HEAD_DIM, (part + 1) * HEAD_DIM)
                out[columns, :] = lax.dot_general(
                    keys_ref[:, columns] * tail_ref[...],
                    values_ref[:, columns],
                    (((0,), (0,)), ((), ())),
                    preferred_element_type=jnp.float32,
                )


def block_update(arrived, tail_slots):
    near, _, place, _ = run_of_blocks()
    slots, columns = arrived.shape[0], arrived.shape[1] // 2
    share = columns // near
    direct = share % HEAD_DIM == 0
    width, blocks = (share, near) if direct else (columns, 1)

    def column_spec(first):
        return pl.BlockSpec((slots, width), lambda j, place_ref: (0, first + (j ^ place_ref[0])))

    updates = pl.pallas_call(
        update_kernel,
        out_shape=(jax.ShapeDtypeStruct((width, HEAD_DIM), jnp.float32),) * blocks,
        grid_spec=pltpu.PrefetchScalarGridSpec(
            num_scalar_prefetch=1,
            grid=(blocks,),
            in_specs=[
                pl.BlockSpec((slots, HEAD_DIM), lambda j, place_ref: (0, 0)),
                column_spec(0),
                column_spec(blocks),
            ],
            out_specs=(pl.BlockSpec((width, HEAD_DIM), lambda j, place_ref: (0, 0)),) * blocks,
        ),
        cost_estimate=pl.CostEstimate(
            flops=2 * slots * columns * HEAD_DIM,
            bytes_accessed=4 * columns * (slots + HEAD_DIM),
            transcendentals=0,
        ),
        name="block_update",
    )(jnp.reshape(place if direct else 0 * place, (1,)), tail_slots, arrived, arrived)
    if direct:
        return list(updates)
    return [
        lax.dynamic_slice_in_dim(updates[0], (place ^ k) * share, share, axis=0)
        for k in range(near)
    ]


def tables_kernel(land_ref, seg_col_ref, seg_row_ref, mask_ref, order, causal, carried):
    rows = lax.broadcasted_iota(jnp.int32, order.shape, 0)
    order[...] = jnp.where(land_ref[...] == rows, 1.0, 0.0).astype(order.dtype)
    later = lax.broadcasted_iota(jnp.int32, causal.shape, 0)
    earlier = lax.broadcasted_iota(jnp.int32, causal.shape, 1)
    open_pair = (earlier <= later) & (seg_col_ref[...] == seg_row_ref[...])
    causal[...] = jnp.where(open_pair, 1.0, 0.0).astype(causal.dtype)
    carried[...] = jnp.broadcast_to(
        jnp.where(mask_ref[...] != 0, 1.0, 0.0).astype(carried.dtype), carried.shape
    )


def block_tables(land_row, segment, carried_mask):
    slots, tok_rows = land_row.shape[1], segment.shape[0]
    return pl.pallas_call(
        tables_kernel,
        out_shape=tuple(
            jax.ShapeDtypeStruct((tok_rows, n), jnp.bfloat16) for n in (slots, tok_rows, HEAD_DIM)
        ),
        cost_estimate=pl.CostEstimate(
            flops=8 * tok_rows * (slots + tok_rows),
            bytes_accessed=2 * tok_rows * (slots + tok_rows),
            transcendentals=0,
        ),
        name="block_tables",
    )(land_row, segment[:, None], segment[None, :], carried_mask)


def unpack_kernel(order_ref, keys_ref, values_ref, *refs):
    for source, out in zip((keys_ref, values_ref), refs[-2:]):
        out[...] = jnp.dot(
            order_ref[...], source[...], preferred_element_type=jnp.float32
        ).astype(out.dtype)


def unpack_keys_values(arrived, order, start, mine, filled):
    slots, columns = arrived.shape[0], arrived.shape[1] // 2
    tok_rows = order.shape[0]
    width = math.gcd(math.gcd(columns, start), 4 * HEAD_DIM)
    blocks, first = columns // width, start // width
    packed = jax.ShapeDtypeStruct((tok_rows, mine), arrived.dtype)
    column_spec = pl.BlockSpec((tok_rows, width), lambda j: (0, first + j))
    return pl.pallas_call(
        unpack_kernel,
        out_shape=(packed, packed),
        grid=(blocks,),
        in_specs=[
            pl.BlockSpec((tok_rows, slots), lambda j: (0, 0)),
            pl.BlockSpec((slots, width), lambda j: (0, j)),
            pl.BlockSpec((slots, width), lambda j: (0, blocks + j)),
        ]
        + [pl.BlockSpec(memory_space=pl.ANY) for _ in filled],
        out_specs=(column_spec, column_spec),
        input_output_aliases={3 + number: number for number in range(len(filled))},
        cost_estimate=pl.CostEstimate(
            flops=4 * tok_rows * columns * slots,
            bytes_accessed=4 * columns * (slots + tok_rows),
            transcendentals=0,
        ),
        name="unpack_keys_values",
    )(order, arrived, arrived, *filled)


def sum_kernel(take_ref, *refs):
    count = take_ref.shape[1]
    pieces, outs = refs[:count], refs[count:]
    for number, out in enumerate(outs):
        total = jnp.zeros(out.shape, jnp.float32)
        for piece in range(count):
            total = total + jnp.where(take_ref[number, piece] != 0, pieces[piece][...], 0.0)
        out[...] = total


def sum_pieces(take, pieces):
    rows = pieces[0].shape[0]
    count = take.shape[0]
    whole = pl.BlockSpec(memory_space=pltpu.VMEM)
    return pl.pallas_call(
        sum_kernel,
        out_shape=(jax.ShapeDtypeStruct((rows, HEAD_DIM), jnp.float32),) * count,
        in_specs=[pl.BlockSpec(memory_space=pltpu.SMEM)] + [whole] * len(pieces),
        out_specs=(whole,) * count,
        cost_estimate=pl.CostEstimate(
            flops=count * len(pieces) * rows * HEAD_DIM,
            bytes_accessed=4 * (len(pieces) + count) * rows * HEAD_DIM,
            transcendentals=0,
        ),
        name="sum_pieces",
    )(take.astype(jnp.int32), *pieces)


def run_of_blocks():
    seq_count, block = lax.axis_size("seq"), lax.axis_index("seq")
    near = run_size()
    return near, seq_count // near, block % near, block // near


def swap_places(value, k):
    seq_count = lax.axis_size("seq")
    return lax.ppermute(value, "seq", [(i, i ^ k) for i in range(seq_count)])


def carry_tables(last_segment):
    near, far, place, run = run_of_blocks()
    base = run * near
    source = base + (place ^ jnp.arange(near))
    before = last_segment[jnp.maximum(source - 1, 0)]
    of_source = last_segment[source]
    inside = (source[None, :] < source[:, None]) & (of_source[None, :] == before[:, None])
    whole = of_source == last_segment[base + near - 1]
    within = jnp.concatenate([inside, whole[None]])
    shifts = jnp.arange(1, far // 2 + 1)
    ends = last_segment[jnp.maximum(run - shifts, 0) * near + near - 1]
    across = (run >= shifts)[None, :] & (ends[None, :] == before[:, None])
    own = jnp.arange(near)[:, None] == jnp.arange(near)[None, :]
    return within, jnp.concatenate([own, across], axis=1)


def carry_within(shares, within):
    return sum_pieces(within, [shares[0]] + [swap_places(shares[k], k) for k in range(1, len(shares))])


def pass_totals(sums):
    seq_count = lax.axis_size("seq")
    near, far, _, _ = run_of_blocks()
    pieces = list(sums[:near])
    for shift in range(1, far // 2 + 1):
        step = shift * near
        pieces.append(
            lax.ppermute(sums[near], "seq", [(i, i + step) for i in range(seq_count - step)])
        )
    return pieces


def hand_back(pieces, across):
    handed = sum_pieces(across, pieces)
    return [handed[0]] + [swap_places(handed[k], k) for k in range(1, len(handed))]


def two_terms(value):
    high = value.astype(jnp.bfloat16)
    return high, (value - high.astype(jnp.float32)).astype(jnp.bfloat16)


def assemble_kernel(place_ref, *refs):
    pieces, out = refs[:-1], refs[-1]
    near = run_size()
    number = 0
    for chunk in range(0, len(pieces), near):
        share = pieces[chunk].shape[0]
        step = math.gcd(share, HEAD_DIM)
        for place in range(near):
            for row in range(0, share, step):
                value = pieces[chunk + place][row : row + step, :]
                for other in range(1, near):
                    piece = pieces[chunk + (place ^ other)]
                    value = jnp.where(place_ref[0] == other, piece[row : row + step, :], value)
                head, within = divmod(number, HEAD_DIM)
                for term, part in enumerate(two_terms(value)):
                    first = (2 * head + term) * HEAD_DIM + within
                    out[first : first + step, :] = part
                number += step


def run_size():
    return math.gcd(lax.axis_size("seq"), 4)


def assemble_states(pieces):
    _, _, place, _ = run_of_blocks()
    rows = sum(piece.shape[0] for piece in pieces)
    whole = pl.BlockSpec(memory_space=pltpu.VMEM)
    return pl.pallas_call(
        assemble_kernel,
        out_shape=jax.ShapeDtypeStruct((2 * rows, HEAD_DIM), jnp.bfloat16),
        in_specs=[pl.BlockSpec(memory_space=pltpu.SMEM)] + [whole] * len(pieces),
        out_specs=whole,
        cost_estimate=pl.CostEstimate(
            flops=8 * rows * HEAD_DIM, bytes_accessed=8 * rows * HEAD_DIM, transcendentals=0
        ),
        name="assemble_states",
    )(jnp.reshape(place, (1,)), *pieces)


def product(left, right):
    return jnp.dot(left, right, preferred_element_type=jnp.float32)


def attend_kernel(
    order_ref, causal_ref, carried_ref, gain_ref, arrived_ref, keys_ref, values_ref, states_ref, *refs
):
    out_ref = refs[-1]
    tok_rows = order_ref.shape[0]
    half = tok_rows // 2

    ones = jnp.full((2 * HEAD_DIM, HEAD_DIM), 1.0, jnp.bfloat16)
    query = product(order_ref[...], arrived_ref[...]).astype(keys_ref.dtype)
    heads = query.shape[1] // HEAD_DIM
    together = math.gcd(heads, 2)
    for group in range(0, heads, together):
        tiles = []
        for part in range(group, group + together):
            columns = slice(part * HEAD_DIM, (part + 1) * HEAD_DIM)
            for rows, reach in ((slice(0, half), half), (slice(half, tok_rows), tok_rows)):
                scores = lax.dot_general(
                    query[rows, columns],
                    keys_ref[:reach, columns],
                    (((1,), (1,)), ((), ())),
                    preferred_element_type=jnp.float32,
                )
                weights = scores.astype(keys_ref.dtype) * causal_ref[rows, :reach]
                tiles.append((part, columns, rows, reach, weights))
        raws = []
        for part, columns, rows, reach, weights in tiles:
            carrying = query[rows, columns] * carried_ref[rows, :]
            states = states_ref[2 * part * HEAD_DIM : 2 * (part + 1) * HEAD_DIM, :]
            raws.append(
                product(
                    jnp.concatenate([weights, carrying, carrying], axis=1),
                    jnp.concatenate([values_ref[:reach, columns], states], axis=0),
                )
            )
        for (part, columns, rows, reach, weights), raw_out in zip(tiles, raws):
            square = jnp.concatenate(two_terms(raw_out * raw_out), axis=1)
            mean = product(square, ones) * (1.0 / HEAD_DIM)
            out_ref[rows, columns] = (
                raw_out * lax.rsqrt(mean + norm_eps) * gain_ref[:, columns]
            ).astype(out_ref.dtype)


def attend(arrived, keys, values, states, tables, gain, start, filled):
    slots, columns = arrived.shape
    tok_rows, mine = keys.shape
    width = math.gcd(math.gcd(columns, start), 4 * HEAD_DIM)
    first = start // width
    column_spec = pl.BlockSpec((tok_rows, width), lambda j: (0, first + j))
    return pl.pallas_call(
        attend_kernel,
        out_shape=jax.ShapeDtypeStruct((tok_rows, mine), jnp.bfloat16),
        grid=(columns // width,),
        in_specs=[pl.BlockSpec(table.shape, lambda j: (0, 0)) for table in tables]
        + [
            pl.BlockSpec((1, width), lambda j: (0, first + j)),
            pl.BlockSpec((slots, width), lambda j: (0, j)),
            column_spec,
            column_spec,
            pl.BlockSpec((2 * width, HEAD_DIM), lambda j: (first + j, 0)),
        ]
        + [pl.BlockSpec(memory_space=pl.ANY) for _ in filled],
        out_specs=column_spec,
        input_output_aliases={8: 0} if filled else {},
        cost_estimate=pl.CostEstimate(
            flops=ATTEND_WEIGHT * tok_rows * columns * (slots + 2 * tok_rows + 4 * HEAD_DIM) // 5,
            bytes_accessed=2 * columns * (slots + 4 * tok_rows),
            transcendentals=0,
        ),
        name="attend",
    )(*tables, gain, arrived, keys, values, states, *filled)


def local_kernel(order_ref, causal_ref, carried_ref, arrived_ref, keys_ref, values_ref, *refs):
    query_out, local_out = refs[-2:]
    tok_rows = order_ref.shape[0]
    half = tok_rows // 2
    query = product(order_ref[...], arrived_ref[...]).astype(keys_ref.dtype)
    heads = query.shape[1] // HEAD_DIM
    together = math.gcd(heads, 2)
    for group in range(0, heads, together):
        tiles = []
        for part in range(group, group + together):
            columns = slice(part * HEAD_DIM, (part + 1) * HEAD_DIM)
            query_out[:, columns] = query[:, columns] * carried_ref[...]
            for rows, reach in ((slice(0, half), half), (slice(half, tok_rows), tok_rows)):
                scores = lax.dot_general(
                    query[rows, columns],
                    keys_ref[:reach, columns],
                    (((1,), (1,)), ((), ())),
                    preferred_element_type=jnp.float32,
                )
                weights = scores.astype(keys_ref.dtype) * causal_ref[rows, :reach]
                tiles.append((columns, rows, reach, weights))
        for columns, rows, reach, weights in tiles:
            local_out[rows, columns] = product(weights, values_ref[:reach, columns])


def attend_locally(arrived, keys, values, tables):
    slots, columns = arrived.shape
    tok_rows = keys.shape[0]
    width = math.gcd(columns, 4 * HEAD_DIM)
    column_spec = pl.BlockSpec((tok_rows, width), lambda j: (0, j))
    return pl.pallas_call(
        local_kernel,
        out_shape=tuple(
            jax.ShapeDtypeStruct((tok_rows, columns), dtype) for dtype in (jnp.bfloat16, jnp.float32)
        ),
        grid=(columns // width,),
        in_specs=[pl.BlockSpec(table.shape, lambda j: (0, 0)) for table in tables]
        + [pl.BlockSpec((slots, width), lambda j: (0, j)), column_spec, column_spec],
        out_specs=(column_spec, column_spec),
        cost_estimate=pl.CostEstimate(
            flops=ATTEND_WEIGHT * tok_rows * columns * (slots + 2 * tok_rows) // 5,
            bytes_accessed=2 * columns * (slots + 5 * tok_rows),
            transcendentals=0,
        ),
        name="attend_locally",
    )(*tables, arrived, keys, values)


def finish_kernel(gain_ref, query_ref, local_ref, states_ref, out_ref):
    ones = jnp.full((2 * HEAD_DIM, HEAD_DIM), 1.0, jnp.bfloat16)
    raws = []
    for part in range(out_ref.shape[1] // HEAD_DIM):
        columns = slice(part * HEAD_DIM, (part + 1) * HEAD_DIM)
        query = query_ref[:, columns]
        states = states_ref[2 * part * HEAD_DIM : 2 * (part + 1) * HEAD_DIM, :]
        carried_term = product(jnp.concatenate([query, query], axis=1), states)
        raws.append((columns, local_ref[:, columns] + carried_term))
    for columns, raw_out in raws:
        square = jnp.concatenate(two_terms(raw_out * raw_out), axis=1)
        mean = product(square, ones) * (1.0 / HEAD_DIM)
        out_ref[:, columns] = (raw_out * lax.rsqrt(mean + norm_eps) * gain_ref[:, columns]).astype(
            out_ref.dtype
        )


def finish(query, local_term, states, gain):
    tok_rows, columns = query.shape
    width = math.gcd(columns, 4 * HEAD_DIM)
    column_spec = pl.BlockSpec((tok_rows, width), lambda j: (0, j))
    return pl.pallas_call(
        finish_kernel,
        out_shape=jax.ShapeDtypeStruct((tok_rows, gain.shape[1]), jnp.bfloat16),
        grid=(columns // width,),
        in_specs=[
            pl.BlockSpec((1, width), lambda j: (0, j)),
            column_spec,
            column_spec,
            pl.BlockSpec((2 * width, HEAD_DIM), lambda j: (j, 0)),
        ],
        out_specs=column_spec,
        cost_estimate=pl.CostEstimate(
            flops=FINISH_WEIGHT * 8 * tok_rows * columns * HEAD_DIM,
            bytes_accessed=8 * columns * tok_rows,
            transcendentals=0,
        ),
        name="finish",
    )(gain, query, local_term, states)


def swap_heads(qkv, plane_start, planes, start, columns):
    head_count = lax.axis_size("head")
    rows = qkv.shape[1]
    mine = qkv.shape[2] // head_count
    part = lax.slice_in_dim(qkv, plane_start, plane_start + planes, axis=0)
    if head_count == 2:
        low = part[:, :, start : start + columns]
        high = part[:, :, mine + start : mine + start + columns]
        outgoing = jnp.where(lax.axis_index("head") == 0, high, low)
        return lax.ppermute(outgoing, "head", [(0, 1), (1, 0)])
    split = part.reshape(planes, rows, head_count, mine)[..., start : start + columns]
    incoming = lax.all_to_all(
        jnp.moveaxis(split, 2, 0), "head", split_axis=0, concat_axis=0, tiled=False
    )
    return jnp.moveaxis(incoming, 0, 1).reshape(planes, head_count * rows, columns)


def pack_chunk(qkv, incoming, send_rows, plane_start, planes, start, columns, offset=0):
    head_count = lax.axis_size("head")
    place = lax.axis_index("head")
    rows = qkv.shape[1]
    mine = qkv.shape[2] // head_count
    slots = send_rows.reshape(-1, 1)
    width = math.gcd(math.gcd(columns, start), math.gcd(mine, 512))
    picks, sources = (slots,), ((incoming, 0, lambda at, width: offset // width),)
    if head_count == 2:
        picks = (slots - place * rows, slots - (1 - place) * rows)
        sources = (
            (qkv, plane_start, lambda at, width: at * (mine // width) + start // width),
        ) + sources
    return pack_rows(
        jnp.reshape(place, (1,)).astype(jnp.int32), picks, sources, planes, columns, width
    )


def to_owners(outgoing):
    return lax.all_to_all(outgoing, "seq", split_axis=0, concat_axis=0, tiled=True)


def on_device(qkv, send_rows, recv_pos, req_lengths, norm_gain):
    seq_count, head_count = lax.axis_size("seq"), lax.axis_size("head")
    block = lax.axis_index("seq")
    tok_rows = qkv.shape[1] * head_count
    columns = qkv.shape[2] // head_count

    req_ends = jnp.cumsum(req_lengths)
    req_starts = req_ends - req_lengths
    first_row = block * tok_rows
    positions = first_row + jnp.arange(tok_rows, dtype=jnp.int32)
    segment = jnp.sum((req_starts[None, :] <= positions[:, None]).astype(jnp.int32), axis=1) - 1
    last_rows = (jnp.arange(seq_count, dtype=jnp.int32) + 1) * tok_rows - 1
    last_segment = jnp.sum((req_starts[None, :] <= last_rows[:, None]).astype(jnp.int32), axis=1) - 1
    prev_segment = jnp.sum((req_starts < first_row).astype(jnp.int32)) - 1
    carried_mask = (segment == prev_segment).astype(jnp.int32)[:, None]
    land_row = recv_pos[0].reshape(1, -1)
    landing = first_row + land_row.reshape(-1, 1)
    landing_segment = jnp.sum((req_starts[None, :] <= landing).astype(jnp.int32), axis=1, keepdims=True) - 1
    in_tail = (land_row.reshape(-1, 1) >= 0) & (landing_segment == last_segment[block])
    tail_slots = jnp.broadcast_to(in_tail.astype(jnp.bfloat16), (land_row.shape[1], HEAD_DIM))
    gain = norm_gain.reshape(1, -1)

    rows = send_rows[0]
    head_share = columns // HEAD_DIM
    first = max(2, head_share // 4) * HEAD_DIM
    second = columns - first
    outgoing = pack_chunk(qkv, swap_heads(qkv, KEYS, 2, 0, first), rows, KEYS, 2, 0, first)
    arrived = to_owners(outgoing)
    outgoing = pack_chunk(
        qkv, swap_heads(qkv, KEYS, 2, first, second), rows, KEYS, 2, first, second
    )
    arrived_next = to_owners(outgoing)
    within, across = carry_tables(last_segment)
    sums = carry_within(block_update(arrived, tail_slots), within)
    tables = block_tables(land_row, segment, carried_mask)
    filled = unpack_keys_values(arrived, tables[0], 0, columns, ())
    incoming = swap_heads(qkv, QUERY, 1, 0, columns)
    incoming, sums, filled, tables, small = lax.optimization_barrier(
        (incoming, sums, filled, tables, (tail_slots, within, across))
    )
    tail_slots, within, across = small
    part = max(2, head_share // 2) * HEAD_DIM
    outgoing, outgoing_next = (
        pack_chunk(qkv, incoming, rows, QUERY, 1, start, size, start)
        for start, size in ((0, part), (part, columns - part))
    )
    outgoing, outgoing_next, pieces = lax.optimization_barrier(
        (outgoing, outgoing_next, pass_totals(sums))
    )
    query = to_owners(outgoing)
    shares, pieces = lax.optimization_barrier((block_update(arrived_next, tail_slots), pieces))
    states = hand_back(pieces, across)
    sums = carry_within(shares, within)
    outgoing_next, sums, states, arrived_next = lax.optimization_barrier(
        (outgoing_next, sums, states, arrived_next)
    )
    pieces = pass_totals(sums)
    filled = unpack_keys_values(arrived_next, tables[0], first, columns, filled)
    query_next = to_owners(outgoing_next)
    states += hand_back(pieces, across)
    local = attend_locally(query, *filled, tables)
    states = assemble_states(states)
    out = finish(*local, states, gain)
    return attend(query_next, *filled, states, tables, gain, part, (out,))


def solution(mesh):
    return jax.shard_map(
        on_device,
        mesh=mesh,
        in_specs=(
            P(None, ("seq", "head"), None),
            P("seq", None, None),
            P("seq", None, None),
            P(),
            P("head"),
        ),
        out_specs=P("seq", "head"),
        check_vma=False,
    )
```

```python
import math

import jax
import jax.numpy as jnp
from jax import lax
from jax.experimental import pallas as pl
from jax.experimental.pallas import tpu as pltpu
from jax.sharding import PartitionSpec as P

HEAD_DIM = 128

norm_eps = 1e-06

QUERY, KEYS, VALUES = 0, 1, 2

PACK_WEIGHT = 20
FINISH_WEIGHT = 1
ATTEND_WEIGHT = 145


def pack_kernel(place_ref, *refs):
    count = (len(refs) - 1) // 3
    picks, sources = refs[:count], refs[count : 2 * count]
    out_ref, chosen = refs[2 * count], refs[2 * count + 1 :]

    @pl.when((pl.program_id(0) == 0) & (pl.program_id(1) == 0))
    def _():
        for pick, onehot in zip(picks, chosen):
            rows = lax.broadcasted_iota(jnp.int32, onehot.shape, 1)
            onehot[...] = jnp.where(pick[...] == rows, 1.0, 0.0).astype(onehot.dtype)

    total = None
    for source, onehot in zip(sources, chosen):
        part = jnp.dot(onehot[...], source[0], preferred_element_type=jnp.float32)
        total = part if total is None else total + part
    out_ref[...] = total.astype(out_ref.dtype)


def pack_rows(place, picks, sources, planes, columns, width):
    slots = picks[0].shape[0]
    blocks = columns // width
    lens = [array.shape[1] for array, _, _ in sources]

    def source_spec(array, plane_start, first):
        return pl.BlockSpec(
            (1, array.shape[1], width),
            lambda p, j, place_ref: (plane_start + p, 0, first(place_ref[0], width) + j),
        )

    return pl.pallas_call(
        pack_kernel,
        out_shape=jax.ShapeDtypeStruct((slots, planes * columns), jnp.bfloat16),
        grid_spec=pltpu.PrefetchScalarGridSpec(
            num_scalar_prefetch=1,
            grid=(planes, blocks),
            in_specs=[pl.BlockSpec((slots, 1), lambda p, j, place_ref: (0, 0)) for _ in picks]
            + [source_spec(*source) for source in sources],
            out_specs=pl.BlockSpec((slots, width), lambda p, j, place_ref: (0, p * blocks + j)),
            scratch_shapes=[pltpu.VMEM((slots, length), jnp.bfloat16) for length in lens],
        ),
        cost_estimate=pl.CostEstimate(
            flops=PACK_WEIGHT * 2 * slots * sum(lens) * planes * columns,
            bytes_accessed=2 * planes * columns * (slots + sum(lens)),
            transcendentals=0,
        ),
        name="pack_rows",
    )(place, *picks, *[array for array, _, _ in sources])


def update_kernel(place_ref, tail_ref, keys_ref, values_ref, *outs):
    for number, out in enumerate(outs):

        @pl.when(pl.program_id(0) == number)
        def _():
            for part in range(keys_ref.shape[1] // HEAD_DIM):
                columns = slice(part * HEAD_DIM, (part + 1) * HEAD_DIM)
                out[columns, :] = lax.dot_general(
                    keys_ref[:, columns] * tail_ref[...],
                    values_ref[:, columns],
                    (((0,), (0,)), ((), ())),
                    preferred_element_type=jnp.float32,
                )


def block_update(arrived, tail_slots):
    near, _, place, _ = run_of_blocks()
    slots, columns = arrived.shape[0], arrived.shape[1] // 2
    share = columns // near
    direct = share % HEAD_DIM == 0
    width, blocks = (share, near) if direct else (columns, 1)

    def column_spec(first):
        return pl.BlockSpec((slots, width), lambda j, place_ref: (0, first + (j ^ place_ref[0])))

    updates = pl.pallas_call(
        update_kernel,
        out_shape=(jax.ShapeDtypeStruct((width, HEAD_DIM), jnp.float32),) * blocks,
        grid_spec=pltpu.PrefetchScalarGridSpec(
            num_scalar_prefetch=1,
            grid=(blocks,),
            in_specs=[
                pl.BlockSpec((slots, HEAD_DIM), lambda j, place_ref: (0, 0)),
                column_spec(0),
                column_spec(blocks),
            ],
            out_specs=(pl.BlockSpec((width, HEAD_DIM), lambda j, place_ref: (0, 0)),) * blocks,
        ),
        cost_estimate=pl.CostEstimate(
            flops=2 * slots * columns * HEAD_DIM,
            bytes_accessed=4 * columns * (slots + HEAD_DIM),
            transcendentals=0,
        ),
        name="block_update",
    )(jnp.reshape(place if direct else 0 * place, (1,)), tail_slots, arrived, arrived)
    if direct:
        return list(updates)
    return [
        lax.dynamic_slice_in_dim(updates[0], (place ^ k) * share, share, axis=0)
        for k in range(near)
    ]


def tables_kernel(land_ref, seg_col_ref, seg_row_ref, mask_ref, order, causal, carried):
    rows = lax.broadcasted_iota(jnp.int32, order.shape, 0)
    order[...] = jnp.where(land_ref[...] == rows, 1.0, 0.0).astype(order.dtype)
    later = lax.broadcasted_iota(jnp.int32, causal.shape, 0)
    earlier = lax.broadcasted_iota(jnp.int32, causal.shape, 1)
    open_pair = (earlier <= later) & (seg_col_ref[...] == seg_row_ref[...])
    causal[...] = jnp.where(open_pair, 1.0, 0.0).astype(causal.dtype)
    carried[...] = jnp.broadcast_to(
        jnp.where(mask_ref[...] != 0, 1.0, 0.0).astype(carried.dtype), carried.shape
    )


def block_tables(land_row, segment, carried_mask):
    slots, tok_rows = land_row.shape[1], segment.shape[0]
    return pl.pallas_call(
        tables_kernel,
        out_shape=tuple(
            jax.ShapeDtypeStruct((tok_rows, n), jnp.bfloat16) for n in (slots, tok_rows, HEAD_DIM)
        ),
        cost_estimate=pl.CostEstimate(
            flops=8 * tok_rows * (slots + tok_rows),
            bytes_accessed=2 * tok_rows * (slots + tok_rows),
            transcendentals=0,
        ),
        name="block_tables",
    )(land_row, segment[:, None], segment[None, :], carried_mask)


def unpack_kernel(order_ref, keys_ref, values_ref, *refs):
    for source, out in zip((keys_ref, values_ref), refs[-2:]):
        out[...] = jnp.dot(
            order_ref[...], source[...], preferred_element_type=jnp.float32
        ).astype(out.dtype)


def unpack_keys_values(arrived, order, start, mine, filled):
    slots, columns = arrived.shape[0], arrived.shape[1] // 2
    tok_rows = order.shape[0]
    width = math.gcd(math.gcd(columns, start), 4 * HEAD_DIM)
    blocks, first = columns // width, start // width
    packed = jax.ShapeDtypeStruct((tok_rows, mine), arrived.dtype)
    column_spec = pl.BlockSpec((tok_rows, width), lambda j: (0, first + j))
    return pl.pallas_call(
        unpack_kernel,
        out_shape=(packed, packed),
        grid=(blocks,),
        in_specs=[
            pl.BlockSpec((tok_rows, slots), lambda j: (0, 0)),
            pl.BlockSpec((slots, width), lambda j: (0, j)),
            pl.BlockSpec((slots, width), lambda j: (0, blocks + j)),
        ]
        + [pl.BlockSpec(memory_space=pl.ANY) for _ in filled],
        out_specs=(column_spec, column_spec),
        input_output_aliases={3 + number: number for number in range(len(filled))},
        cost_estimate=pl.CostEstimate(
            flops=4 * tok_rows * columns * slots,
            bytes_accessed=4 * columns * (slots + tok_rows),
            transcendentals=0,
        ),
        name="unpack_keys_values",
    )(order, arrived, arrived, *filled)


def sum_kernel(take_ref, *refs):
    count = take_ref.shape[1]
    pieces, outs = refs[:count], refs[count:]
    for number, out in enumerate(outs):
        total = jnp.zeros(out.shape, jnp.float32)
        for piece in range(count):
            value = pieces[piece][...].astype(jnp.float32)
            total = total + jnp.where(take_ref[number, piece] != 0, value, 0.0)
        out[...] = total.astype(out.dtype)


def sum_pieces(take, pieces, last=jnp.float32):
    rows = pieces[0].shape[0]
    count = take.shape[0]
    whole = pl.BlockSpec(memory_space=pltpu.VMEM)
    return pl.pallas_call(
        sum_kernel,
        out_shape=(jax.ShapeDtypeStruct((rows, HEAD_DIM), jnp.float32),) * (count - 1)
        + (jax.ShapeDtypeStruct((rows, HEAD_DIM), last),),
        in_specs=[pl.BlockSpec(memory_space=pltpu.SMEM)] + [whole] * len(pieces),
        out_specs=(whole,) * count,
        cost_estimate=pl.CostEstimate(
            flops=count * len(pieces) * rows * HEAD_DIM,
            bytes_accessed=4 * (len(pieces) + count) * rows * HEAD_DIM,
            transcendentals=0,
        ),
        name="sum_pieces",
    )(take.astype(jnp.int32), *pieces)


def run_of_blocks():
    seq_count, block = lax.axis_size("seq"), lax.axis_index("seq")
    near = run_size()
    return near, seq_count // near, block % near, block // near


def swap_places(value, k):
    seq_count = lax.axis_size("seq")
    return lax.ppermute(value, "seq", [(i, i ^ k) for i in range(seq_count)])


def carry_tables(last_segment):
    near, far, place, run = run_of_blocks()
    base = run * near
    source = base + (place ^ jnp.arange(near))
    before = last_segment[jnp.maximum(source - 1, 0)]
    of_source = last_segment[source]
    inside = (source[None, :] < source[:, None]) & (of_source[None, :] == before[:, None])
    whole = of_source == last_segment[base + near - 1]
    within = jnp.concatenate([inside, whole[None]])
    shifts = jnp.arange(1, far // 2 + 1)
    ends = last_segment[jnp.maximum(run - shifts, 0) * near + near - 1]
    across = (run >= shifts)[None, :] & (ends[None, :] == before[:, None])
    own = jnp.arange(near)[:, None] == jnp.arange(near)[None, :]
    return within, jnp.concatenate([own, across], axis=1)


def carry_within(shares, within, total_type):
    pieces = [shares[0]] + [swap_places(shares[k], k) for k in range(1, len(shares))]
    return sum_pieces(within, pieces, total_type)


def pass_totals(sums):
    seq_count = lax.axis_size("seq")
    near, far, _, _ = run_of_blocks()
    pieces = list(sums[:near])
    for shift in range(1, far // 2 + 1):
        step = shift * near
        pieces.append(
            lax.ppermute(sums[near], "seq", [(i, i + step) for i in range(seq_count - step)])
        )
    return pieces


def hand_back(pieces, across):
    handed = sum_pieces(across, pieces)
    return [handed[0]] + [swap_places(handed[k], k) for k in range(1, len(handed))]


def two_terms(value):
    high = value.astype(jnp.bfloat16)
    return high, (value - high.astype(jnp.float32)).astype(jnp.bfloat16)


def assemble_kernel(place_ref, *refs):
    pieces, out = refs[:-1], refs[-1]
    near = run_size()
    number = 0
    for chunk in range(0, len(pieces), near):
        share = pieces[chunk].shape[0]
        step = math.gcd(share, HEAD_DIM)
        for place in range(near):
            for row in range(0, share, step):
                value = pieces[chunk + place][row : row + step, :]
                for other in range(1, near):
                    piece = pieces[chunk + (place ^ other)]
                    value = jnp.where(place_ref[0] == other, piece[row : row + step, :], value)
                head, within = divmod(number, HEAD_DIM)
                for term, part in enumerate(two_terms(value)):
                    first = (2 * head + term) * HEAD_DIM + within
                    out[first : first + step, :] = part
                number += step


def run_size():
    return math.gcd(lax.axis_size("seq"), 4)


def assemble_states(pieces):
    _, _, place, _ = run_of_blocks()
    rows = sum(piece.shape[0] for piece in pieces)
    whole = pl.BlockSpec(memory_space=pltpu.VMEM)
    return pl.pallas_call(
        assemble_kernel,
        out_shape=jax.ShapeDtypeStruct((2 * rows, HEAD_DIM), jnp.bfloat16),
        in_specs=[pl.BlockSpec(memory_space=pltpu.SMEM)] + [whole] * len(pieces),
        out_specs=whole,
        cost_estimate=pl.CostEstimate(
            flops=8 * rows * HEAD_DIM, bytes_accessed=8 * rows * HEAD_DIM, transcendentals=0
        ),
        name="assemble_states",
    )(jnp.reshape(place, (1,)), *pieces)


def product(left, right):
    return jnp.dot(left, right, preferred_element_type=jnp.float32)


def attend_kernel(
    order_ref, causal_ref, carried_ref, gain_ref, arrived_ref, keys_ref, values_ref, states_ref, *refs
):
    out_ref = refs[-1]
    tok_rows = order_ref.shape[0]
    half = tok_rows // 2

    ones = jnp.full((2 * HEAD_DIM, HEAD_DIM), 1.0, jnp.bfloat16)
    query = product(order_ref[...], arrived_ref[...]).astype(keys_ref.dtype)
    heads = query.shape[1] // HEAD_DIM
    together = math.gcd(heads, 2)
    for group in range(0, heads, together):
        tiles = []
        for part in range(group, group + together):
            columns = slice(part * HEAD_DIM, (part + 1) * HEAD_DIM)
            for rows, reach in ((slice(0, half), half), (slice(half, tok_rows), tok_rows)):
                scores = lax.dot_general(
                    query[rows, columns],
                    keys_ref[:reach, columns],
                    (((1,), (1,)), ((), ())),
                    preferred_element_type=jnp.float32,
                )
                weights = scores.astype(keys_ref.dtype) * causal_ref[rows, :reach]
                tiles.append((part, columns, rows, reach, weights))
        raws = []
        for part, columns, rows, reach, weights in tiles:
            carrying = query[rows, columns] * carried_ref[rows, :]
            states = states_ref[2 * part * HEAD_DIM : 2 * (part + 1) * HEAD_DIM, :]
            raws.append(
                product(
                    jnp.concatenate([weights, carrying, carrying], axis=1),
                    jnp.concatenate([values_ref[:reach, columns], states], axis=0),
                )
            )
        for (part, columns, rows, reach, weights), raw_out in zip(tiles, raws):
            square = jnp.concatenate(two_terms(raw_out * raw_out), axis=1)
            mean = product(square, ones) * (1.0 / HEAD_DIM)
            out_ref[rows, columns] = (
                raw_out * lax.rsqrt(mean + norm_eps) * gain_ref[:, columns]
            ).astype(out_ref.dtype)


def attend(arrived, keys, values, states, tables, gain, start, filled):
    slots, columns = arrived.shape
    tok_rows, mine = keys.shape
    width = math.gcd(math.gcd(columns, start), 4 * HEAD_DIM)
    first = start // width
    column_spec = pl.BlockSpec((tok_rows, width), lambda j: (0, first + j))
    return pl.pallas_call(
        attend_kernel,
        out_shape=jax.ShapeDtypeStruct((tok_rows, mine), jnp.bfloat16),
        grid=(columns // width,),
        in_specs=[pl.BlockSpec(table.shape, lambda j: (0, 0)) for table in tables]
        + [
            pl.BlockSpec((1, width), lambda j: (0, first + j)),
            pl.BlockSpec((slots, width), lambda j: (0, j)),
            column_spec,
            column_spec,
            pl.BlockSpec((2 * width, HEAD_DIM), lambda j: (first + j, 0)),
        ]
        + [pl.BlockSpec(memory_space=pl.ANY) for _ in filled],
        out_specs=column_spec,
        input_output_aliases={8: 0} if filled else {},
        cost_estimate=pl.CostEstimate(
            flops=ATTEND_WEIGHT * tok_rows * columns * (slots + 2 * tok_rows + 4 * HEAD_DIM) // 5,
            bytes_accessed=2 * columns * (slots + 4 * tok_rows),
            transcendentals=0,
        ),
        name="attend",
    )(*tables, gain, arrived, keys, values, states, *filled)


def local_kernel(order_ref, causal_ref, carried_ref, arrived_ref, keys_ref, values_ref, *refs):
    query_out, local_out = refs[-2:]
    tok_rows = order_ref.shape[0]
    half = tok_rows // 2
    query = product(order_ref[...], arrived_ref[...]).astype(keys_ref.dtype)
    heads = query.shape[1] // HEAD_DIM
    together = math.gcd(heads, 2)
    for group in range(0, heads, together):
        tiles = []
        for part in range(group, group + together):
            columns = slice(part * HEAD_DIM, (part + 1) * HEAD_DIM)
            query_out[:, columns] = query[:, columns] * carried_ref[...]
            for rows, reach in ((slice(0, half), half), (slice(half, tok_rows), tok_rows)):
                scores = lax.dot_general(
                    query[rows, columns],
                    keys_ref[:reach, columns],
                    (((1,), (1,)), ((), ())),
                    preferred_element_type=jnp.float32,
                )
                weights = scores.astype(keys_ref.dtype) * causal_ref[rows, :reach]
                tiles.append((columns, rows, reach, weights))
        for columns, rows, reach, weights in tiles:
            local_out[rows, columns] = product(weights, values_ref[:reach, columns])


def attend_locally(arrived, keys, values, tables):
    slots, columns = arrived.shape
    tok_rows = keys.shape[0]
    width = math.gcd(columns, 4 * HEAD_DIM)
    column_spec = pl.BlockSpec((tok_rows, width), lambda j: (0, j))
    return pl.pallas_call(
        local_kernel,
        out_shape=tuple(
            jax.ShapeDtypeStruct((tok_rows, columns), dtype) for dtype in (jnp.bfloat16, jnp.float32)
        ),
        grid=(columns // width,),
        in_specs=[pl.BlockSpec(table.shape, lambda j: (0, 0)) for table in tables]
        + [pl.BlockSpec((slots, width), lambda j: (0, j)), column_spec, column_spec],
        out_specs=(column_spec, column_spec),
        cost_estimate=pl.CostEstimate(
            flops=ATTEND_WEIGHT * tok_rows * columns * (slots + 2 * tok_rows) // 5,
            bytes_accessed=2 * columns * (slots + 5 * tok_rows),
            transcendentals=0,
        ),
        name="attend_locally",
    )(*tables, arrived, keys, values)


def finish_kernel(gain_ref, query_ref, local_ref, states_ref, out_ref):
    ones = jnp.full((2 * HEAD_DIM, HEAD_DIM), 1.0, jnp.bfloat16)
    raws = []
    for part in range(out_ref.shape[1] // HEAD_DIM):
        columns = slice(part * HEAD_DIM, (part + 1) * HEAD_DIM)
        query = query_ref[:, columns]
        states = states_ref[2 * part * HEAD_DIM : 2 * (part + 1) * HEAD_DIM, :]
        carried_term = product(jnp.concatenate([query, query], axis=1), states)
        raws.append((columns, local_ref[:, columns] + carried_term))
    for columns, raw_out in raws:
        square = jnp.concatenate(two_terms(raw_out * raw_out), axis=1)
        mean = product(square, ones) * (1.0 / HEAD_DIM)
        out_ref[:, columns] = (raw_out * lax.rsqrt(mean + norm_eps) * gain_ref[:, columns]).astype(
            out_ref.dtype
        )


def finish(query, local_term, states, gain):
    tok_rows, columns = query.shape
    width = math.gcd(columns, 4 * HEAD_DIM)
    column_spec = pl.BlockSpec((tok_rows, width), lambda j: (0, j))
    return pl.pallas_call(
        finish_kernel,
        out_shape=jax.ShapeDtypeStruct((tok_rows, gain.shape[1]), jnp.bfloat16),
        grid=(columns // width,),
        in_specs=[
            pl.BlockSpec((1, width), lambda j: (0, j)),
            column_spec,
            column_spec,
            pl.BlockSpec((2 * width, HEAD_DIM), lambda j: (j, 0)),
        ],
        out_specs=column_spec,
        cost_estimate=pl.CostEstimate(
            flops=FINISH_WEIGHT * 8 * tok_rows * columns * HEAD_DIM,
            bytes_accessed=8 * columns * tok_rows,
            transcendentals=0,
        ),
        name="finish",
    )(gain, query, local_term, states)


def swap_heads(qkv, plane_start, planes, start, columns):
    head_count = lax.axis_size("head")
    rows = qkv.shape[1]
    mine = qkv.shape[2] // head_count
    part = lax.slice_in_dim(qkv, plane_start, plane_start + planes, axis=0)
    if head_count == 2:
        low = part[:, :, start : start + columns]
        high = part[:, :, mine + start : mine + start + columns]
        outgoing = jnp.where(lax.axis_index("head") == 0, high, low)
        return lax.ppermute(outgoing, "head", [(0, 1), (1, 0)])
    split = part.reshape(planes, rows, head_count, mine)[..., start : start + columns]
    incoming = lax.all_to_all(
        jnp.moveaxis(split, 2, 0), "head", split_axis=0, concat_axis=0, tiled=False
    )
    return jnp.moveaxis(incoming, 0, 1).reshape(planes, head_count * rows, columns)


def pack_chunk(qkv, incoming, send_rows, plane_start, planes, start, columns, offset=0):
    head_count = lax.axis_size("head")
    place = lax.axis_index("head")
    rows = qkv.shape[1]
    mine = qkv.shape[2] // head_count
    slots = send_rows.reshape(-1, 1)
    width = math.gcd(math.gcd(columns, start), math.gcd(mine, 512))
    picks, sources = (slots,), ((incoming, 0, lambda at, width: offset // width),)
    if head_count == 2:
        picks = (slots - place * rows, slots - (1 - place) * rows)
        sources = (
            (qkv, plane_start, lambda at, width: at * (mine // width) + start // width),
        ) + sources
    return pack_rows(
        jnp.reshape(place, (1,)).astype(jnp.int32), picks, sources, planes, columns, width
    )


def to_owners(outgoing):
    return lax.all_to_all(outgoing, "seq", split_axis=0, concat_axis=0, tiled=True)


def on_device(qkv, send_rows, recv_pos, req_lengths, norm_gain):
    seq_count, head_count = lax.axis_size("seq"), lax.axis_size("head")
    block = lax.axis_index("seq")
    tok_rows = qkv.shape[1] * head_count
    columns = qkv.shape[2] // head_count

    req_ends = jnp.cumsum(req_lengths)
    req_starts = req_ends - req_lengths
    first_row = block * tok_rows
    positions = first_row + jnp.arange(tok_rows, dtype=jnp.int32)
    segment = jnp.sum((req_starts[None, :] <= positions[:, None]).astype(jnp.int32), axis=1) - 1
    last_rows = (jnp.arange(seq_count, dtype=jnp.int32) + 1) * tok_rows - 1
    last_segment = jnp.sum((req_starts[None, :] <= last_rows[:, None]).astype(jnp.int32), axis=1) - 1
    prev_segment = jnp.sum((req_starts < first_row).astype(jnp.int32)) - 1
    carried_mask = (segment == prev_segment).astype(jnp.int32)[:, None]
    land_row = recv_pos[0].reshape(1, -1)
    landing = first_row + land_row.reshape(-1, 1)
    landing_segment = jnp.sum((req_starts[None, :] <= landing).astype(jnp.int32), axis=1, keepdims=True) - 1
    in_tail = (land_row.reshape(-1, 1) >= 0) & (landing_segment == last_segment[block])
    tail_slots = jnp.broadcast_to(in_tail.astype(jnp.bfloat16), (land_row.shape[1], HEAD_DIM))
    gain = norm_gain.reshape(1, -1)

    rows = send_rows[0]
    head_share = columns // HEAD_DIM
    first = max(2, head_share // 4) * HEAD_DIM
    second = columns - first
    outgoing = pack_chunk(qkv, swap_heads(qkv, KEYS, 2, 0, first), rows, KEYS, 2, 0, first)
    arrived = to_owners(outgoing)
    outgoing = pack_chunk(
        qkv, swap_heads(qkv, KEYS, 2, first, second), rows, KEYS, 2, first, second
    )
    arrived_next = to_owners(outgoing)
    within, across = carry_tables(last_segment)
    sums = carry_within(block_update(arrived, tail_slots), within, jnp.float32)
    tables = block_tables(land_row, segment, carried_mask)
    filled = unpack_keys_values(arrived, tables[0], 0, columns, ())
    incoming = swap_heads(qkv, QUERY, 1, 0, columns)
    incoming, sums, filled, tables, small = lax.optimization_barrier(
        (incoming, sums, filled, tables, (tail_slots, within, across))
    )
    tail_slots, within, across = small
    part = max(2, head_share // 2) * HEAD_DIM
    outgoing, outgoing_next = (
        pack_chunk(qkv, incoming, rows, QUERY, 1, start, size, start)
        for start, size in ((0, part), (part, columns - part))
    )
    outgoing, outgoing_next, pieces = lax.optimization_barrier(
        (outgoing, outgoing_next, pass_totals(sums))
    )
    query = to_owners(outgoing)
    shares, pieces = lax.optimization_barrier((block_update(arrived_next, tail_slots), pieces))
    states = hand_back(pieces, across)
    sums = carry_within(shares, within, jnp.bfloat16)
    outgoing_next, sums, states, arrived_next = lax.optimization_barrier(
        (outgoing_next, sums, states, arrived_next)
    )
    pieces = pass_totals(sums)
    filled = unpack_keys_values(arrived_next, tables[0], first, columns, filled)
    query_next = to_owners(outgoing_next)
    states += hand_back(pieces, across)
    local = attend_locally(query, *filled, tables)
    states = assemble_states(states)
    out = finish(*local, states, gain)
    return attend(query_next, *filled, states, tables, gain, part, (out,))


def solution(mesh):
    return jax.shard_map(
        on_device,
        mesh=mesh,
        in_specs=(
            P(None, ("seq", "head"), None),
            P("seq", None, None),
            P("seq", None, None),
            P(),
            P("head"),
        ),
        out_specs=P("seq", "head"),
        check_vma=False,
    )
```

```python
import math

import jax
import jax.numpy as jnp
from jax import lax
from jax.experimental import pallas as pl
from jax.experimental.pallas import tpu as pltpu
from jax.sharding import PartitionSpec as P

HEAD_DIM = 128

norm_eps = 1e-06

QUERY, KEYS, VALUES = 0, 1, 2

PACK_WEIGHT = 20
FINISH_WEIGHT = 1
ATTEND_WEIGHT = 145


def pack_kernel(place_ref, *refs):
    count = (len(refs) - 1) // 3
    picks, sources = refs[:count], refs[count : 2 * count]
    out_ref, chosen = refs[2 * count], refs[2 * count + 1 :]

    @pl.when((pl.program_id(0) == 0) & (pl.program_id(1) == 0))
    def _():
        for pick, onehot in zip(picks, chosen):
            rows = lax.broadcasted_iota(jnp.int32, onehot.shape, 1)
            onehot[...] = jnp.where(pick[...] == rows, 1.0, 0.0).astype(onehot.dtype)

    total = None
    for source, onehot in zip(sources, chosen):
        part = jnp.dot(onehot[...], source[0], preferred_element_type=jnp.float32)
        total = part if total is None else total + part
    out_ref[...] = total.astype(out_ref.dtype)


def pack_rows(place, picks, sources, planes, columns, width):
    slots = picks[0].shape[0]
    blocks = columns // width
    lens = [array.shape[1] for array, _, _ in sources]

    def source_spec(array, plane_start, first):
        return pl.BlockSpec(
            (1, array.shape[1], width),
            lambda p, j, place_ref: (plane_start + p, 0, first(place_ref[0], width) + j),
        )

    return pl.pallas_call(
        pack_kernel,
        out_shape=jax.ShapeDtypeStruct((slots, planes * columns), jnp.bfloat16),
        grid_spec=pltpu.PrefetchScalarGridSpec(
            num_scalar_prefetch=1,
            grid=(planes, blocks),
            in_specs=[pl.BlockSpec((slots, 1), lambda p, j, place_ref: (0, 0)) for _ in picks]
            + [source_spec(*source) for source in sources],
            out_specs=pl.BlockSpec((slots, width), lambda p, j, place_ref: (0, p * blocks + j)),
            scratch_shapes=[pltpu.VMEM((slots, length), jnp.bfloat16) for length in lens],
        ),
        cost_estimate=pl.CostEstimate(
            flops=PACK_WEIGHT * 2 * slots * sum(lens) * planes * columns,
            bytes_accessed=2 * planes * columns * (slots + sum(lens)),
            transcendentals=0,
        ),
        name="pack_rows",
    )(place, *picks, *[array for array, _, _ in sources])


def update_kernel(place_ref, tail_ref, keys_ref, values_ref, *outs):
    for number, out in enumerate(outs):

        @pl.when(pl.program_id(0) == number)
        def _():
            for part in range(keys_ref.shape[1] // HEAD_DIM):
                columns = slice(part * HEAD_DIM, (part + 1) * HEAD_DIM)
                out[columns, :] = lax.dot_general(
                    keys_ref[:, columns] * tail_ref[...],
                    values_ref[:, columns],
                    (((0,), (0,)), ((), ())),
                    preferred_element_type=jnp.float32,
                )


def block_update(arrived, tail_slots):
    near, _, place, _ = run_of_blocks()
    slots, columns = arrived.shape[0], arrived.shape[1] // 2
    share = columns // near
    direct = share % HEAD_DIM == 0
    width, blocks = (share, near) if direct else (columns, 1)

    def column_spec(first):
        return pl.BlockSpec((slots, width), lambda j, place_ref: (0, first + (j ^ place_ref[0])))

    updates = pl.pallas_call(
        update_kernel,
        out_shape=(jax.ShapeDtypeStruct((width, HEAD_DIM), jnp.float32),) * blocks,
        grid_spec=pltpu.PrefetchScalarGridSpec(
            num_scalar_prefetch=1,
            grid=(blocks,),
            in_specs=[
                pl.BlockSpec((slots, HEAD_DIM), lambda j, place_ref: (0, 0)),
                column_spec(0),
                column_spec(blocks),
            ],
            out_specs=(pl.BlockSpec((width, HEAD_DIM), lambda j, place_ref: (0, 0)),) * blocks,
        ),
        cost_estimate=pl.CostEstimate(
            flops=2 * slots * columns * HEAD_DIM,
            bytes_accessed=4 * columns * (slots + HEAD_DIM),
            transcendentals=0,
        ),
        name="block_update",
    )(jnp.reshape(place if direct else 0 * place, (1,)), tail_slots, arrived, arrived)
    if direct:
        return list(updates)
    return [
        lax.dynamic_slice_in_dim(updates[0], (place ^ k) * share, share, axis=0)
        for k in range(near)
    ]


def tables_kernel(land_ref, seg_col_ref, seg_row_ref, mask_ref, order, causal, carried):
    rows = lax.broadcasted_iota(jnp.int32, order.shape, 0)
    order[...] = jnp.where(land_ref[...] == rows, 1.0, 0.0).astype(order.dtype)
    later = lax.broadcasted_iota(jnp.int32, causal.shape, 0)
    earlier = lax.broadcasted_iota(jnp.int32, causal.shape, 1)
    open_pair = (earlier <= later) & (seg_col_ref[...] == seg_row_ref[...])
    causal[...] = jnp.where(open_pair, 1.0, 0.0).astype(causal.dtype)
    carried[...] = jnp.broadcast_to(
        jnp.where(mask_ref[...] != 0, 1.0, 0.0).astype(carried.dtype), carried.shape
    )


def block_tables(land_row, segment, carried_mask):
    slots, tok_rows = land_row.shape[1], segment.shape[0]
    return pl.pallas_call(
        tables_kernel,
        out_shape=tuple(
            jax.ShapeDtypeStruct((tok_rows, n), jnp.bfloat16) for n in (slots, tok_rows, HEAD_DIM)
        ),
        cost_estimate=pl.CostEstimate(
            flops=8 * tok_rows * (slots + tok_rows),
            bytes_accessed=2 * tok_rows * (slots + tok_rows),
            transcendentals=0,
        ),
        name="block_tables",
    )(land_row, segment[:, None], segment[None, :], carried_mask)


def unpack_kernel(order_ref, keys_ref, values_ref, *refs):
    for source, out in zip((keys_ref, values_ref), refs[-2:]):
        out[...] = jnp.dot(
            order_ref[...], source[...], preferred_element_type=jnp.float32
        ).astype(out.dtype)


def unpack_keys_values(arrived, order, start, mine, filled):
    slots, columns = arrived.shape[0], arrived.shape[1] // 2
    tok_rows = order.shape[0]
    width = math.gcd(math.gcd(columns, start), 4 * HEAD_DIM)
    blocks, first = columns // width, start // width
    packed = jax.ShapeDtypeStruct((tok_rows, mine), arrived.dtype)
    column_spec = pl.BlockSpec((tok_rows, width), lambda j: (0, first + j))
    return pl.pallas_call(
        unpack_kernel,
        out_shape=(packed, packed),
        grid=(blocks,),
        in_specs=[
            pl.BlockSpec((tok_rows, slots), lambda j: (0, 0)),
            pl.BlockSpec((slots, width), lambda j: (0, j)),
            pl.BlockSpec((slots, width), lambda j: (0, blocks + j)),
        ]
        + [pl.BlockSpec(memory_space=pl.ANY) for _ in filled],
        out_specs=(column_spec, column_spec),
        input_output_aliases={3 + number: number for number in range(len(filled))},
        cost_estimate=pl.CostEstimate(
            flops=4 * tok_rows * columns * slots,
            bytes_accessed=4 * columns * (slots + tok_rows),
            transcendentals=0,
        ),
        name="unpack_keys_values",
    )(order, arrived, arrived, *filled)


def sum_kernel(take_ref, *refs):
    count = take_ref.shape[1]
    pieces, outs = refs[:count], refs[count:]
    for number, out in enumerate(outs):
        total = jnp.zeros(out.shape, jnp.float32)
        for piece in range(count):
            value = pieces[piece][...].astype(jnp.float32)
            total = total + jnp.where(take_ref[number, piece] != 0, value, 0.0)
        out[...] = total.astype(out.dtype)


def sum_pieces(take, pieces, last=jnp.float32):
    rows = pieces[0].shape[0]
    count = take.shape[0]
    whole = pl.BlockSpec(memory_space=pltpu.VMEM)
    return pl.pallas_call(
        sum_kernel,
        out_shape=(jax.ShapeDtypeStruct((rows, HEAD_DIM), jnp.float32),) * (count - 1)
        + (jax.ShapeDtypeStruct((rows, HEAD_DIM), last),),
        in_specs=[pl.BlockSpec(memory_space=pltpu.SMEM)] + [whole] * len(pieces),
        out_specs=(whole,) * count,
        cost_estimate=pl.CostEstimate(
            flops=count * len(pieces) * rows * HEAD_DIM,
            bytes_accessed=4 * (len(pieces) + count) * rows * HEAD_DIM,
            transcendentals=0,
        ),
        name="sum_pieces",
    )(take.astype(jnp.int32), *pieces)


def run_of_blocks():
    seq_count, block = lax.axis_size("seq"), lax.axis_index("seq")
    near = run_size()
    return near, seq_count // near, block % near, block // near


def swap_places(value, k):
    seq_count = lax.axis_size("seq")
    return lax.ppermute(value, "seq", [(i, i ^ k) for i in range(seq_count)])


def carry_tables(last_segment):
    near, far, place, run = run_of_blocks()
    base = run * near
    source = base + (place ^ jnp.arange(near))
    before = last_segment[jnp.maximum(source - 1, 0)]
    of_source = last_segment[source]
    inside = (source[None, :] < source[:, None]) & (of_source[None, :] == before[:, None])
    whole = of_source == last_segment[base + near - 1]
    within = jnp.concatenate([inside, whole[None]])
    shifts = jnp.arange(1, far // 2 + 1)
    ends = last_segment[jnp.maximum(run - shifts, 0) * near + near - 1]
    across = (run >= shifts)[None, :] & (ends[None, :] == before[:, None])
    own = jnp.arange(near)[:, None] == jnp.arange(near)[None, :]
    return within, jnp.concatenate([own, across], axis=1)


def carry_within(shares, within, total_type):
    pieces = [shares[0]] + [swap_places(shares[k], k) for k in range(1, len(shares))]
    return sum_pieces(within, pieces, total_type)


def pass_totals(sums):
    seq_count = lax.axis_size("seq")
    near, far, _, _ = run_of_blocks()
    pieces = list(sums[:near])
    for shift in range(1, far // 2 + 1):
        step = shift * near
        pieces.append(
            lax.ppermute(sums[near], "seq", [(i, i + step) for i in range(seq_count - step)])
        )
    return pieces


def hand_back(pieces, across):
    handed = sum_pieces(across, pieces)
    return [handed[0]] + [swap_places(handed[k], k) for k in range(1, len(handed))]


def two_terms(value):
    high = value.astype(jnp.bfloat16)
    return high, (value - high.astype(jnp.float32)).astype(jnp.bfloat16)


def assemble_kernel(place_ref, *refs):
    pieces, out = refs[:-1], refs[-1]
    near = run_size()
    number = 0
    for chunk in range(0, len(pieces), near):
        share = pieces[chunk].shape[0]
        step = math.gcd(share, HEAD_DIM)
        for place in range(near):
            for row in range(0, share, step):
                value = pieces[chunk + place][row : row + step, :]
                for other in range(1, near):
                    piece = pieces[chunk + (place ^ other)]
                    value = jnp.where(place_ref[0] == other, piece[row : row + step, :], value)
                head, within = divmod(number, HEAD_DIM)
                for term, part in enumerate(two_terms(value)):
                    first = (2 * head + term) * HEAD_DIM + within
                    out[first : first + step, :] = part
                number += step


def run_size():
    return math.gcd(lax.axis_size("seq"), 4)


def assemble_states(pieces):
    _, _, place, _ = run_of_blocks()
    rows = sum(piece.shape[0] for piece in pieces)
    whole = pl.BlockSpec(memory_space=pltpu.VMEM)
    return pl.pallas_call(
        assemble_kernel,
        out_shape=jax.ShapeDtypeStruct((2 * rows, HEAD_DIM), jnp.bfloat16),
        in_specs=[pl.BlockSpec(memory_space=pltpu.SMEM)] + [whole] * len(pieces),
        out_specs=whole,
        cost_estimate=pl.CostEstimate(
            flops=8 * rows * HEAD_DIM, bytes_accessed=8 * rows * HEAD_DIM, transcendentals=0
        ),
        name="assemble_states",
    )(jnp.reshape(place, (1,)), *pieces)


def product(left, right):
    return jnp.dot(left, right, preferred_element_type=jnp.float32)


def attend_kernel(
    order_ref, causal_ref, carried_ref, gain_ref, arrived_ref, keys_ref, values_ref, states_ref, *refs
):
    out_ref = refs[-1]
    tok_rows = order_ref.shape[0]
    half = tok_rows // 2

    ones = jnp.full((2 * HEAD_DIM, HEAD_DIM), 1.0, jnp.bfloat16)
    query = product(order_ref[...], arrived_ref[...]).astype(keys_ref.dtype)
    heads = query.shape[1] // HEAD_DIM
    together = math.gcd(heads, 2)
    for group in range(0, heads, together):
        tiles = []
        for part in range(group, group + together):
            columns = slice(part * HEAD_DIM, (part + 1) * HEAD_DIM)
            for rows, reach in ((slice(0, half), half), (slice(half, tok_rows), tok_rows)):
                scores = lax.dot_general(
                    query[rows, columns],
                    keys_ref[:reach, columns],
                    (((1,), (1,)), ((), ())),
                    preferred_element_type=jnp.float32,
                )
                weights = scores.astype(keys_ref.dtype) * causal_ref[rows, :reach]
                tiles.append((part, columns, rows, reach, weights))
        raws = []
        for part, columns, rows, reach, weights in tiles:
            carrying = query[rows, columns] * carried_ref[rows, :]
            states = states_ref[2 * part * HEAD_DIM : 2 * (part + 1) * HEAD_DIM, :]
            raws.append(
                product(
                    jnp.concatenate([weights, carrying, carrying], axis=1),
                    jnp.concatenate([values_ref[:reach, columns], states], axis=0),
                )
            )
        for (part, columns, rows, reach, weights), raw_out in zip(tiles, raws):
            square = jnp.concatenate(two_terms(raw_out * raw_out), axis=1)
            mean = product(square, ones) * (1.0 / HEAD_DIM)
            out_ref[rows, columns] = (
                raw_out * lax.rsqrt(mean + norm_eps) * gain_ref[:, columns]
            ).astype(out_ref.dtype)


def attend(arrived, keys, values, states, tables, gain, start, filled):
    slots, columns = arrived.shape
    tok_rows, mine = keys.shape
    width = math.gcd(math.gcd(columns, start), 4 * HEAD_DIM)
    first = start // width
    column_spec = pl.BlockSpec((tok_rows, width), lambda j: (0, first + j))
    return pl.pallas_call(
        attend_kernel,
        out_shape=jax.ShapeDtypeStruct((tok_rows, mine), jnp.bfloat16),
        grid=(columns // width,),
        in_specs=[pl.BlockSpec(table.shape, lambda j: (0, 0)) for table in tables]
        + [
            pl.BlockSpec((1, width), lambda j: (0, first + j)),
            pl.BlockSpec((slots, width), lambda j: (0, j)),
            column_spec,
            column_spec,
            pl.BlockSpec((2 * width, HEAD_DIM), lambda j: (first + j, 0)),
        ]
        + [pl.BlockSpec(memory_space=pl.ANY) for _ in filled],
        out_specs=column_spec,
        input_output_aliases={8: 0} if filled else {},
        cost_estimate=pl.CostEstimate(
            flops=ATTEND_WEIGHT * tok_rows * columns * (slots + 2 * tok_rows + 4 * HEAD_DIM) // 5,
            bytes_accessed=2 * columns * (slots + 4 * tok_rows),
            transcendentals=0,
        ),
        name="attend",
    )(*tables, gain, arrived, keys, values, states, *filled)


def local_kernel(order_ref, causal_ref, carried_ref, arrived_ref, keys_ref, values_ref, *refs):
    query_out, local_out = refs[-2:]
    tok_rows = order_ref.shape[0]
    half = tok_rows // 2
    query = product(order_ref[...], arrived_ref[...]).astype(keys_ref.dtype)
    heads = query.shape[1] // HEAD_DIM
    together = math.gcd(heads, 2)
    for group in range(0, heads, together):
        tiles = []
        for part in range(group, group + together):
            columns = slice(part * HEAD_DIM, (part + 1) * HEAD_DIM)
            query_out[:, columns] = query[:, columns] * carried_ref[...]
            for rows, reach in ((slice(0, half), half), (slice(half, tok_rows), tok_rows)):
                scores = lax.dot_general(
                    query[rows, columns],
                    keys_ref[:reach, columns],
                    (((1,), (1,)), ((), ())),
                    preferred_element_type=jnp.float32,
                )
                weights = scores.astype(keys_ref.dtype) * causal_ref[rows, :reach]
                tiles.append((columns, rows, reach, weights))
        for columns, rows, reach, weights in tiles:
            local_out[rows, columns] = product(weights, values_ref[:reach, columns])


def attend_locally(arrived, keys, values, tables):
    slots, columns = arrived.shape
    tok_rows = keys.shape[0]
    width = math.gcd(columns, 4 * HEAD_DIM)
    column_spec = pl.BlockSpec((tok_rows, width), lambda j: (0, j))
    return pl.pallas_call(
        local_kernel,
        out_shape=tuple(
            jax.ShapeDtypeStruct((tok_rows, columns), dtype) for dtype in (jnp.bfloat16, jnp.float32)
        ),
        grid=(columns // width,),
        in_specs=[pl.BlockSpec(table.shape, lambda j: (0, 0)) for table in tables]
        + [pl.BlockSpec((slots, width), lambda j: (0, j)), column_spec, column_spec],
        out_specs=(column_spec, column_spec),
        cost_estimate=pl.CostEstimate(
            flops=ATTEND_WEIGHT * tok_rows * columns * (slots + 2 * tok_rows) // 5,
            bytes_accessed=2 * columns * (slots + 5 * tok_rows),
            transcendentals=0,
        ),
        name="attend_locally",
    )(*tables, arrived, keys, values)


def finish_kernel(gain_ref, query_ref, local_ref, states_ref, out_ref):
    ones = jnp.full((2 * HEAD_DIM, HEAD_DIM), 1.0, jnp.bfloat16)
    raws = []
    for part in range(out_ref.shape[1] // HEAD_DIM):
        columns = slice(part * HEAD_DIM, (part + 1) * HEAD_DIM)
        query = query_ref[:, columns]
        states = states_ref[2 * part * HEAD_DIM : 2 * (part + 1) * HEAD_DIM, :]
        carried_term = product(jnp.concatenate([query, query], axis=1), states)
        raws.append((columns, local_ref[:, columns] + carried_term))
    for columns, raw_out in raws:
        square = jnp.concatenate(two_terms(raw_out * raw_out), axis=1)
        mean = product(square, ones) * (1.0 / HEAD_DIM)
        out_ref[:, columns] = (raw_out * lax.rsqrt(mean + norm_eps) * gain_ref[:, columns]).astype(
            out_ref.dtype
        )


def finish(query, local_term, states, gain):
    tok_rows, columns = query.shape
    width = math.gcd(columns, 4 * HEAD_DIM)
    column_spec = pl.BlockSpec((tok_rows, width), lambda j: (0, j))
    return pl.pallas_call(
        finish_kernel,
        out_shape=jax.ShapeDtypeStruct((tok_rows, gain.shape[1]), jnp.bfloat16),
        grid=(columns // width,),
        in_specs=[
            pl.BlockSpec((1, width), lambda j: (0, j)),
            column_spec,
            column_spec,
            pl.BlockSpec((2 * width, HEAD_DIM), lambda j: (j, 0)),
        ],
        out_specs=column_spec,
        cost_estimate=pl.CostEstimate(
            flops=FINISH_WEIGHT * 8 * tok_rows * columns * HEAD_DIM,
            bytes_accessed=8 * columns * tok_rows,
            transcendentals=0,
        ),
        name="finish",
    )(gain, query, local_term, states)


def swap_heads(qkv, plane_start, planes, start, columns):
    head_count = lax.axis_size("head")
    rows = qkv.shape[1]
    mine = qkv.shape[2] // head_count
    part = lax.slice_in_dim(qkv, plane_start, plane_start + planes, axis=0)
    if head_count == 2:
        low = part[:, :, start : start + columns]
        high = part[:, :, mine + start : mine + start + columns]
        outgoing = jnp.where(lax.axis_index("head") == 0, high, low)
        return lax.ppermute(outgoing, "head", [(0, 1), (1, 0)])
    split = part.reshape(planes, rows, head_count, mine)[..., start : start + columns]
    incoming = lax.all_to_all(
        jnp.moveaxis(split, 2, 0), "head", split_axis=0, concat_axis=0, tiled=False
    )
    return jnp.moveaxis(incoming, 0, 1).reshape(planes, head_count * rows, columns)


def pack_chunk(qkv, incoming, send_rows, plane_start, planes, start, columns, offset=0):
    head_count = lax.axis_size("head")
    place = lax.axis_index("head")
    rows = qkv.shape[1]
    mine = qkv.shape[2] // head_count
    slots = send_rows.reshape(-1, 1)
    width = math.gcd(math.gcd(columns, start), math.gcd(mine, 512))
    picks, sources = (slots,), ((incoming, 0, lambda at, width: offset // width),)
    if head_count == 2:
        picks = (slots - place * rows, slots - (1 - place) * rows)
        sources = (
            (qkv, plane_start, lambda at, width: at * (mine // width) + start // width),
        ) + sources
    return pack_rows(
        jnp.reshape(place, (1,)).astype(jnp.int32), picks, sources, planes, columns, width
    )


def to_owners(outgoing):
    return lax.all_to_all(outgoing, "seq", split_axis=0, concat_axis=0, tiled=True)


def on_device(qkv, send_rows, recv_pos, req_lengths, norm_gain):
    seq_count, head_count = lax.axis_size("seq"), lax.axis_size("head")
    block = lax.axis_index("seq")
    tok_rows = qkv.shape[1] * head_count
    columns = qkv.shape[2] // head_count

    req_ends = jnp.cumsum(req_lengths)
    req_starts = req_ends - req_lengths
    first_row = block * tok_rows
    positions = first_row + jnp.arange(tok_rows, dtype=jnp.int32)
    segment = jnp.sum((req_starts[None, :] <= positions[:, None]).astype(jnp.int32), axis=1) - 1
    last_rows = (jnp.arange(seq_count, dtype=jnp.int32) + 1) * tok_rows - 1
    last_segment = jnp.sum((req_starts[None, :] <= last_rows[:, None]).astype(jnp.int32), axis=1) - 1
    prev_segment = jnp.sum((req_starts < first_row).astype(jnp.int32)) - 1
    carried_mask = (segment == prev_segment).astype(jnp.int32)[:, None]
    land_row = recv_pos[0].reshape(1, -1)
    landing = first_row + land_row.reshape(-1, 1)
    landing_segment = jnp.sum((req_starts[None, :] <= landing).astype(jnp.int32), axis=1, keepdims=True) - 1
    in_tail = (land_row.reshape(-1, 1) >= 0) & (landing_segment == last_segment[block])
    tail_slots = jnp.broadcast_to(in_tail.astype(jnp.bfloat16), (land_row.shape[1], HEAD_DIM))
    gain = norm_gain.reshape(1, -1)

    rows = send_rows[0]
    head_share = columns // HEAD_DIM
    first = max(2, head_share // 4) * HEAD_DIM
    second = columns - first
    outgoing = pack_chunk(qkv, swap_heads(qkv, KEYS, 2, 0, first), rows, KEYS, 2, 0, first)
    arrived = to_owners(outgoing)
    outgoing = pack_chunk(
        qkv, swap_heads(qkv, KEYS, 2, first, second), rows, KEYS, 2, first, second
    )
    arrived_next = to_owners(outgoing)
    within, across = carry_tables(last_segment)
    sums = carry_within(block_update(arrived, tail_slots), within, jnp.bfloat16)
    tables = block_tables(land_row, segment, carried_mask)
    filled = unpack_keys_values(arrived, tables[0], 0, columns, ())
    incoming = swap_heads(qkv, QUERY, 1, 0, columns)
    incoming, sums, filled, tables, small = lax.optimization_barrier(
        (incoming, sums, filled, tables, (tail_slots, within, across))
    )
    tail_slots, within, across = small
    part = max(2, head_share // 2) * HEAD_DIM
    outgoing, outgoing_next = (
        pack_chunk(qkv, incoming, rows, QUERY, 1, start, size, start)
        for start, size in ((0, part), (part, columns - part))
    )
    outgoing, outgoing_next, pieces = lax.optimization_barrier(
        (outgoing, outgoing_next, pass_totals(sums))
    )
    query = to_owners(outgoing)
    shares, pieces = lax.optimization_barrier((block_update(arrived_next, tail_slots), pieces))
    states = hand_back(pieces, across)
    sums = carry_within(shares, within, jnp.bfloat16)
    outgoing_next, sums, states, arrived_next = lax.optimization_barrier(
        (outgoing_next, sums, states, arrived_next)
    )
    pieces = pass_totals(sums)
    filled = unpack_keys_values(arrived_next, tables[0], first, columns, filled)
    query_next = to_owners(outgoing_next)
    states += hand_back(pieces, across)
    local = attend_locally(query, *filled, tables)
    states = assemble_states(states)
    out = finish(*local, states, gain)
    return attend(query_next, *filled, states, tables, gain, part, (out,))


def solution(mesh):
    return jax.shard_map(
        on_device,
        mesh=mesh,
        in_specs=(
            P(None, ("seq", "head"), None),
            P("seq", None, None),
            P("seq", None, None),
            P(),
            P("head"),
        ),
        out_specs=P("seq", "head"),
        check_vma=False,
    )
```

```python
import math

import jax
import jax.numpy as jnp
from jax import lax
from jax.experimental import pallas as pl
from jax.experimental.pallas import tpu as pltpu
from jax.sharding import PartitionSpec as P

HEAD_DIM = 128

norm_eps = 1e-06

QUERY, KEYS, VALUES = 0, 1, 2

PACK_WEIGHT = 20
FINISH_WEIGHT = 1
ATTEND_WEIGHT = 145


def pick_kernel(*refs):
    half = len(refs) // 2
    for pick, onehot in zip(refs[:half], refs[half:]):
        rows = lax.broadcasted_iota(jnp.int32, onehot.shape, 1)
        onehot[...] = jnp.where(pick[...] == rows, 1.0, 0.0).astype(onehot.dtype)


def pick_matrices(send_rows, rows):
    head_count, place = lax.axis_size("head"), lax.axis_index("head")
    slots = send_rows.reshape(-1, 1)
    picks, length = (slots,), head_count * rows
    if head_count == 2:
        picks, length = (slots - place * rows, slots - (1 - place) * rows), rows
    return pl.pallas_call(
        pick_kernel,
        out_shape=(jax.ShapeDtypeStruct((slots.shape[0], length), jnp.bfloat16),) * len(picks),
        name="pick_matrices",
    )(*picks)


def pack_kernel(place_ref, *refs):
    count = (len(refs) - 1) // 2
    chosen, sources, out_ref = refs[:count], refs[count : 2 * count], refs[-1]
    total = None
    for source, onehot in zip(sources, chosen):
        part = jnp.dot(onehot[...], source[0], preferred_element_type=jnp.float32)
        total = part if total is None else total + part
    out_ref[...] = total.astype(out_ref.dtype)


def pack_rows(place, picks, sources, planes, columns, width):
    slots = picks[0].shape[0]
    blocks = columns // width
    lens = [array.shape[1] for array, _, _ in sources]

    def source_spec(array, plane_start, first):
        return pl.BlockSpec(
            (1, array.shape[1], width),
            lambda p, j, place_ref: (plane_start + p, 0, first(place_ref[0], width) + j),
        )

    return pl.pallas_call(
        pack_kernel,
        out_shape=jax.ShapeDtypeStruct((slots, planes * columns), jnp.bfloat16),
        grid_spec=pltpu.PrefetchScalarGridSpec(
            num_scalar_prefetch=1,
            grid=(planes, blocks),
            in_specs=[pl.BlockSpec(pick.shape, lambda p, j, place_ref: (0, 0)) for pick in picks]
            + [source_spec(*source) for source in sources],
            out_specs=pl.BlockSpec((slots, width), lambda p, j, place_ref: (0, p * blocks + j)),
        ),
        cost_estimate=pl.CostEstimate(
            flops=PACK_WEIGHT * 2 * slots * sum(lens) * planes * columns,
            bytes_accessed=2 * planes * columns * (slots + sum(lens)),
            transcendentals=0,
        ),
        name="pack_rows",
    )(place, *picks, *[array for array, _, _ in sources])


def update_kernel(place_ref, tail_ref, keys_ref, values_ref, *outs):
    for number, out in enumerate(outs):

        @pl.when(pl.program_id(0) == number)
        def _():
            for part in range(keys_ref.shape[1] // HEAD_DIM):
                columns = slice(part * HEAD_DIM, (part + 1) * HEAD_DIM)
                out[columns, :] = lax.dot_general(
                    keys_ref[:, columns] * tail_ref[...],
                    values_ref[:, columns],
                    (((0,), (0,)), ((), ())),
                    preferred_element_type=jnp.float32,
                )


def block_update(arrived, tail_slots):
    near, _, place, _ = run_of_blocks()
    slots, columns = arrived.shape[0], arrived.shape[1] // 2
    share = columns // near
    direct = share % HEAD_DIM == 0
    width, blocks = (share, near) if direct else (columns, 1)

    def column_spec(first):
        return pl.BlockSpec((slots, width), lambda j, place_ref: (0, first + (j ^ place_ref[0])))

    updates = pl.pallas_call(
        update_kernel,
        out_shape=(jax.ShapeDtypeStruct((width, HEAD_DIM), jnp.float32),) * blocks,
        grid_spec=pltpu.PrefetchScalarGridSpec(
            num_scalar_prefetch=1,
            grid=(blocks,),
            in_specs=[
                pl.BlockSpec((slots, HEAD_DIM), lambda j, place_ref: (0, 0)),
                column_spec(0),
                column_spec(blocks),
            ],
            out_specs=(pl.BlockSpec((width, HEAD_DIM), lambda j, place_ref: (0, 0)),) * blocks,
        ),
        cost_estimate=pl.CostEstimate(
            flops=2 * slots * columns * HEAD_DIM,
            bytes_accessed=4 * columns * (slots + HEAD_DIM),
            transcendentals=0,
        ),
        name="block_update",
    )(jnp.reshape(place if direct else 0 * place, (1,)), tail_slots, arrived, arrived)
    if direct:
        return list(updates)
    return [
        lax.dynamic_slice_in_dim(updates[0], (place ^ k) * share, share, axis=0)
        for k in range(near)
    ]


def tables_kernel(land_ref, seg_col_ref, seg_row_ref, mask_ref, order, causal, carried):
    rows = lax.broadcasted_iota(jnp.int32, order.shape, 0)
    order[...] = jnp.where(land_ref[...] == rows, 1.0, 0.0).astype(order.dtype)
    later = lax.broadcasted_iota(jnp.int32, causal.shape, 0)
    earlier = lax.broadcasted_iota(jnp.int32, causal.shape, 1)
    open_pair = (earlier <= later) & (seg_col_ref[...] == seg_row_ref[...])
    causal[...] = jnp.where(open_pair, 1.0, 0.0).astype(causal.dtype)
    carried[...] = jnp.broadcast_to(
        jnp.where(mask_ref[...] != 0, 1.0, 0.0).astype(carried.dtype), carried.shape
    )


def block_tables(land_row, segment, carried_mask):
    slots, tok_rows = land_row.shape[1], segment.shape[0]
    return pl.pallas_call(
        tables_kernel,
        out_shape=tuple(
            jax.ShapeDtypeStruct((tok_rows, n), jnp.bfloat16) for n in (slots, tok_rows, HEAD_DIM)
        ),
        cost_estimate=pl.CostEstimate(
            flops=8 * tok_rows * (slots + tok_rows),
            bytes_accessed=2 * tok_rows * (slots + tok_rows),
            transcendentals=0,
        ),
        name="block_tables",
    )(land_row, segment[:, None], segment[None, :], carried_mask)


def unpack_kernel(order_ref, keys_ref, values_ref, *refs):
    for source, out in zip((keys_ref, values_ref), refs[-2:]):
        out[...] = jnp.dot(
            order_ref[...], source[...], preferred_element_type=jnp.float32
        ).astype(out.dtype)


def unpack_keys_values(arrived, order, start, mine, filled):
    slots, columns = arrived.shape[0], arrived.shape[1] // 2
    tok_rows = order.shape[0]
    width = math.gcd(math.gcd(columns, start), 4 * HEAD_DIM)
    blocks, first = columns // width, start // width
    packed = jax.ShapeDtypeStruct((tok_rows, mine), arrived.dtype)
    column_spec = pl.BlockSpec((tok_rows, width), lambda j: (0, first + j))
    return pl.pallas_call(
        unpack_kernel,
        out_shape=(packed, packed),
        grid=(blocks,),
        in_specs=[
            pl.BlockSpec((tok_rows, slots), lambda j: (0, 0)),
            pl.BlockSpec((slots, width), lambda j: (0, j)),
            pl.BlockSpec((slots, width), lambda j: (0, blocks + j)),
        ]
        + [pl.BlockSpec(memory_space=pl.ANY) for _ in filled],
        out_specs=(column_spec, column_spec),
        input_output_aliases={3 + number: number for number in range(len(filled))},
        cost_estimate=pl.CostEstimate(
            flops=4 * tok_rows * columns * slots,
            bytes_accessed=4 * columns * (slots + tok_rows),
            transcendentals=0,
        ),
        name="unpack_keys_values",
    )(order, arrived, arrived, *filled)


def sum_kernel(take_ref, *refs):
    count = take_ref.shape[1]
    pieces, outs = refs[:count], refs[count:]
    for number, out in enumerate(outs):
        total = jnp.zeros(out.shape, jnp.float32)
        for piece in range(count):
            value = pieces[piece][...].astype(jnp.float32)
            total = total + jnp.where(take_ref[number, piece] != 0, value, 0.0)
        out[...] = total.astype(out.dtype)


def sum_pieces(take, pieces, last=jnp.float32):
    rows = pieces[0].shape[0]
    count = take.shape[0]
    whole = pl.BlockSpec(memory_space=pltpu.VMEM)
    return pl.pallas_call(
        sum_kernel,
        out_shape=(jax.ShapeDtypeStruct((rows, HEAD_DIM), jnp.float32),) * (count - 1)
        + (jax.ShapeDtypeStruct((rows, HEAD_DIM), last),),
        in_specs=[pl.BlockSpec(memory_space=pltpu.SMEM)] + [whole] * len(pieces),
        out_specs=(whole,) * count,
        cost_estimate=pl.CostEstimate(
            flops=count * len(pieces) * rows * HEAD_DIM,
            bytes_accessed=4 * (len(pieces) + count) * rows * HEAD_DIM,
            transcendentals=0,
        ),
        name="sum_pieces",
    )(take.astype(jnp.int32), *pieces)


def run_of_blocks():
    seq_count, block = lax.axis_size("seq"), lax.axis_index("seq")
    near = run_size()
    return near, seq_count // near, block % near, block // near


def swap_places(value, k):
    seq_count = lax.axis_size("seq")
    return lax.ppermute(value, "seq", [(i, i ^ k) for i in range(seq_count)])


def carry_tables(last_segment):
    near, far, place, run = run_of_blocks()
    base = run * near
    source = base + (place ^ jnp.arange(near))
    before = last_segment[jnp.maximum(source - 1, 0)]
    of_source = last_segment[source]
    inside = (source[None, :] < source[:, None]) & (of_source[None, :] == before[:, None])
    whole = of_source == last_segment[base + near - 1]
    within = jnp.concatenate([inside, whole[None]])
    shifts = jnp.arange(1, far // 2 + 1)
    ends = last_segment[jnp.maximum(run - shifts, 0) * near + near - 1]
    across = (run >= shifts)[None, :] & (ends[None, :] == before[:, None])
    own = jnp.arange(near)[:, None] == jnp.arange(near)[None, :]
    return within, jnp.concatenate([own, across], axis=1)


def carry_within(shares, within, total_type):
    pieces = [shares[0]] + [swap_places(shares[k], k) for k in range(1, len(shares))]
    return sum_pieces(within, pieces, total_type)


def pass_totals(sums):
    seq_count = lax.axis_size("seq")
    near, far, _, _ = run_of_blocks()
    pieces = list(sums[:near])
    for shift in range(1, far // 2 + 1):
        step = shift * near
        pieces.append(
            lax.ppermute(sums[near], "seq", [(i, i + step) for i in range(seq_count - step)])
        )
    return pieces


def hand_back(pieces, across):
    handed = sum_pieces(across, pieces)
    return [handed[0]] + [swap_places(handed[k], k) for k in range(1, len(handed))]


def two_terms(value):
    high = value.astype(jnp.bfloat16)
    return high, (value - high.astype(jnp.float32)).astype(jnp.bfloat16)


def assemble_kernel(place_ref, *refs):
    pieces, out = refs[:-1], refs[-1]
    near = run_size()
    number = 0
    for chunk in range(0, len(pieces), near):
        share = pieces[chunk].shape[0]
        step = math.gcd(share, HEAD_DIM)
        for place in range(near):
            for row in range(0, share, step):
                value = pieces[chunk + place][row : row + step, :]
                for other in range(1, near):
                    piece = pieces[chunk + (place ^ other)]
                    value = jnp.where(place_ref[0] == other, piece[row : row + step, :], value)
                head, within = divmod(number, HEAD_DIM)
                for term, part in enumerate(two_terms(value)):
                    first = (2 * head + term) * HEAD_DIM + within
                    out[first : first + step, :] = part
                number += step


def run_size():
    return math.gcd(lax.axis_size("seq"), 4)


def assemble_states(pieces):
    _, _, place, _ = run_of_blocks()
    rows = sum(piece.shape[0] for piece in pieces)
    whole = pl.BlockSpec(memory_space=pltpu.VMEM)
    return pl.pallas_call(
        assemble_kernel,
        out_shape=jax.ShapeDtypeStruct((2 * rows, HEAD_DIM), jnp.bfloat16),
        in_specs=[pl.BlockSpec(memory_space=pltpu.SMEM)] + [whole] * len(pieces),
        out_specs=whole,
        cost_estimate=pl.CostEstimate(
            flops=8 * rows * HEAD_DIM, bytes_accessed=8 * rows * HEAD_DIM, transcendentals=0
        ),
        name="assemble_states",
    )(jnp.reshape(place, (1,)), *pieces)


def product(left, right):
    return jnp.dot(left, right, preferred_element_type=jnp.float32)


def attend_kernel(
    order_ref, causal_ref, carried_ref, gain_ref, arrived_ref, keys_ref, values_ref, states_ref, *refs
):
    out_ref = refs[-1]
    tok_rows = order_ref.shape[0]
    half = tok_rows // 2

    ones = jnp.full((2 * HEAD_DIM, HEAD_DIM), 1.0, jnp.bfloat16)
    query = product(order_ref[...], arrived_ref[...]).astype(keys_ref.dtype)
    heads = query.shape[1] // HEAD_DIM
    together = math.gcd(heads, 2)
    for group in range(0, heads, together):
        tiles = []
        for part in range(group, group + together):
            columns = slice(part * HEAD_DIM, (part + 1) * HEAD_DIM)
            for rows, reach in ((slice(0, half), half), (slice(half, tok_rows), tok_rows)):
                scores = lax.dot_general(
                    query[rows, columns],
                    keys_ref[:reach, columns],
                    (((1,), (1,)), ((), ())),
                    preferred_element_type=jnp.float32,
                )
                weights = scores.astype(keys_ref.dtype) * causal_ref[rows, :reach]
                tiles.append((part, columns, rows, reach, weights))
        raws = []
        for part, columns, rows, reach, weights in tiles:
            carrying = query[rows, columns] * carried_ref[rows, :]
            states = states_ref[2 * part * HEAD_DIM : 2 * (part + 1) * HEAD_DIM, :]
            raws.append(
                product(
                    jnp.concatenate([weights, carrying, carrying], axis=1),
                    jnp.concatenate([values_ref[:reach, columns], states], axis=0),
                )
            )
        for (part, columns, rows, reach, weights), raw_out in zip(tiles, raws):
            square = jnp.concatenate(two_terms(raw_out * raw_out), axis=1)
            mean = product(square, ones) * (1.0 / HEAD_DIM)
            out_ref[rows, columns] = (
                raw_out * lax.rsqrt(mean + norm_eps) * gain_ref[:, columns]
            ).astype(out_ref.dtype)


def attend(arrived, keys, values, states, tables, gain, start, filled):
    slots, columns = arrived.shape
    tok_rows, mine = keys.shape
    width = math.gcd(math.gcd(columns, start), 4 * HEAD_DIM)
    first = start // width
    column_spec = pl.BlockSpec((tok_rows, width), lambda j: (0, first + j))
    return pl.pallas_call(
        attend_kernel,
        out_shape=jax.ShapeDtypeStruct((tok_rows, mine), jnp.bfloat16),
        grid=(columns // width,),
        in_specs=[pl.BlockSpec(table.shape, lambda j: (0, 0)) for table in tables]
        + [
            pl.BlockSpec((1, width), lambda j: (0, first + j)),
            pl.BlockSpec((slots, width), lambda j: (0, j)),
            column_spec,
            column_spec,
            pl.BlockSpec((2 * width, HEAD_DIM), lambda j: (first + j, 0)),
        ]
        + [pl.BlockSpec(memory_space=pl.ANY) for _ in filled],
        out_specs=column_spec,
        input_output_aliases={8: 0} if filled else {},
        cost_estimate=pl.CostEstimate(
            flops=ATTEND_WEIGHT * tok_rows * columns * (slots + 2 * tok_rows + 4 * HEAD_DIM) // 5,
            bytes_accessed=2 * columns * (slots + 4 * tok_rows),
            transcendentals=0,
        ),
        name="attend",
    )(*tables, gain, arrived, keys, values, states, *filled)


def local_kernel(order_ref, causal_ref, carried_ref, arrived_ref, keys_ref, values_ref, *refs):
    query_out, local_out = refs[-2:]
    tok_rows = order_ref.shape[0]
    half = tok_rows // 2
    query = product(order_ref[...], arrived_ref[...]).astype(keys_ref.dtype)
    heads = query.shape[1] // HEAD_DIM
    together = math.gcd(heads, 2)
    for group in range(0, heads, together):
        tiles = []
        for part in range(group, group + together):
            columns = slice(part * HEAD_DIM, (part + 1) * HEAD_DIM)
            query_out[:, columns] = query[:, columns] * carried_ref[...]
            for rows, reach in ((slice(0, half), half), (slice(half, tok_rows), tok_rows)):
                scores = lax.dot_general(
                    query[rows, columns],
                    keys_ref[:reach, columns],
                    (((1,), (1,)), ((), ())),
                    preferred_element_type=jnp.float32,
                )
                weights = scores.astype(keys_ref.dtype) * causal_ref[rows, :reach]
                tiles.append((columns, rows, reach, weights))
        for columns, rows, reach, weights in tiles:
            local_out[rows, columns] = product(weights, values_ref[:reach, columns])


def attend_locally(arrived, keys, values, tables):
    slots, columns = arrived.shape
    tok_rows = keys.shape[0]
    width = math.gcd(columns, 4 * HEAD_DIM)
    column_spec = pl.BlockSpec((tok_rows, width), lambda j: (0, j))
    return pl.pallas_call(
        local_kernel,
        out_shape=tuple(
            jax.ShapeDtypeStruct((tok_rows, columns), dtype) for dtype in (jnp.bfloat16, jnp.float32)
        ),
        grid=(columns // width,),
        in_specs=[pl.BlockSpec(table.shape, lambda j: (0, 0)) for table in tables]
        + [pl.BlockSpec((slots, width), lambda j: (0, j)), column_spec, column_spec],
        out_specs=(column_spec, column_spec),
        cost_estimate=pl.CostEstimate(
            flops=ATTEND_WEIGHT * tok_rows * columns * (slots + 2 * tok_rows) // 5,
            bytes_accessed=2 * columns * (slots + 5 * tok_rows),
            transcendentals=0,
        ),
        name="attend_locally",
    )(*tables, arrived, keys, values)


def finish_kernel(gain_ref, query_ref, local_ref, states_ref, out_ref):
    ones = jnp.full((2 * HEAD_DIM, HEAD_DIM), 1.0, jnp.bfloat16)
    raws = []
    for part in range(out_ref.shape[1] // HEAD_DIM):
        columns = slice(part * HEAD_DIM, (part + 1) * HEAD_DIM)
        query = query_ref[:, columns]
        states = states_ref[2 * part * HEAD_DIM : 2 * (part + 1) * HEAD_DIM, :]
        carried_term = product(jnp.concatenate([query, query], axis=1), states)
        raws.append((columns, local_ref[:, columns] + carried_term))
    for columns, raw_out in raws:
        square = jnp.concatenate(two_terms(raw_out * raw_out), axis=1)
        mean = product(square, ones) * (1.0 / HEAD_DIM)
        out_ref[:, columns] = (raw_out * lax.rsqrt(mean + norm_eps) * gain_ref[:, columns]).astype(
            out_ref.dtype
        )


def finish(query, local_term, states, gain):
    tok_rows, columns = query.shape
    width = math.gcd(columns, 4 * HEAD_DIM)
    column_spec = pl.BlockSpec((tok_rows, width), lambda j: (0, j))
    return pl.pallas_call(
        finish_kernel,
        out_shape=jax.ShapeDtypeStruct((tok_rows, gain.shape[1]), jnp.bfloat16),
        grid=(columns // width,),
        in_specs=[
            pl.BlockSpec((1, width), lambda j: (0, j)),
            column_spec,
            column_spec,
            pl.BlockSpec((2 * width, HEAD_DIM), lambda j: (j, 0)),
        ],
        out_specs=column_spec,
        cost_estimate=pl.CostEstimate(
            flops=FINISH_WEIGHT * 8 * tok_rows * columns * HEAD_DIM,
            bytes_accessed=8 * columns * tok_rows,
            transcendentals=0,
        ),
        name="finish",
    )(gain, query, local_term, states)


def swap_heads(qkv, plane_start, planes, start, columns):
    head_count = lax.axis_size("head")
    rows = qkv.shape[1]
    mine = qkv.shape[2] // head_count
    part = lax.slice_in_dim(qkv, plane_start, plane_start + planes, axis=0)
    if head_count == 2:
        low = part[:, :, start : start + columns]
        high = part[:, :, mine + start : mine + start + columns]
        outgoing = jnp.where(lax.axis_index("head") == 0, high, low)
        return lax.ppermute(outgoing, "head", [(0, 1), (1, 0)])
    split = part.reshape(planes, rows, head_count, mine)[..., start : start + columns]
    incoming = lax.all_to_all(
        jnp.moveaxis(split, 2, 0), "head", split_axis=0, concat_axis=0, tiled=False
    )
    return jnp.moveaxis(incoming, 0, 1).reshape(planes, head_count * rows, columns)


def pack_chunk(qkv, incoming, picks, plane_start, planes, start, columns, offset=0):
    head_count = lax.axis_size("head")
    place = lax.axis_index("head")
    mine = qkv.shape[2] // head_count
    width = math.gcd(math.gcd(columns, start), math.gcd(mine, 512))
    sources = ((incoming, 0, lambda at, width: offset // width),)
    if head_count == 2:
        sources = (
            (qkv, plane_start, lambda at, width: at * (mine // width) + start // width),
        ) + sources
    return pack_rows(
        jnp.reshape(place, (1,)).astype(jnp.int32), picks, sources, planes, columns, width
    )


def to_owners(outgoing):
    return lax.all_to_all(outgoing, "seq", split_axis=0, concat_axis=0, tiled=True)


def on_device(qkv, send_rows, recv_pos, req_lengths, norm_gain):
    seq_count, head_count = lax.axis_size("seq"), lax.axis_size("head")
    block = lax.axis_index("seq")
    tok_rows = qkv.shape[1] * head_count
    columns = qkv.shape[2] // head_count

    req_ends = jnp.cumsum(req_lengths)
    req_starts = req_ends - req_lengths
    first_row = block * tok_rows
    positions = first_row + jnp.arange(tok_rows, dtype=jnp.int32)
    segment = jnp.sum((req_starts[None, :] <= positions[:, None]).astype(jnp.int32), axis=1) - 1
    last_rows = (jnp.arange(seq_count, dtype=jnp.int32) + 1) * tok_rows - 1
    last_segment = jnp.sum((req_starts[None, :] <= last_rows[:, None]).astype(jnp.int32), axis=1) - 1
    prev_segment = jnp.sum((req_starts < first_row).astype(jnp.int32)) - 1
    carried_mask = (segment == prev_segment).astype(jnp.int32)[:, None]
    land_row = recv_pos[0].reshape(1, -1)
    landing = first_row + land_row.reshape(-1, 1)
    landing_segment = jnp.sum((req_starts[None, :] <= landing).astype(jnp.int32), axis=1, keepdims=True) - 1
    in_tail = (land_row.reshape(-1, 1) >= 0) & (landing_segment == last_segment[block])
    tail_slots = jnp.broadcast_to(in_tail.astype(jnp.bfloat16), (land_row.shape[1], HEAD_DIM))
    gain = norm_gain.reshape(1, -1)

    rows = pick_matrices(send_rows[0], qkv.shape[1])
    head_share = columns // HEAD_DIM
    first = max(2, head_share // 4) * HEAD_DIM
    second = columns - first
    outgoing = pack_chunk(qkv, swap_heads(qkv, KEYS, 2, 0, first), rows, KEYS, 2, 0, first)
    arrived = to_owners(outgoing)
    outgoing = pack_chunk(
        qkv, swap_heads(qkv, KEYS, 2, first, second), rows, KEYS, 2, first, second
    )
    arrived_next = to_owners(outgoing)
    within, across = carry_tables(last_segment)
    sums = carry_within(block_update(arrived, tail_slots), within, jnp.bfloat16)
    tables = block_tables(land_row, segment, carried_mask)
    filled = unpack_keys_values(arrived, tables[0], 0, columns, ())
    incoming = swap_heads(qkv, QUERY, 1, 0, columns)
    incoming, sums, filled, tables, small = lax.optimization_barrier(
        (incoming, sums, filled, tables, (tail_slots, within, across))
    )
    tail_slots, within, across = small
    part = max(2, head_share // 2) * HEAD_DIM
    outgoing, outgoing_next = (
        pack_chunk(qkv, incoming, rows, QUERY, 1, start, size, start)
        for start, size in ((0, part), (part, columns - part))
    )
    outgoing, outgoing_next, pieces = lax.optimization_barrier(
        (outgoing, outgoing_next, pass_totals(sums))
    )
    query = to_owners(outgoing)
    shares, pieces = lax.optimization_barrier((block_update(arrived_next, tail_slots), pieces))
    states = hand_back(pieces, across)
    sums = carry_within(shares, within, jnp.bfloat16)
    outgoing_next, sums, states, arrived_next = lax.optimization_barrier(
        (outgoing_next, sums, states, arrived_next)
    )
    pieces = pass_totals(sums)
    filled = unpack_keys_values(arrived_next, tables[0], first, columns, filled)
    query_next = to_owners(outgoing_next)
    states += hand_back(pieces, across)
    local = attend_locally(query, *filled, tables)
    states = assemble_states(states)
    out = finish(*local, states, gain)
    return attend(query_next, *filled, states, tables, gain, part, (out,))


def solution(mesh):
    return jax.shard_map(
        on_device,
        mesh=mesh,
        in_specs=(
            P(None, ("seq", "head"), None),
            P("seq", None, None),
            P("seq", None, None),
            P(),
            P("head"),
        ),
        out_specs=P("seq", "head"),
        check_vma=False,
    )
```
